256 devices in a mesh: rep: 8 (over x, z_hi), seq: 4 (over y), tp: 8 (over z_lo, core).
Axes of the slice: x: 4, y: 4, z: 8 (z_hi: 2, z_lo: 4; z = z_hi * 4 + z_lo), core: 2. Of those that a mesh axis runs over, the one named last changes fastest.
Arguments:
- hidden_in: bfloat16 [32768, 1536], P(('rep', 'seq', 'tp')), may hold values from -3 to 3
- routes: int32 [32768, 4], P(('rep', 'seq', 'tp')), may hold values from 0 to 31, all different within a row; in each aligned block of 128 rows (0 to 127, 128 to 255, ...) at most 24 rows name the same one
- prefix_len: int32 [8], replicated, may hold values from 256 to 2048, as said below
- cache: bfloat16 [8, 2, 2048, 256], P(None, None, ('rep', 'seq')), may hold values from -400 to 400, as said below
- attn_gain: float32 [1536], replicated, may hold values from 0.1 to 1.9
- w_query: bfloat16 [1536, 1024], P(None, 'tp'), may hold values from -0.375 to 0.375
- w_keyval: bfloat16 [2, 1536, 256], replicated, may hold values from -0.15625 to 0.15625
- w_out: bfloat16 [1024, 1536], P('tp'), may hold values from -0.375 to 0.375
- moe_gain: float32 [1536], replicated, may hold values from 0.1 to 1.9
- w_router: bfloat16 [1536, 32], replicated, may hold values from -0.15625 to 0.15625
- expert_in: bfloat16 [32, 1536, 1536], P(('seq', 'tp')), may hold values from -0.15625 to 0.15625
- expert_out: bfloat16 [32, 768, 1536], P(('seq', 'tp')), may hold values from -0.875 to 0.875
Outputs:
- hidden_out: bfloat16 [32768, 1536], P(('rep', 'seq', 'tp'))
- new_cache: bfloat16 [32768, 512], P(('rep', 'seq'), 'tp')
The draws below stay inside these ranges and needn't reach their ends.
Inputs may be any that keep to these rules, and one draw needn't show every extreme that they name: `routes`: each row names 4 different experts; within the rows of one device (aligned blocks of 128 rows) no expert is named by more than 24 rows. prefix_len[r] cached positions (0 to prefix_len[r] - 1) of request r are valid; some request has 2048. cache[r, g, p, 0:128] is a key, cache[r, g, p, 128:] a value.
All inputs are finite; a program needn't handle non-finite values.
Results may differ from the reference program's by a relative error of at most 0.029.
The reference program's roundings to bfloat16 on the way count: a program that leaves them out, or rounds other values in their place, can miss the bound.
Values may be sent and summed in bfloat16 or wider, within the bound.
No kernel may reach another device: no remote copies, remote signals or barrier semaphores. Data moves between devices by JAX's collectives and lax.ppermute only.
A program may use at most 64 MiB of HBM per device.

```python
import math
import jax
import jax.numpy as jnp
import numpy as np
from jax import lax

D = 1536
HD = 128
HQ = 8
KVH = 2
FFE = 768
EXPERTS = 32
TOPK = 4
ROWS_DEV = 128
PREFIX = 2048
REPLICAS = 8
NEW = 4096
TOKENS = 32768
CAP = 24


def draw_prefix_len(key, part):
    first, second = jax.random.split(jax.random.fold_in(key, 11))
    lengths = jax.random.randint(first, (REPLICAS,), PREFIX // 8, PREFIX + 1)
    order = jax.random.permutation(second, REPLICAS)
    lengths = lengths.at[order[0]].set(PREFIX)
    return lengths.astype(jnp.int32)


def draw_cache(key, part):
    base_key = jax.random.fold_in(jax.random.fold_in(key, 23), 0)
    values = jax.random.normal(base_key, (REPLICAS, KVH, PREFIX, 2 * HD), jnp.float32)
    values = jnp.clip(values, -6.0, 6.0)
    return values.astype(jnp.bfloat16)


def shard_levels(rng, shape, cuts, least, largest):
    level = 1.0
    for dim, parts in cuts:
        heights = jax.random.uniform(jax.random.fold_in(jax.random.fold_in(rng, 6), dim), (parts,), jnp.float32, least / len(cuts), largest / len(cuts))
        level = level * jnp.repeat(jnp.exp(heights), shape[dim] // parts).reshape((-1,) + (1,) * (len(shape) - 1 - dim))
    return level


def deal_out(key, own, number, rows, amount, top, bound, lean):
    ranking = jax.random.permutation(key, amount)
    heavy_load, usual = portions_of(amount, rows * top, bound, lean, True), portions_of(amount, rows * top, bound, lean, False)
    places = jnp.arange(amount)

    def named(sizes, turn):
        used = int((sizes > 0).sum())
        fixed = max(1, used // 4)
        shifted = fixed + (places - fixed + turn * (used - fixed)) % max(1, amount - fixed)
        return jnp.zeros((amount,), jnp.int32).at[ranking[jnp.where(places < fixed, places, shifted)]].set(jnp.asarray(sizes, jnp.int32))

    sizes = jnp.where(number % 4 == 0, named(heavy_load, number // 4), named(usual, number - number // 4 - 1))
    mixed = jax.random.permutation(jax.random.fold_in(own, 3), amount)
    donor, receiver = mixed[0:amount // 2 * 2:2], mixed[1:amount // 2 * 2:2]
    room = jnp.minimum(sizes[donor] - 1, bound - sizes[receiver]) // 2
    room = jnp.where((donor == ranking[0]) | (receiver == ranking[0]) | (sizes[receiver] == 0), 0, jnp.maximum(room, 0))
    shifted = jax.random.randint(jax.random.fold_in(own, 4), (amount // 2,), 0, 1 << 20) % (room + 1)
    sizes = sizes.at[donor].add(-shifted).at[receiver].add(shifted)
    labels = jnp.searchsorted(jnp.cumsum(sizes), jnp.arange(rows * top), side="right").astype(jnp.int32)
    grid = labels.reshape(top, rows).T
    grid = grid[jax.random.permutation(jax.random.fold_in(own, 1), rows)]
    turn = jax.random.randint(jax.random.fold_in(own, 2), (rows, 1), 0, top)
    return jnp.take_along_axis(grid, (jnp.arange(top)[None, :] + turn) % top, axis=1)


def portions_of(count, total, limit, slope, full):
    portions = [(1 << 20) // math.isqrt(rank ** slope) + 1 for rank in range(1, count + 1)]
    largest = limit if full else min(limit, max(-(-total // count), total * portions[0] // sum(portions)))
    least = 1 if total - largest >= count - 1 else 0
    given, surplus = [largest] + [least] * (count - 1), total - largest - least * (count - 1)
    while surplus > 0:
        candidates = [i for i in range(1, count) if given[i] < largest] or [i for i in range(1, count) if given[i] < limit]
        pool, left = sum([portions[i] for i in candidates]), surplus
        for i in candidates:
            more = min(limit - given[i], max(1, left * portions[i] // pool), surplus)
            given[i] = given[i] + more
            surplus = surplus - more
    return np.array(given)


def bell_draw(rng, dims, width, reach, shards=(), kind=jnp.bfloat16):
    result = jax.random.normal(rng, dims, jnp.float32) * width
    if len(shards) > 0:
        result = shard_levels(rng, dims, shards, -0.22, 0.18) * result
    return jnp.clip(result, min=-reach, max=reach).astype(kind)


def setup_inputs(seed: int = 0) -> dict:
    arg_keys = jax.random.split(jax.random.key(seed), 13)
    hidden_in = bell_draw(arg_keys[0], (TOKENS, D), 0.5, 3.0, ((0, 256),))
    routes_keys = jax.random.split(jax.random.fold_in(arg_keys[1], 1), TOKENS // ROWS_DEV)
    routes_turns = jax.random.permutation(jax.random.fold_in(arg_keys[1], 3), TOKENS // ROWS_DEV)
    routes = jax.vmap(lambda own, number: deal_out(jax.random.fold_in(arg_keys[1], 2), own, number, ROWS_DEV, EXPERTS, TOPK, CAP, 2))(routes_keys, routes_turns).reshape((TOKENS, TOPK))
    prefix_len = draw_prefix_len(jax.random.fold_in(arg_keys[12], 71), 0)
    cache = draw_cache(jax.random.fold_in(arg_keys[12], 71), 0)
    attn_gain = jnp.clip(1.0 + 0.18 * jax.random.normal(arg_keys[4], (D,), jnp.float32), 0.1, 1.9)
    w_query = bell_draw(arg_keys[5], (D, HQ * HD), (D // 6) ** -0.5, 0.375, ((1, 8),))
    w_keyval = bell_draw(arg_keys[6], (KVH, D, 2 * HD), D ** -0.5, 0.15625)
    w_out = bell_draw(arg_keys[7], (HQ * HD, D), (HQ * HD // 4) ** -0.5, 0.375, ((0, 8),))
    moe_gain = jnp.clip(1.0 + 0.18 * jax.random.normal(arg_keys[8], (D,), jnp.float32), 0.1, 1.9)
    w_router = bell_draw(arg_keys[9], (D, EXPERTS), D ** -0.5, 0.15625)
    expert_in = bell_draw(arg_keys[10], (EXPERTS, D, 2 * FFE), D ** -0.5, 0.15625, ((0, 32),))
    expert_out = bell_draw(arg_keys[11], (EXPERTS, FFE, D), (FFE // 16) ** -0.5, 0.875, ((0, 32),))
    return dict(hidden_in=hidden_in, routes=routes, prefix_len=prefix_len, cache=cache, attn_gain=attn_gain, w_query=w_query, w_keyval=w_keyval, w_out=w_out, moe_gain=moe_gain, w_router=w_router, expert_in=expert_in, expert_out=expert_out)


epsilon = 1e-06
masked_score = -1e+30

def rms_scale(rows, gain):
    values = rows.astype(jnp.float32)
    inverse = lax.rsqrt(lax.optimization_barrier(jnp.mean(values * values, axis=-1, keepdims=True)) + epsilon)
    return (values * inverse * gain).astype(jnp.bfloat16)

def head_attention(query_rows, keys, values, visible):
    scores = lax.dot_general(query_rows, keys, (((1,), (1,)), ((), ())), preferred_element_type=jnp.float32)
    scores = scores * (1.0 / float(HD) ** 0.5)
    scores = jnp.where(visible, scores, masked_score)
    best = lax.optimization_barrier(jnp.max(scores, axis=1, keepdims=True))
    weights = jnp.where(visible, jnp.exp(scores - best), 0.0)
    total = lax.optimization_barrier(jnp.sum(weights, axis=1, keepdims=True))
    summed = jnp.dot(weights.astype(jnp.bfloat16), values, preferred_element_type=jnp.float32)
    return (summed / total).astype(jnp.bfloat16)

def replica_attention(queries, new_cache, cache, prefix_len):
    group = HQ // KVH
    block = ROWS_DEV

    def per_replica(replica):
        rep_queries = lax.dynamic_slice_in_dim(queries, replica * NEW, NEW, 0)
        rep_fresh = lax.dynamic_slice_in_dim(new_cache, replica * NEW, NEW, 0)
        rep_cache = lax.dynamic_index_in_dim(cache, replica, 0, keepdims=False)
        length = lax.dynamic_index_in_dim(prefix_len, replica, 0, keepdims=False)
        prefix_ok = jnp.arange(PREFIX, dtype=jnp.int32) < length

        def per_head(head):
            kv_head = head // group
            query_cols = lax.dynamic_slice_in_dim(rep_queries, head * HD, HD, 1)
            pages = lax.dynamic_index_in_dim(rep_cache, kv_head, 0, keepdims=False)
            fresh = lax.dynamic_slice_in_dim(rep_fresh, kv_head * 2 * HD, 2 * HD, 1)
            keys = jnp.concatenate([pages[:, :HD], fresh[:, :HD]], axis=0)
            values = jnp.concatenate([pages[:, HD:], fresh[:, HD:]], axis=0)

            def per_block(index):
                rows = lax.dynamic_slice_in_dim(query_cols, index * block, block, 0)
                position = index * block + jnp.arange(block, dtype=jnp.int32)
                causal = jnp.arange(NEW, dtype=jnp.int32)[None, :] <= position[:, None]
                visible = jnp.concatenate([jnp.broadcast_to(prefix_ok[None, :], (block, PREFIX)), causal], axis=1)
                return head_attention(rows, keys, values, visible)
            return lax.map(per_block, jnp.arange(NEW // block, dtype=jnp.int32)).reshape(NEW, HD)
        return lax.map(per_head, jnp.arange(HQ, dtype=jnp.int32))
    heads = lax.map(per_replica, jnp.arange(REPLICAS, dtype=jnp.int32))
    return jnp.transpose(heads, (0, 2, 1, 3)).reshape(REPLICAS * NEW, HQ * HD)

def expert_layer(normed_moe, routes, w_router, expert_in, expert_out):
    logits = jnp.dot(normed_moe, w_router, preferred_element_type=jnp.float32)
    chosen = jnp.take_along_axis(logits, routes, axis=1)
    raised = jnp.exp(chosen)
    gates = raised / lax.optimization_barrier(jnp.sum(raised, axis=1, keepdims=True))
    blocks = TOKENS // ROWS_DEV
    flat_routes = routes.reshape(blocks, ROWS_DEV * TOPK)
    onehot = (flat_routes[:, :, None] == jnp.arange(EXPERTS, dtype=jnp.int32)[None, None, :]).astype(jnp.int32)
    before = jnp.cumsum(onehot, axis=1) - onehot
    slot = lax.optimization_barrier(jnp.sum(before * onehot, axis=2))
    block_ids = jnp.arange(blocks, dtype=jnp.int32)[:, None]
    target = ((flat_routes * blocks + block_ids) * CAP + slot).reshape(-1).astype(jnp.int32)
    source = jnp.full((EXPERTS * blocks * CAP,), TOKENS * TOPK, jnp.int32)
    source = source.at[target].set(jnp.arange(TOKENS * TOPK, dtype=jnp.int32))
    padded = jnp.concatenate([jnp.repeat(normed_moe, TOPK, axis=0), jnp.zeros((1, D), jnp.bfloat16)], axis=0)

    def per_expert(expert):
        index = lax.dynamic_slice_in_dim(source, expert * blocks * CAP, blocks * CAP, 0)
        rows = padded[index]
        weights_in = lax.dynamic_index_in_dim(expert_in, expert, 0, keepdims=False)
        weights_out = lax.dynamic_index_in_dim(expert_out, expert, 0, keepdims=False)
        inner = jnp.dot(rows, weights_in, preferred_element_type=jnp.float32)
        active = (jnp.maximum(inner[:, :FFE], 0.0) * inner[:, FFE:]).astype(jnp.bfloat16)
        return jnp.dot(active, weights_out, preferred_element_type=jnp.float32).astype(jnp.bfloat16)
    results = lax.map(per_expert, jnp.arange(EXPERTS, dtype=jnp.int32)).reshape(EXPERTS * blocks * CAP, D)
    picked = results[target].reshape(TOKENS, TOPK, D).astype(jnp.float32)
    return lax.optimization_barrier(jnp.sum(gates[:, :, None] * picked, axis=1))

def reference(hidden_in, routes, prefix_len, cache, attn_gain, w_query, w_keyval, w_out, moe_gain, w_router, expert_in, expert_out):
    normed = rms_scale(hidden_in, attn_gain)
    queries = jnp.dot(normed, w_query, preferred_element_type=jnp.float32).astype(jnp.bfloat16)
    new_cache = jnp.concatenate([jnp.dot(normed, w_keyval[head], preferred_element_type=jnp.float32).astype(jnp.bfloat16) for head in range(KVH)], axis=1)
    attended = replica_attention(queries, new_cache, cache, prefix_len)
    mid = (hidden_in.astype(jnp.float32) + jnp.dot(attended, w_out, preferred_element_type=jnp.float32)).astype(jnp.bfloat16)
    normed_moe = rms_scale(mid, moe_gain)
    mixed = expert_layer(normed_moe, routes, w_router, expert_in, expert_out)
    hidden_out = (mid.astype(jnp.float32) + mixed).astype(jnp.bfloat16)
    return (hidden_out, new_cache)
```

```python
import jax
import jax.numpy as jnp
from jax import lax
from jax.experimental import pallas as pl
from jax.experimental.pallas import tpu as pltpu
from jax.sharding import Mesh
from jax.sharding import PartitionSpec as P

CAP = 24
epsilon = 1e-06
masked_score = -1e30
log2e = 1.4426950408889634

X, ZH, Y, ZL, C = 4, 2, 4, 4, 2


def rms_scale(rows, gain):
    values = rows.astype(jnp.float32)
    inverse = lax.rsqrt(jnp.mean(values * values, axis=-1, keepdims=True) + epsilon)
    return (values * inverse * gain).astype(jnp.bfloat16)


def swap_core(a):
    return lax.ppermute(a, "c", [(0, 1), (1, 0)])


def shift_line(a, s):
    return lax.ppermute(a, "zl", [(i, (i + s) % ZL) for i in range(ZL)])


def shift_y(a, s):
    pairs = []
    for y in range(Y):
        for c in range(C):
            t = (y + (s if c == 0 else -s)) % Y
            pairs.append((y * C + c, t * C + c))
    return lax.ppermute(a, ("y", "c"), pairs)


def attention_kernel(
    meta, q_ref, own_ref, a_ref, b_ref, f_ref, o_ref, qs, m_ref, l_ref, acc_ref, *, pages, fresh
):
    rows = qs.shape[0]
    heads = rows // 256
    scale = log2e / float(128) ** 0.5
    y, zl, c, length = meta[0], meta[1], meta[2], meta[3]
    for s in range(heads):
        h = lax.rem(zl - s + 4, 4)
        qs[s * 256 : (s + 1) * 256, :] = q_ref[:, pl.ds(pl.multiple_of(h * 128, 128), 128)]

    def scores_of(keys):
        return (
            lax.dot_general(
                qs[...], keys, (((1,), (1,)), ((), ())), preferred_element_type=jnp.float32
            )
            * scale
        )

    def fold(scores, values):
        old = m_ref[...]
        new = jnp.maximum(old, jnp.max(scores, axis=1, keepdims=True))
        m_ref[...] = new
        weights = jnp.exp2(scores - new[:, :1])
        factor = jnp.exp2(old - new)
        l_ref[...] = l_ref[...] * factor + jnp.sum(weights, axis=1, keepdims=True)
        acc_ref[...] = acc_ref[...] * factor + jnp.dot(
            weights.astype(jnp.bfloat16), values, preferred_element_type=jnp.float32
        )

    m_ref[...] = jnp.full(m_ref.shape, masked_score, jnp.float32)
    l_ref[...] = jnp.zeros(l_ref.shape, jnp.float32)
    acc_ref[...] = jnp.zeros(acc_ref.shape, jnp.float32)

    def half_of(index):
        return ((index % 256) // 128) * (1 - 2 * c) + c

    key = lax.broadcasted_iota(jnp.int32, (1, fresh), 1)
    key_chip = (zl - key // 256 + 4) % 4
    key_pos = key_chip * 256 + half_of(key) * 128 + key % 128
    row = lax.broadcasted_iota(jnp.int32, (rows, 1), 0)
    row_pos = zl * 256 + half_of(row) * 128 + row % 128
    scores = scores_of(own_ref[pages:, :128])
    scores = jnp.where(key_pos <= row_pos, scores, masked_score)
    fold(scores, own_ref[pages:, 128:])

    step = 1 - 2 * c
    shards = ((own_ref, y), (a_ref, y - step), (b_ref, y + step), (f_ref, y + 2))
    page = lax.broadcasted_iota(jnp.int32, (1, pages), 1)
    for ref, source in shards:
        source = lax.rem(source + 4, 4)
        position = (page // 64 * 4 + source) * 64 + page % 64
        scores = scores_of(ref[:pages, :128])
        scores = jnp.where(position < length, scores, masked_score)
        fold(scores, ref[:pages, 128:])
        if ref is not own_ref:

            @pl.when(source < y)
            def _(ref=ref):
                fold(scores_of(ref[pages:, :128]), ref[pages:, 128:])

    done = (acc_ref[...] / l_ref[...]).astype(o_ref.dtype)
    for s in range(heads):
        o_ref[:, s * 128 : (s + 1) * 128] = done[s * 256 : (s + 1) * 256, :]


def order_kernel(meta, x_ref, o_ref):
    zl, c = meta[1], meta[2]
    col = pl.multiple_of(lax.rem(zl, 2) * 128, 128)
    for z in range(ZL):
        slot = lax.rem(zl - z + 4, 4)
        for half in range(2):
            inner = half * (1 - 2 * c) + c
            start = pl.multiple_of(slot * 256 + inner * 128, 128)
            o_ref[z * 256 + half * 128 : z * 256 + half * 128 + 128, :] = x_ref[
                pl.ds(start, 128), pl.ds(col, 128)
            ]


def body(
    hidden_in,
    routes,
    prefix_len,
    cache,
    attn_gain,
    w_query,
    w_keyval,
    w_out,
    moe_gain,
    w_router,
    expert_in,
    expert_out,
):
    y, zl, c = lax.axis_index("y"), lax.axis_index("zl"), lax.axis_index("c")
    rep = lax.axis_index(("x", "zh"))
    rows_dev, width = hidden_in.shape
    length = lax.dynamic_index_in_dim(prefix_len, rep, 0, keepdims=False)
    meta = jnp.stack([y, zl, c, length]).astype(jnp.int32)
    smem = pl.BlockSpec(memory_space=pltpu.SMEM)
    vmem = pl.BlockSpec(memory_space=pltpu.VMEM)

    group_size = 4
    with jax.named_scope("weights"):
        wq_all = lax.all_gather(w_query, ("zl", "c"), axis=0, tiled=False)
        to_group = []
        for z in range(ZL):
            for k in range(C):
                to_group.append((z * C + k, (2 * (z % 2) + k) * C + z // 2))
        wo_here = lax.ppermute(w_out, ("zl", "c"), to_group)
        wo = jnp.concatenate([wo_here] + [shift_line(wo_here, s) for s in (1, 2, 3)], axis=0)

    with jax.named_scope("pages"):
        own_pages = lax.dynamic_index_in_dim(cache, c, 1, keepdims=True)
        fetched = lax.all_to_all(own_pages, ("x", "zh"), split_axis=0, concat_axis=2, tiled=True)
        pages = fetched.reshape(-1, 256)

    with jax.named_scope("keys"):
        normed = rms_scale(hidden_in, attn_gain)
        both = jnp.concatenate([normed, swap_core(normed)], axis=0)
        w_kv = lax.dynamic_index_in_dim(w_keyval, c, 0, keepdims=False)
        kv = jnp.dot(both, w_kv, preferred_element_type=jnp.float32).astype(jnp.bfloat16)
        line = [kv] + [shift_line(kv, s) for s in (1, 2, 3)]
        shard = jnp.concatenate([pages] + line, axis=0)
        up = shift_y(shard, 1)
        down = shift_y(shard, -1)
        far = shift_y(up, 1)

    with jax.named_scope("new_cache"):
        ordered = pl.pallas_call(
            order_kernel,
            out_shape=jax.ShapeDtypeStruct((1024, 128), jnp.bfloat16),
            in_specs=[smem, vmem],
            out_specs=vmem,
        )(meta, jnp.concatenate(line, axis=0))
        other = swap_core(ordered)
        held = jnp.where(c == zl // 2, ordered, other)
        new_cache = jnp.where(c == 0, held[:, :64], held[:, 64:])

    with jax.named_scope("queries"):
        wq = lax.dynamic_slice_in_dim(wq_all, c * group_size, group_size, 0)
        queries = jnp.concatenate(
            [jnp.dot(both, wq[h], preferred_element_type=jnp.float32) for h in range(group_size)],
            axis=1,
        ).astype(jnp.bfloat16)

    with jax.named_scope("attention"):
        n_pages = pages.shape[0]
        n_rows = 2 * rows_dev * group_size
        attended = pl.pallas_call(
            lambda *refs: attention_kernel(*refs, pages=n_pages, fresh=1024),
            out_shape=jax.ShapeDtypeStruct((2 * rows_dev, group_size * 128), jnp.bfloat16),
            in_specs=[smem] + [vmem] * 5,
            out_specs=vmem,
            scratch_shapes=[
                pltpu.VMEM((n_rows, 128), jnp.bfloat16),
                pltpu.VMEM((n_rows, 128), jnp.float32),
                pltpu.VMEM((n_rows, 128), jnp.float32),
                pltpu.VMEM((n_rows, 128), jnp.float32),
            ],
            compiler_params=pltpu.CompilerParams(vmem_limit_bytes=48 * 2**20),
            cost_estimate=pl.CostEstimate(
                flops=4 * n_rows * 6144 * 128,
                bytes_accessed=4 * 2**20,
                transcendentals=n_rows * 6144,
            ),
            name="attention",
        )(meta, queries, shard, up, down, far)

    with jax.named_scope("out_projection"):
        partial = jnp.dot(attended, wo, preferred_element_type=jnp.float32)
        received = swap_core(partial[rows_dev:])
        mid = (hidden_in.astype(jnp.float32) + (partial[:rows_dev] + received)).astype(jnp.bfloat16)
        normed_moe = rms_scale(mid, moe_gain)

    with jax.named_scope("routing"):
        experts_all = w_router.shape[1]
        top = routes.shape[1]
        slots = experts_all * CAP
        expert_ids = jnp.arange(experts_all, dtype=jnp.int32)
        matches = routes[:, :, None] == expert_ids[None, None, :]
        named = jnp.sum(matches.astype(jnp.float32), axis=1)
        lower = (
            jnp.arange(rows_dev)[:, None] > jnp.arange(rows_dev)[None, :]
        ).astype(jnp.float32)
        before = jnp.dot(lower, named, preferred_element_type=jnp.float32)
        slot = jnp.sum(jnp.where(matches, before[:, None, :], 0.0), axis=2).astype(jnp.int32)
        target = routes * CAP + slot
        slot_ids = jnp.arange(slots, dtype=jnp.int32)
        placed = sum((target[:, k : k + 1] == slot_ids[None, :]) for k in range(top)).astype(
            jnp.bfloat16
        )

    with jax.named_scope("dispatch"):
        outgoing = lax.dot_general(
            placed, normed_moe, (((0,), (0,)), ((), ())), preferred_element_type=jnp.float32
        ).astype(jnp.bfloat16)
        arrived = lax.all_to_all(
            outgoing.reshape(experts_all, CAP, width),
            ("y", "zl", "c"),
            split_axis=0,
            concat_axis=0,
            tiled=True,
        )

    with jax.named_scope("gates"):
        logits = jnp.dot(normed_moe, w_router, preferred_element_type=jnp.float32)
        chosen = jnp.sum(jnp.where(matches, logits[:, None, :], 0.0), axis=2)
        raised = jnp.exp(chosen)
        gates = raised / jnp.sum(raised, axis=1, keepdims=True)
        mix = sum(
            jnp.where(target[:, k : k + 1] == slot_ids[None, :], gates[:, k : k + 1], 0.0)
            for k in range(top)
        )
        mix_high = mix.astype(jnp.bfloat16)
        mix_low = (mix - mix_high.astype(jnp.float32)).astype(jnp.bfloat16)
        mix_both = jnp.concatenate([mix_high, mix_low], axis=0)

    with jax.named_scope("experts"):
        inner_dim = expert_out.shape[1]
        inner = jnp.dot(
            arrived.reshape(slots, width), expert_in[0], preferred_element_type=jnp.float32
        )
        active = (jnp.maximum(inner[:, :inner_dim], 0.0) * inner[:, inner_dim:]).astype(
            jnp.bfloat16
        )
        output = jnp.dot(active, expert_out[0], preferred_element_type=jnp.float32).astype(
            jnp.bfloat16
        )

    with jax.named_scope("combine"):
        returned = lax.all_to_all(
            output.reshape(experts_all, CAP, width),
            ("y", "zl", "c"),
            split_axis=0,
            concat_axis=0,
            tiled=True,
        ).reshape(slots, width)
        mixed = jnp.dot(mix_both, returned, preferred_element_type=jnp.float32)
        hidden_out = (mid.astype(jnp.float32) + (mixed[:rows_dev] + mixed[rows_dev:])).astype(
            jnp.bfloat16
        )
    return (hidden_out, new_cache)


def solution(mesh):
    axes = ("x", "zh", "y", "zl", "c")
    split = Mesh(mesh.devices.reshape(X, ZH, Y, ZL, C), axes)
    placed = (
        P(axes, None),
        P(axes, None),
        P(),
        P(None, None, ("x", "zh", "y"), None),
        P(),
        P(None, ("zl", "c")),
        P(),
        P(("zl", "c"), None),
        P(),
        P(),
        P(("y", "zl", "c"), None, None),
        P(("y", "zl", "c"), None, None),
    )
    return jax.shard_map(
        body,
        mesh=split,
        in_specs=placed,
        out_specs=(P(axes, None), P(("x", "zh", "y"), ("zl", "c"))),
        check_vma=False,
    )
```

```python
import jax
import jax.numpy as jnp
from jax import lax
from jax.experimental import pallas as pl
from jax.experimental.pallas import tpu as pltpu
from jax.sharding import Mesh
from jax.sharding import PartitionSpec as P

CAP = 24
epsilon = 1e-06
masked_score = -1e30
log2e = 1.4426950408889634

X, ZH, Y, ZL, C = 4, 2, 4, 4, 2


def rms_scale(rows, gain):
    values = rows.astype(jnp.float32)
    inverse = lax.rsqrt(jnp.mean(values * values, axis=-1, keepdims=True) + epsilon)
    return (values * inverse * gain).astype(jnp.bfloat16)


def swap_core(a):
    return lax.ppermute(a, "c", [(0, 1), (1, 0)])


def shift_line(a, s):
    return lax.ppermute(a, "zl", [(i, (i + s) % ZL) for i in range(ZL)])


def shift_y(a, s):
    pairs = []
    for y in range(Y):
        for c in range(C):
            t = (y + (s if c == 0 else -s)) % Y
            pairs.append((y * C + c, t * C + c))
    return lax.ppermute(a, ("y", "c"), pairs)


def shift_z(a, s):
    pairs = []
    n = ZH * ZL
    for z in range(n):
        for c in range(C):
            t = (z + (s if c == 0 else -s)) % n
            pairs.append((z * C + c, t * C + c))
    return lax.ppermute(a, ("zh", "zl", "c"), pairs)


def attention_kernel(
    meta, q_ref, own_ref, a_ref, b_ref, f_ref, o_ref, qs, m_ref, l_ref, acc_ref, *, pages, fresh
):
    rows = qs.shape[0]
    heads = rows // 256
    scale = log2e / float(128) ** 0.5
    y, zl, c, length = meta[0], meta[1], meta[2], meta[3]
    for s in range(heads):
        h = lax.rem(zl - s + 4, 4)
        qs[s * 256 : (s + 1) * 256, :] = q_ref[:, pl.ds(pl.multiple_of(h * 128, 128), 128)]

    def scores_of(keys):
        return (
            lax.dot_general(
                qs[...], keys, (((1,), (1,)), ((), ())), preferred_element_type=jnp.float32
            )
            * scale
        )

    def fold(scores, values):
        old = m_ref[...]
        new = jnp.maximum(old, jnp.max(scores, axis=1, keepdims=True))
        m_ref[...] = new
        weights = jnp.exp2(scores - new[:, :1])
        factor = jnp.exp2(old - new)
        l_ref[...] = l_ref[...] * factor + jnp.sum(weights, axis=1, keepdims=True)
        acc_ref[...] = acc_ref[...] * factor + jnp.dot(
            weights.astype(jnp.bfloat16), values, preferred_element_type=jnp.float32
        )

    m_ref[...] = jnp.full(m_ref.shape, masked_score, jnp.float32)
    l_ref[...] = jnp.zeros(l_ref.shape, jnp.float32)
    acc_ref[...] = jnp.zeros(acc_ref.shape, jnp.float32)

    def half_of(index):
        return ((index % 256) // 128) * (1 - 2 * c) + c

    key = lax.broadcasted_iota(jnp.int32, (1, fresh), 1)
    key_chip = (zl - key // 256 + 4) % 4
    key_pos = key_chip * 256 + half_of(key) * 128 + key % 128
    row = lax.broadcasted_iota(jnp.int32, (rows, 1), 0)
    row_pos = zl * 256 + half_of(row) * 128 + row % 128
    scores = scores_of(own_ref[pages:, :128])
    scores = jnp.where(key_pos <= row_pos, scores, masked_score)
    fold(scores, own_ref[pages:, 128:])

    step = 1 - 2 * c
    shards = ((own_ref, y), (a_ref, y - step), (b_ref, y + step), (f_ref, y + 2))
    page = lax.broadcasted_iota(jnp.int32, (1, pages), 1)
    for ref, source in shards:
        source = lax.rem(source + 4, 4)
        position = (page // 64 * 4 + source) * 64 + page % 64
        scores = scores_of(ref[:pages, :128])
        scores = jnp.where(position < length, scores, masked_score)
        fold(scores, ref[:pages, 128:])
        if ref is not own_ref:

            @pl.when(source < y)
            def _(ref=ref):
                fold(scores_of(ref[pages:, :128]), ref[pages:, 128:])

    done = (acc_ref[...] / l_ref[...]).astype(o_ref.dtype)
    for s in range(heads):
        o_ref[:, s * 128 : (s + 1) * 128] = done[s * 256 : (s + 1) * 256, :]


def order_kernel(meta, x_ref, o_ref):
    zl, c = meta[1], meta[2]
    col = pl.multiple_of(lax.rem(zl, 2) * 128, 128)
    for z in range(ZL):
        slot = lax.rem(zl - z + 4, 4)
        for half in range(2):
            inner = half * (1 - 2 * c) + c
            start = pl.multiple_of(slot * 256 + inner * 128, 128)
            o_ref[z * 256 + half * 128 : z * 256 + half * 128 + 128, :] = x_ref[
                pl.ds(start, 128), pl.ds(col, 128)
            ]


def body(
    hidden_in,
    routes,
    prefix_len,
    cache,
    attn_gain,
    w_query,
    w_keyval,
    w_out,
    moe_gain,
    w_router,
    expert_in,
    expert_out,
):
    y, zl, c = lax.axis_index("y"), lax.axis_index("zl"), lax.axis_index("c")
    rep = lax.axis_index(("x", "zh"))
    rows_dev, width = hidden_in.shape
    length = lax.dynamic_index_in_dim(prefix_len, rep, 0, keepdims=False)
    meta = jnp.stack([y, zl, c, length]).astype(jnp.int32)
    smem = pl.BlockSpec(memory_space=pltpu.SMEM)
    vmem = pl.BlockSpec(memory_space=pltpu.VMEM)

    group_size = 4
    with jax.named_scope("weights"):
        wq_all = lax.all_gather(w_query, ("zl", "c"), axis=0, tiled=False)
        to_group = []
        for z in range(ZL):
            for k in range(C):
                to_group.append((z * C + k, (2 * (z % 2) + k) * C + z // 2))
        wo_here = lax.ppermute(w_out, ("zl", "c"), to_group)
        wo = jnp.concatenate([wo_here] + [shift_line(wo_here, s) for s in (1, 2, 3)], axis=0)

    with jax.named_scope("pages"):
        own_pages = lax.dynamic_index_in_dim(cache, c, 1, keepdims=True)
        fetched = lax.all_to_all(own_pages, ("x", "zh"), split_axis=0, concat_axis=2, tiled=True)
        pages = fetched.reshape(-1, 256)

    with jax.named_scope("keys"):
        normed = rms_scale(hidden_in, attn_gain)
        both = jnp.concatenate([normed, swap_core(normed)], axis=0)
        w_kv = lax.dynamic_index_in_dim(w_keyval, c, 0, keepdims=False)
        kv = jnp.dot(both, w_kv, preferred_element_type=jnp.float32).astype(jnp.bfloat16)
        line = [kv] + [shift_line(kv, s) for s in (1, 2, 3)]
        shard = jnp.concatenate([pages] + line, axis=0)
        up = shift_y(shard, 1)
        down = shift_y(shard, -1)
        far = shift_y(up, 1)

    with jax.named_scope("new_cache"):
        ordered = pl.pallas_call(
            order_kernel,
            out_shape=jax.ShapeDtypeStruct((1024, 128), jnp.bfloat16),
            in_specs=[smem, vmem],
            out_specs=vmem,
        )(meta, jnp.concatenate(line, axis=0))
        other = swap_core(ordered)
        held = jnp.where(c == zl // 2, ordered, other)
        new_cache = jnp.where(c == 0, held[:, :64], held[:, 64:])

    with jax.named_scope("queries"):
        wq = lax.dynamic_slice_in_dim(wq_all, c * group_size, group_size, 0)
        queries = jnp.concatenate(
            [jnp.dot(both, wq[h], preferred_element_type=jnp.float32) for h in range(group_size)],
            axis=1,
        ).astype(jnp.bfloat16)

    with jax.named_scope("attention"):
        n_pages = pages.shape[0]
        n_rows = 2 * rows_dev * group_size
        attended = pl.pallas_call(
            lambda *refs: attention_kernel(*refs, pages=n_pages, fresh=1024),
            out_shape=jax.ShapeDtypeStruct((2 * rows_dev, group_size * 128), jnp.bfloat16),
            in_specs=[smem] + [vmem] * 5,
            out_specs=vmem,
            scratch_shapes=[
                pltpu.VMEM((n_rows, 128), jnp.bfloat16),
                pltpu.VMEM((n_rows, 128), jnp.float32),
                pltpu.VMEM((n_rows, 128), jnp.float32),
                pltpu.VMEM((n_rows, 128), jnp.float32),
            ],
            compiler_params=pltpu.CompilerParams(vmem_limit_bytes=48 * 2**20),
            cost_estimate=pl.CostEstimate(
                flops=4 * n_rows * 6144 * 128,
                bytes_accessed=4 * 2**20,
                transcendentals=n_rows * 6144,
            ),
            name="attention",
        )(meta, queries, shard, up, down, far)

    with jax.named_scope("out_projection"):
        partial = jnp.dot(attended, wo, preferred_element_type=jnp.float32)
        received = swap_core(partial[rows_dev:])
        mid = (hidden_in.astype(jnp.float32) + (partial[:rows_dev] + received)).astype(jnp.bfloat16)
        normed_moe = rms_scale(mid, moe_gain)

    with jax.named_scope("routing"):
        step = 1 - 2 * c
        z = lax.axis_index(("zh", "zl"))
        y_slots = jnp.stack([y, y - step, y + step, y + 2]) % Y
        z_slots = jnp.stack([z, z - step, z + step, z - 2 * step]) % (ZH * ZL)
        y_goals = jnp.stack([y, y + step, y - step, y + 2]) % Y
        z_goals = jnp.stack([z, z + step, z - step, z + 2 * step]) % ZL
        cores = jnp.stack([c, 1 - c])
        experts_all = w_router.shape[1]
        top = routes.shape[1]
        half = width // 2
        matches = routes[:, :, None] == jnp.arange(experts_all, dtype=jnp.int32)[None, None, :]
        named = jnp.sum(matches.astype(jnp.float32), axis=1)
        lower = (jnp.arange(rows_dev)[:, None] > jnp.arange(rows_dev)[None, :]).astype(jnp.float32)
        before = jnp.dot(lower, named, preferred_element_type=jnp.float32)
        slot = jnp.sum(jnp.where(matches, before[:, None, :], 0.0), axis=2).astype(jnp.int32)
        target = (routes * CAP + slot).T
        routes_t = routes.T
        target, wq_all = lax.optimization_barrier((target, wq_all))
        target_y = lax.all_gather(target, "y", axis=0)
        target_z = lax.all_gather(target, ("zh", "zl"), axis=0)
        spread = experts_all * CAP

        def pick(table, slots):
            return jnp.concatenate(
                [lax.dynamic_index_in_dim(table, slots[i], 0, keepdims=False) for i in range(4)],
                axis=1,
            )

        source_mark = (jnp.arange(4 * rows_dev, dtype=jnp.int32) // rows_dev * spread)[None, :]
        named_z = pick(target_z, z_slots) + source_mark
        named_y = pick(target_y, y_slots) + source_mark

        def keys_of(first):
            inner = jnp.arange(4, dtype=jnp.int32)[:, None] * spread + jnp.arange(CAP, dtype=jnp.int32)
            return (first[:, :, None, None] * CAP + inner[None, None]).reshape(-1)

        keys_1 = keys_of(y_goals[:, None] * 8 + (z % ZL) * 2 + cores[None, :])
        keys_2 = keys_of(y * 8 + z_goals[:, None] * 2 + cores[None, :])

        def placed_of(keys, table):
            return sum((keys[:, None] == table[k : k + 1]) for k in range(top)).astype(jnp.bfloat16)

        placed_1, placed_2 = placed_of(keys_1, named_z), placed_of(keys_2, named_y)

    def to_y(a, s):
        return shift_y(a, s)

    def to_z(a, s):
        return shift_z(a, s)

    def spread_out(a, send):
        return [a, send(a, 1), send(a, -1), send(a, 2)]

    block = 2 * 4 * CAP

    with jax.named_scope("dispatch"):
        near_1 = jnp.concatenate(spread_out(normed_moe[:, :half], to_z), axis=0)
        near_2 = jnp.concatenate(spread_out(normed_moe[:, half:], to_y), axis=0)

        def pack(placed, near, send):
            out = []
            for d, s in enumerate((0, 1, -1, 2)):
                packed = jnp.dot(
                    placed[d * block : (d + 1) * block], near, preferred_element_type=jnp.float32
                ).astype(jnp.bfloat16)
                out.append((send(packed, s) if s else packed).reshape(2, 4, CAP, half))
            return out

        held_1 = pack(placed_1, near_1, to_y)
        held_2 = pack(placed_2, near_2, to_z)

        def joined(core):
            return jnp.concatenate(
                [
                    jnp.stack([a[core] for a in held_1], axis=0),
                    jnp.stack([a[core] for a in held_2], axis=1),
                ],
                axis=-1,
            ).reshape(16 * CAP, width)

        passed = swap_core(joined(1))
        kept = joined(0)

    with jax.named_scope("gates"):
        logits = lax.dot_general(
            w_router, normed_moe, (((0,), (1,)), ((), ())), preferred_element_type=jnp.float32
        )
        here = routes_t[:, None, :] == jnp.arange(experts_all, dtype=jnp.int32)[None, :, None]
        raised = jnp.exp(jnp.sum(jnp.where(here, logits[None], 0.0), axis=1))
        gates = raised / jnp.sum(raised, axis=0, keepdims=True)
        gates_y = lax.all_gather(gates, "y", axis=0)
        gates_z = lax.all_gather(gates, ("zh", "zl"), axis=0)

        def mix_of(keys, table, weights):
            mix = sum(
                jnp.where(keys[:, None] == table[k : k + 1], weights[k : k + 1], 0.0)
                for k in range(top)
            )
            high = mix.astype(jnp.bfloat16)
            low = (mix - high.astype(jnp.float32)).astype(jnp.bfloat16)
            return jnp.concatenate([high, low], axis=1)

        mix_1 = mix_of(keys_1, named_z, pick(gates_z, z_slots))
        mix_2 = mix_of(keys_2, named_y, pick(gates_y, y_slots))

    with jax.named_scope("experts"):
        inner_dim = expert_out.shape[1]

        def expert(rows):
            inner = jnp.dot(rows, expert_in[0], preferred_element_type=jnp.float32)
            active = (jnp.maximum(inner[:, :inner_dim], 0.0) * inner[:, inner_dim:]).astype(
                jnp.bfloat16
            )
            return jnp.dot(active, expert_out[0], preferred_element_type=jnp.float32).astype(
                jnp.bfloat16
            )

        shape = (4, 4, CAP, width)
        passed_back = swap_core(expert(passed)).reshape(shape)
        kept_back = expert(kept).reshape(shape)

    with jax.named_scope("combine"):

        def give_back(parts, send):
            out = []
            for d, s in enumerate((0, -1, 1, -2)):
                out.append(send(parts[d], s) if s else parts[d])
            return out

        parts_1 = [
            jnp.stack([kept_back[i, :, :, :half], passed_back[i, :, :, :half]]).reshape(block, half)
            for i in range(4)
        ]
        parts_2 = [
            jnp.stack([kept_back[:, j, :, half:], passed_back[:, j, :, half:]]).reshape(block, half)
            for j in range(4)
        ]

        def summed(mix, parts, send, back):
            rows = jnp.concatenate(give_back(parts, send), axis=0)
            both_sums = lax.dot_general(
                mix, rows, (((0,), (0,)), ((), ())), preferred_element_type=jnp.float32
            )
            sums = both_sums[: 4 * rows_dev] + both_sums[4 * rows_dev :]
            mine = sums[:rows_dev]
            away = [
                sums[d * rows_dev : (d + 1) * rows_dev].astype(jnp.bfloat16) for d in range(4)
            ]
            return [mine] + give_back(away, back)[1:]

        total_1 = summed(mix_1, parts_1, to_y, to_z)
        total_2 = summed(mix_2, parts_2, to_z, to_y)
        mixed = jnp.concatenate(
            [sum(a.astype(jnp.float32) for a in t) for t in (total_1, total_2)], axis=1
        )
        hidden_out = (mid.astype(jnp.float32) + mixed).astype(jnp.bfloat16)
    return (hidden_out, new_cache)


def solution(mesh):
    axes = ("x", "zh", "y", "zl", "c")
    split = Mesh(mesh.devices.reshape(X, ZH, Y, ZL, C), axes)
    placed = (
        P(axes, None),
        P(axes, None),
        P(),
        P(None, None, ("x", "zh", "y"), None),
        P(),
        P(None, ("zl", "c")),
        P(),
        P(("zl", "c"), None),
        P(),
        P(),
        P(("y", "zl", "c"), None, None),
        P(("y", "zl", "c"), None, None),
    )
    return jax.shard_map(
        body,
        mesh=split,
        in_specs=placed,
        out_specs=(P(axes, None), P(("x", "zh", "y"), ("zl", "c"))),
        check_vma=False,
    )
```

```python
import jax
import jax.numpy as jnp
from jax import lax
from jax.experimental import pallas as pl
from jax.experimental.pallas import tpu as pltpu
from jax.sharding import Mesh
from jax.sharding import PartitionSpec as P

CAP = 24
epsilon = 1e-06
masked_score = -1e30
log2e = 1.4426950408889634

X, ZH, Y, ZL, C = 4, 2, 4, 4, 2


def rms_scale(rows, gain):
    values = rows.astype(jnp.float32)
    inverse = lax.rsqrt(jnp.mean(values * values, axis=-1, keepdims=True) + epsilon)
    return (values * inverse * gain).astype(jnp.bfloat16)


def swap_core(a):
    return lax.ppermute(a, "c", [(0, 1), (1, 0)])


def shift_line(a, s):
    return lax.ppermute(a, "zl", [(i, (i + s) % ZL) for i in range(ZL)])


def shift_y(a, s):
    pairs = []
    for y in range(Y):
        for c in range(C):
            t = (y + (s if c == 0 else -s)) % Y
            pairs.append((y * C + c, t * C + c))
    return lax.ppermute(a, ("y", "c"), pairs)


def shift_z(a, s):
    pairs = []
    n = ZH * ZL
    for z in range(n):
        for c in range(C):
            t = (z + (s if c == 0 else -s)) % n
            pairs.append((z * C + c, t * C + c))
    return lax.ppermute(a, ("zh", "zl", "c"), pairs)


def attention_kernel(meta, q_ref, *refs, sources, first, last, pages, heads):
    refs = list(refs)
    shards = [refs.pop(0) for _ in sources]
    before = None if first else (refs.pop(0), refs.pop(0))
    outs = [refs.pop(0)] if last else [refs.pop(0), refs.pop(0)]
    keys_ref, values_ref, m_ref, sum_ref = refs
    span = keys_ref.shape[0]
    rows = q_ref.shape[0] // heads
    scale = log2e / float(128) ** 0.5
    y, zl, c, length = meta[0], meta[1], meta[2], meta[3]
    if first:
        m_ref[...] = jnp.full(m_ref.shape, masked_score, jnp.float32)
        sum_ref[...] = jnp.zeros(sum_ref.shape, jnp.float32)
    else:
        m_ref[...] = before[0][...]
        sum_ref[...] = before[1][...]
    values_ref[:, 128:] = jnp.ones((span, 128), jnp.bfloat16)

    def half_of(index):
        return ((index % 256) // 128) * (1 - 2 * c) + c

    key = lax.broadcasted_iota(jnp.int32, (1, span), 1)
    fresh = key - pages

    def fold(index, _):
        away = 0
        for i, ref in enumerate(shards):
            away = jnp.where(index == i, sources[i], away)

            @pl.when(index == i)
            def _(ref=ref):
                keys_ref[...] = ref[:, :128]
                values_ref[:, :128] = ref[:, 128:]

        source = lax.rem(y + away * (1 - 2 * c) + 4, 4)
        position = (key // 64 * 4 + source) * 64 + key % 64
        if first:
            place = ((zl - fresh // 256 + 4) % 4) * 256 + half_of(fresh) * 128 + fresh % 128
            bound = jnp.where(key < pages, jnp.where(position < length, -1, 2**20), place)
            row = lax.broadcasted_iota(jnp.int32, (rows, 1), 0)
            row_place = zl * 256 + half_of(row) * 128 + row % 128
            visible = bound <= row_place
        else:
            visible = jnp.where(key < pages, position, source) < jnp.where(key < pages, length, y)
        for h in range(heads):
            part = pl.ds(h * rows, rows)
            scores = lax.dot_general(
                q_ref[part, :],
                keys_ref[...],
                (((1,), (1,)), ((), ())),
                preferred_element_type=jnp.float32,
            )
            scores = jnp.where(visible, scores, masked_score)
            old = m_ref[part, :]
            new = jnp.maximum(old, jnp.max(scores, axis=1, keepdims=True))
            m_ref[part, :] = new
            weights = jnp.exp2(scores * scale - new[:, :1] * scale)
            factor = jnp.exp2((old - new) * scale)
            sum_ref[part, :] = sum_ref[part, :] * jnp.concatenate([factor, factor], axis=1) + jnp.dot(
                weights.astype(jnp.bfloat16), values_ref[...], preferred_element_type=jnp.float32
            )
        return 0

    lax.fori_loop(0, len(shards), fold, 0)
    if last:
        done = (sum_ref[:, :128] / sum_ref[:, 128:]).astype(jnp.bfloat16)
        for h in range(heads):
            outs[0][:, h * 128 : (h + 1) * 128] = done[h * rows : (h + 1) * rows, :]
    else:
        outs[0][...] = m_ref[...]
        outs[1][...] = sum_ref[...]


def attention(meta, queries, shards, sources, state, last, pages):
    heads = 4
    n, span = queries.shape[0], shards[0].shape[0]
    vmem = pl.BlockSpec(memory_space=pltpu.VMEM)
    kinds = (
        [jax.ShapeDtypeStruct((n // heads, heads * 128), jnp.bfloat16)]
        if last
        else [
            jax.ShapeDtypeStruct((n, 128), jnp.float32),
            jax.ShapeDtypeStruct((n, 256), jnp.float32),
        ]
    )
    return pl.pallas_call(
        lambda *refs: attention_kernel(
            *refs, sources=sources, first=not state, last=last, pages=pages, heads=heads
        ),
        out_shape=kinds,
        in_specs=[pl.BlockSpec(memory_space=pltpu.SMEM)]
        + [vmem] * (1 + len(shards) + len(state)),
        out_specs=[vmem] * len(kinds),
        scratch_shapes=[
            pltpu.VMEM((span, 128), jnp.bfloat16),
            pltpu.VMEM((span, 256), jnp.bfloat16),
            pltpu.VMEM((n, 128), jnp.float32),
            pltpu.VMEM((n, 256), jnp.float32),
        ],
        compiler_params=pltpu.CompilerParams(vmem_limit_bytes=40 * 2**20),
        cost_estimate=pl.CostEstimate(
            flops=6 * n * span * 128 * len(shards),
            bytes_accessed=4 * 2**20,
            transcendentals=n * span * len(shards),
        ),
        name="attention",
    )(meta, queries, *shards, *state)


def order_kernel(meta, x_ref, o_ref):
    zl, c = meta[1], meta[2]
    col = pl.multiple_of(lax.rem(zl, 2) * 128, 128)
    for z in range(ZL):
        slot = lax.rem(zl - z + 4, 4)
        for half in range(2):
            inner = half * (1 - 2 * c) + c
            start = pl.multiple_of(slot * 256 + inner * 128, 128)
            o_ref[z * 256 + half * 128 : z * 256 + half * 128 + 128, :] = x_ref[
                pl.ds(start, 128), pl.ds(col, 128)
            ]


def body(
    hidden_in,
    routes,
    prefix_len,
    cache,
    attn_gain,
    w_query,
    w_keyval,
    w_out,
    moe_gain,
    w_router,
    expert_in,
    expert_out,
):
    y, zl, c = lax.axis_index("y"), lax.axis_index("zl"), lax.axis_index("c")
    rep = lax.axis_index(("x", "zh"))
    rows_dev, width = hidden_in.shape
    length = lax.dynamic_index_in_dim(prefix_len, rep, 0, keepdims=False)
    meta = jnp.stack([y, zl, c, length]).astype(jnp.int32)
    smem = pl.BlockSpec(memory_space=pltpu.SMEM)
    vmem = pl.BlockSpec(memory_space=pltpu.VMEM)

    group_size = 4
    to_group = []
    for z in range(ZL):
        for k in range(C):
            to_group.append((z * C + k, (2 * (z % 2) + k) * C + z // 2))

    def line_of(a):
        return [a] + [shift_line(a, s) for s in (1, 2, 3)]

    with jax.named_scope("keys"):
        part = width // X
        quarter = lax.dynamic_slice_in_dim(w_query, lax.axis_index("x") * part, part, 0)
        quarter = lax.ppermute(quarter, ("zl", "c"), to_group)
        normed = rms_scale(hidden_in, attn_gain)
        quarter, normed = lax.optimization_barrier((quarter, normed))
        both = jnp.concatenate([normed, swap_core(normed)], axis=0)
        w_kv = lax.dynamic_index_in_dim(w_keyval, c, 0, keepdims=False)
        kv = jnp.dot(both, w_kv, preferred_element_type=jnp.float32).astype(jnp.bfloat16)
        own_pages = lax.dynamic_index_in_dim(cache, c, 1, keepdims=True)
        heads = jnp.stack(line_of(quarter))
        line = line_of(kv)
        own_pages, _ = lax.optimization_barrier((own_pages, kv))
        heads, _ = lax.optimization_barrier((heads, kv))
        fetched = lax.all_to_all(own_pages, ("x", "zh"), split_axis=0, concat_axis=2, tiled=True)
        pages = fetched.reshape(-1, 256)
        wq = lax.all_gather(heads, "x", axis=1, tiled=True)
        shard = jnp.concatenate([pages] + line, axis=0)
        shard, w_out = lax.optimization_barrier((shard, w_out))
        up = shift_y(shard, 1)
        down = shift_y(shard, -1)
        far = shift_y(up, 1)

    with jax.named_scope("weights"):
        wo = jnp.concatenate(line_of(lax.ppermute(w_out, ("zl", "c"), to_group)), axis=0)

    with jax.named_scope("new_cache"):
        ordered = pl.pallas_call(
            order_kernel,
            out_shape=jax.ShapeDtypeStruct((1024, 128), jnp.bfloat16),
            in_specs=[smem, vmem],
            out_specs=vmem,
        )(meta, jnp.concatenate(line, axis=0))
        other = swap_core(ordered)
        held = jnp.where(c == zl // 2, ordered, other)
        new_cache = jnp.where(c == 0, held[:, :64], held[:, 64:])

    with jax.named_scope("queries"):
        queries = jnp.concatenate(
            [jnp.dot(both, wq[h], preferred_element_type=jnp.float32) for h in range(group_size)],
            axis=0,
        ).astype(jnp.bfloat16)

    with jax.named_scope("attention"):
        n_pages = pages.shape[0]
        queries, new_cache = lax.optimization_barrier((queries, new_cache))
        state = attention(meta, queries, [shard], [0], (), False, n_pages)
        state = attention(meta, queries, [up, down], [-1, 1], state, False, n_pages)
        (attended,) = attention(meta, queries, [far], [2], state, True, n_pages)

    with jax.named_scope("out_projection"):
        partial = jnp.dot(attended, wo, preferred_element_type=jnp.float32)
        received = swap_core(partial[rows_dev:])
        mid = (hidden_in.astype(jnp.float32) + (partial[:rows_dev] + received)).astype(jnp.bfloat16)
        normed_moe = rms_scale(mid, moe_gain)

    with jax.named_scope("routing"):
        step = 1 - 2 * c
        z = lax.axis_index(("zh", "zl"))
        y_goals = jnp.stack([y, y + step, y - step, y + 2]) % Y
        z_goals = jnp.stack([z, z + step, z - step, z + 2 * step]) % ZL
        cores = jnp.stack([c, 1 - c])
        experts_all = w_router.shape[1]
        top = routes.shape[1]
        half = width // 2
        matches = routes[:, :, None] == jnp.arange(experts_all, dtype=jnp.int32)[None, None, :]
        named = jnp.sum(matches.astype(jnp.float32), axis=1)
        lower = (jnp.arange(rows_dev)[:, None] > jnp.arange(rows_dev)[None, :]).astype(jnp.float32)
        before = jnp.dot(lower, named, preferred_element_type=jnp.float32)
        slot = jnp.sum(jnp.where(matches, before[:, None, :], 0.0), axis=2)
        spread = experts_all * CAP

        def keys_of(first):
            inner = jnp.arange(4, dtype=jnp.int32)[:, None] * spread + jnp.arange(CAP, dtype=jnp.int32)
            return (first[:, :, None, None] * CAP + inner[None, None]).reshape(1, -1)

        keys_1 = keys_of(y_goals[:, None] * 8 + (z % ZL) * 2 + cores[None, :])
        keys_2 = keys_of(y * 8 + z_goals[:, None] * 2 + cores[None, :])

    with jax.named_scope("gates"):
        logits = jnp.dot(normed_moe, w_router, preferred_element_type=jnp.float32)
        raised = jnp.exp(jnp.sum(jnp.where(matches, logits[:, None, :], 0.0), axis=2))
        gates = raised / jnp.sum(raised, axis=1, keepdims=True)
        gates_high = gates.astype(jnp.bfloat16)
        gates_low = (gates - gates_high.astype(jnp.float32)).astype(jnp.bfloat16)
        table = jnp.concatenate(
            [
                routes.astype(jnp.bfloat16),
                slot.astype(jnp.bfloat16),
                gates_high,
                gates_low,
                jnp.zeros((rows_dev, 128 - 4 * top), jnp.bfloat16),
            ],
            axis=1,
        )

    def to_y(a, s):
        return shift_y(a, s)

    def to_z(a, s):
        return shift_z(a, s)

    def spread_out(a, send):
        return [a, send(a, 1), send(a, -1), send(a, 2)]

    block = 2 * 4 * CAP

    with jax.named_scope("dispatch"):
        near_1 = jnp.concatenate(
            spread_out(jnp.concatenate([normed_moe[:, :half], table], axis=1), to_z), axis=0
        )
        near_2 = jnp.concatenate(
            spread_out(jnp.concatenate([normed_moe[:, half:], table], axis=1), to_y), axis=0
        )

        def named_of(near):
            ids = near[:, half : half + top].astype(jnp.int32)
            slots = near[:, half + top : half + 2 * top].astype(jnp.int32)
            source = lax.broadcasted_iota(jnp.int32, ids.shape, 0) // rows_dev
            return ids * CAP + slots + source * spread

        def placed_of(keys, named):
            return sum((named[:, k : k + 1] == keys) for k in range(top)).astype(jnp.bfloat16)

        named_1, named_2 = named_of(near_1), named_of(near_2)
        placed_1, placed_2 = placed_of(keys_1, named_1), placed_of(keys_2, named_2)

        def pack(placed, near, send):
            out = []
            for d, s in enumerate((0, 1, -1, 2)):
                packed = lax.dot_general(
                    placed[:, d * block : (d + 1) * block],
                    near[:, :half],
                    (((0,), (0,)), ((), ())),
                    preferred_element_type=jnp.float32,
                ).astype(jnp.bfloat16)
                out.append((send(packed, s) if s else packed).reshape(2, 4, CAP, half))
            return out

        held_1 = pack(placed_1, near_1, to_y)
        held_2 = pack(placed_2, near_2, to_z)

        def joined(core):
            return jnp.concatenate(
                [
                    jnp.stack([a[core] for a in held_1], axis=0),
                    jnp.stack([a[core] for a in held_2], axis=1),
                ],
                axis=-1,
            ).reshape(16 * CAP, width)

        passed = swap_core(joined(1))
        kept = joined(0)

    with jax.named_scope("mix"):

        def mix_of(keys, named, near):
            def weighted(first):
                return sum(
                    jnp.where(
                        named[:, k : k + 1] == keys,
                        near[:, half + first + k : half + first + k + 1].astype(jnp.float32),
                        0.0,
                    )
                    for k in range(top)
                ).astype(jnp.bfloat16)

            return jnp.concatenate([weighted(2 * top), weighted(3 * top)], axis=0)

        mix_1 = mix_of(keys_1, named_1, near_1)
        mix_2 = mix_of(keys_2, named_2, near_2)

    with jax.named_scope("experts"):
        inner_dim = expert_out.shape[1]

        def expert(rows):
            inner = jnp.dot(rows, expert_in[0], preferred_element_type=jnp.float32)
            active = (jnp.maximum(inner[:, :inner_dim], 0.0) * inner[:, inner_dim:]).astype(
                jnp.bfloat16
            )
            return jnp.dot(active, expert_out[0], preferred_element_type=jnp.float32).astype(
                jnp.bfloat16
            )

        shape = (4, 4, CAP, width)
        passed_back = swap_core(expert(passed)).reshape(shape)
        kept_back = expert(kept).reshape(shape)

    with jax.named_scope("combine"):

        def give_back(parts, send):
            out = []
            for d, s in enumerate((0, -1, 1, -2)):
                out.append(send(parts[d], s) if s else parts[d])
            return out

        parts_1 = [
            jnp.stack([kept_back[i, :, :, :half], passed_back[i, :, :, :half]]).reshape(block, half)
            for i in range(4)
        ]
        parts_2 = [
            jnp.stack([kept_back[:, j, :, half:], passed_back[:, j, :, half:]]).reshape(block, half)
            for j in range(4)
        ]

        def summed(mix, parts, send, back):
            rows = jnp.concatenate(give_back(parts, send), axis=0)
            both_sums = jnp.dot(mix, rows, preferred_element_type=jnp.float32)
            sums = both_sums[: 4 * rows_dev] + both_sums[4 * rows_dev :]
            mine = sums[:rows_dev]
            away = [
                sums[d * rows_dev : (d + 1) * rows_dev].astype(jnp.bfloat16) for d in range(4)
            ]
            return [mine] + give_back(away, back)[1:]

        total_1 = summed(mix_1, parts_1, to_y, to_z)
        total_2 = summed(mix_2, parts_2, to_z, to_y)
        mixed = jnp.concatenate(
            [sum(a.astype(jnp.float32) for a in t) for t in (total_1, total_2)], axis=1
        )
        hidden_out = (mid.astype(jnp.float32) + mixed).astype(jnp.bfloat16)
    return (hidden_out, new_cache)


def solution(mesh):
    axes = ("x", "zh", "y", "zl", "c")
    split = Mesh(mesh.devices.reshape(X, ZH, Y, ZL, C), axes)
    placed = (
        P(axes, None),
        P(axes, None),
        P(),
        P(None, None, ("x", "zh", "y"), None),
        P(),
        P(None, ("zl", "c")),
        P(),
        P(("zl", "c"), None),
        P(),
        P(),
        P(("y", "zl", "c"), None, None),
        P(("y", "zl", "c"), None, None),
    )
    return jax.shard_map(
        body,
        mesh=split,
        in_specs=placed,
        out_specs=(P(axes, None), P(("x", "zh", "y"), ("zl", "c"))),
        check_vma=False,
    )
```

```python
import jax
import jax.numpy as jnp
from jax import lax
from jax.experimental import pallas as pl
from jax.experimental.pallas import tpu as pltpu
from jax.sharding import Mesh
from jax.sharding import PartitionSpec as P

CAP = 24
epsilon = 1e-06
masked_score = -1e30
log2e = 1.4426950408889634

X, ZH, Y, ZL, C = 4, 2, 4, 4, 2


def rms_scale(rows, gain):
    values = rows.astype(jnp.float32)
    inverse = lax.rsqrt(jnp.mean(values * values, axis=-1, keepdims=True) + epsilon)
    return (values * inverse * gain).astype(jnp.bfloat16)


def swap_core(a):
    return lax.ppermute(a, "c", [(0, 1), (1, 0)])


def shift_line(a, s):
    return lax.ppermute(a, "zl", [(i, (i + s) % ZL) for i in range(ZL)])


def shift_y(a, s):
    pairs = []
    for y in range(Y):
        for c in range(C):
            t = (y + (s if c == 0 else -s)) % Y
            pairs.append((y * C + c, t * C + c))
    return lax.ppermute(a, ("y", "c"), pairs)


def shift_z(a, s):
    pairs = []
    n = ZH * ZL
    for z in range(n):
        for c in range(C):
            t = (z + (s if c == 0 else -s)) % n
            pairs.append((z * C + c, t * C + c))
    return lax.ppermute(a, ("zh", "zl", "c"), pairs)


def attention_kernel(meta, q_ref, *refs, sources, first, last, pages, heads):
    refs = list(refs)
    shards = [refs.pop(0) for _ in sources]
    before = None if first else (refs.pop(0), refs.pop(0))
    outs = [refs.pop(0)] if last else [refs.pop(0), refs.pop(0)]
    keys_ref, values_ref, m_ref, sum_ref = refs
    span = keys_ref.shape[0]
    rows = q_ref.shape[0] // heads
    scale = log2e / float(128) ** 0.5
    y, zl, c, length = meta[0], meta[1], meta[2], meta[3]
    if first:
        m_ref[...] = jnp.full(m_ref.shape, masked_score, jnp.float32)
        sum_ref[...] = jnp.zeros(sum_ref.shape, jnp.float32)
    else:
        m_ref[...] = before[0][...]
        sum_ref[...] = before[1][...]
    values_ref[:, 128:] = jnp.ones((span, 128), jnp.bfloat16)

    def half_of(index):
        return ((index % 256) // 128) * (1 - 2 * c) + c

    key = lax.broadcasted_iota(jnp.int32, (1, span), 1)
    fresh = key - pages

    def fold(index, _):
        away = 0
        for i, ref in enumerate(shards):
            away = jnp.where(index == i, sources[i], away)

            @pl.when(index == i)
            def _(ref=ref):
                keys_ref[...] = ref[:, :128]
                values_ref[:, :128] = ref[:, 128:]

        source = lax.rem(y + away * (1 - 2 * c) + 4, 4)
        position = (key // 64 * 4 + source) * 64 + key % 64
        if first:
            place = ((zl - fresh // 256 + 4) % 4) * 256 + half_of(fresh) * 128 + fresh % 128
            bound = jnp.where(key < pages, jnp.where(position < length, -1, 2**20), place)
            row = lax.broadcasted_iota(jnp.int32, (rows, 1), 0)
            row_place = zl * 256 + half_of(row) * 128 + row % 128
            visible = bound <= row_place
        else:
            visible = jnp.where(key < pages, position, source) < jnp.where(key < pages, length, y)
        for h in range(heads):
            part = pl.ds(h * rows, rows)
            scores = lax.dot_general(
                q_ref[part, :],
                keys_ref[...],
                (((1,), (1,)), ((), ())),
                preferred_element_type=jnp.float32,
            )
            scores = jnp.where(visible, scores, masked_score)
            old = m_ref[part, :]
            new = jnp.maximum(old, jnp.max(scores, axis=1, keepdims=True))
            m_ref[part, :] = new
            weights = jnp.exp2(scores * scale - new[:, :1] * scale)
            factor = jnp.exp2((old - new) * scale)
            sum_ref[part, :] = sum_ref[part, :] * jnp.concatenate([factor, factor], axis=1) + jnp.dot(
                weights.astype(jnp.bfloat16), values_ref[...], preferred_element_type=jnp.float32
            )
        return 0

    lax.fori_loop(0, len(shards), fold, 0)
    if last:
        done = (sum_ref[:, :128] / sum_ref[:, 128:]).astype(jnp.bfloat16)
        for h in range(heads):
            outs[0][:, h * 128 : (h + 1) * 128] = done[h * rows : (h + 1) * rows, :]
    else:
        outs[0][...] = m_ref[...]
        outs[1][...] = sum_ref[...]


def attention(meta, queries, shards, sources, state, last, pages):
    heads = 4
    n, span = queries.shape[0], shards[0].shape[0]
    vmem = pl.BlockSpec(memory_space=pltpu.VMEM)
    kinds = (
        [jax.ShapeDtypeStruct((n // heads, heads * 128), jnp.bfloat16)]
        if last
        else [
            jax.ShapeDtypeStruct((n, 128), jnp.float32),
            jax.ShapeDtypeStruct((n, 256), jnp.float32),
        ]
    )
    return pl.pallas_call(
        lambda *refs: attention_kernel(
            *refs, sources=sources, first=not state, last=last, pages=pages, heads=heads
        ),
        out_shape=kinds,
        in_specs=[pl.BlockSpec(memory_space=pltpu.SMEM)]
        + [vmem] * (1 + len(shards) + len(state)),
        out_specs=[vmem] * len(kinds),
        scratch_shapes=[
            pltpu.VMEM((span, 128), jnp.bfloat16),
            pltpu.VMEM((span, 256), jnp.bfloat16),
            pltpu.VMEM((n, 128), jnp.float32),
            pltpu.VMEM((n, 256), jnp.float32),
        ],
        compiler_params=pltpu.CompilerParams(vmem_limit_bytes=40 * 2**20),
        cost_estimate=pl.CostEstimate(
            flops=6 * n * span * 128 * len(shards),
            bytes_accessed=4 * 2**20,
            transcendentals=n * span * len(shards),
        ),
        name="attention",
    )(meta, queries, *shards, *state)


def order_kernel(meta, x_ref, o_ref):
    zl, c = meta[1], meta[2]
    col = pl.multiple_of(lax.rem(zl, 2) * 128, 128)
    for z in range(ZL):
        slot = lax.rem(zl - z + 4, 4)
        for half in range(2):
            inner = half * (1 - 2 * c) + c
            start = pl.multiple_of(slot * 256 + inner * 128, 128)
            o_ref[z * 256 + half * 128 : z * 256 + half * 128 + 128, :] = x_ref[
                pl.ds(start, 128), pl.ds(col, 128)
            ]


def body(
    hidden_in,
    routes,
    prefix_len,
    cache,
    attn_gain,
    w_query,
    w_keyval,
    w_out,
    moe_gain,
    w_router,
    expert_in,
    expert_out,
):
    y, zl, c = lax.axis_index("y"), lax.axis_index("zl"), lax.axis_index("c")
    rep = lax.axis_index(("x", "zh"))
    rows_dev, width = hidden_in.shape
    length = lax.dynamic_index_in_dim(prefix_len, rep, 0, keepdims=False)
    meta = jnp.stack([y, zl, c, length]).astype(jnp.int32)
    smem = pl.BlockSpec(memory_space=pltpu.SMEM)
    vmem = pl.BlockSpec(memory_space=pltpu.VMEM)

    group_size = 4
    to_group = []
    for z in range(ZL):
        for k in range(C):
            to_group.append((z * C + k, (2 * (z % 2) + k) * C + z // 2))

    def line_of(a):
        return [a] + [shift_line(a, s) for s in (1, 2, 3)]

    with jax.named_scope("weights"):
        wq_here = lax.ppermute(w_query, ("zl", "c"), to_group)
        wo_here = lax.ppermute(w_out, ("zl", "c"), to_group)

    with jax.named_scope("keys"):
        normed = rms_scale(hidden_in, attn_gain)
        both = jnp.concatenate([normed, swap_core(normed)], axis=0)
        w_kv = lax.dynamic_index_in_dim(w_keyval, c, 0, keepdims=False)
        kv = jnp.dot(both, w_kv, preferred_element_type=jnp.float32).astype(jnp.bfloat16)
        line = line_of(kv)
        own_pages = lax.dynamic_index_in_dim(cache, c, 1, keepdims=True)
        fetched = lax.all_to_all(own_pages, ("x", "zh"), split_axis=0, concat_axis=2, tiled=True)
        pages = fetched.reshape(-1, 256)
        shard = jnp.concatenate([pages] + line, axis=0)
        up = shift_y(shard, 1)
        down = shift_y(shard, -1)
        far = shift_y(up, 1)

    with jax.named_scope("new_cache"):
        ordered = pl.pallas_call(
            order_kernel,
            out_shape=jax.ShapeDtypeStruct((1024, 128), jnp.bfloat16),
            in_specs=[smem, vmem],
            out_specs=vmem,
        )(meta, jnp.concatenate(line, axis=0))
        other, wq_here, wo_here = lax.optimization_barrier((swap_core(ordered), wq_here, wo_here))
        held = jnp.where(c == zl // 2, ordered, other)
        new_cache = jnp.where(c == 0, held[:, :64], held[:, 64:])

    with jax.named_scope("weights"):
        wq = line_of(wq_here)
        wq, wo_here = lax.optimization_barrier((wq, wo_here))
        wo = jnp.concatenate(line_of(wo_here), axis=0)

    with jax.named_scope("routing"):
        experts_all = w_router.shape[1]
        top = routes.shape[1]
        matches = routes[:, :, None] == jnp.arange(experts_all, dtype=jnp.int32)[None, None, :]
        named = jnp.sum(matches.astype(jnp.float32), axis=1)
        lower = (jnp.arange(rows_dev)[:, None] > jnp.arange(rows_dev)[None, :]).astype(jnp.float32)
        before = jnp.dot(lower, named, preferred_element_type=jnp.float32)
        slot = jnp.sum(jnp.where(matches, before[:, None, :], 0.0), axis=2)

    with jax.named_scope("queries"):
        queries = jnp.concatenate(
            [jnp.dot(both, wq[h], preferred_element_type=jnp.float32) for h in range(group_size)],
            axis=0,
        ).astype(jnp.bfloat16)

    with jax.named_scope("attention"):
        n_pages = pages.shape[0]
        queries, new_cache, slot = lax.optimization_barrier((queries, new_cache, slot))
        state = attention(meta, queries, [shard], [0], (), False, n_pages)
        state = attention(meta, queries, [up, down], [-1, 1], state, False, n_pages)
        (attended,) = attention(meta, queries, [far], [2], state, True, n_pages)

    with jax.named_scope("out_projection"):
        partial = jnp.dot(attended, wo, preferred_element_type=jnp.float32)
        received = swap_core(partial[rows_dev:])
        mid = (hidden_in.astype(jnp.float32) + (partial[:rows_dev] + received)).astype(jnp.bfloat16)
        normed_moe = rms_scale(mid, moe_gain)

    with jax.named_scope("routing"):
        step = 1 - 2 * c
        z = lax.axis_index(("zh", "zl"))
        y_goals = jnp.stack([y, y + step, y - step, y + 2]) % Y
        z_goals = jnp.stack([z, z + step, z - step, z + 2 * step]) % ZL
        cores = jnp.stack([c, 1 - c])
        half = width // 2
        spread = experts_all * CAP

        def keys_of(first):
            inner = jnp.arange(4, dtype=jnp.int32)[:, None] * spread + jnp.arange(CAP, dtype=jnp.int32)
            return (first[:, :, None, None] * CAP + inner[None, None]).reshape(1, -1)

        keys_1 = keys_of(y_goals[:, None] * 8 + (z % ZL) * 2 + cores[None, :])
        keys_2 = keys_of(y * 8 + z_goals[:, None] * 2 + cores[None, :])

    with jax.named_scope("gates"):
        logits = jnp.dot(normed_moe, w_router, preferred_element_type=jnp.float32)
        raised = jnp.exp(jnp.sum(jnp.where(matches, logits[:, None, :], 0.0), axis=2))
        gates = raised / jnp.sum(raised, axis=1, keepdims=True)
        gates_high = gates.astype(jnp.bfloat16)
        gates_low = (gates - gates_high.astype(jnp.float32)).astype(jnp.bfloat16)
        table = jnp.concatenate(
            [
                routes.astype(jnp.bfloat16),
                slot.astype(jnp.bfloat16),
                gates_high,
                gates_low,
                jnp.zeros((rows_dev, 128 - 4 * top), jnp.bfloat16),
            ],
            axis=1,
        )

    def to_y(a, s):
        return shift_y(a, s)

    def to_z(a, s):
        return shift_z(a, s)

    def spread_out(a, send):
        return [a, send(a, 1), send(a, -1), send(a, 2)]

    block = 2 * 4 * CAP

    with jax.named_scope("dispatch"):
        near_1 = jnp.concatenate(
            spread_out(jnp.concatenate([normed_moe[:, :half], table], axis=1), to_z), axis=0
        )
        near_2 = jnp.concatenate(
            spread_out(jnp.concatenate([normed_moe[:, half:], table], axis=1), to_y), axis=0
        )

        def named_of(near):
            ids = near[:, half : half + top].astype(jnp.int32)
            slots = near[:, half + top : half + 2 * top].astype(jnp.int32)
            source = lax.broadcasted_iota(jnp.int32, ids.shape, 0) // rows_dev
            return ids * CAP + slots + source * spread

        def placed_of(keys, named):
            return sum((named[:, k : k + 1] == keys) for k in range(top)).astype(jnp.bfloat16)

        named_1, named_2 = named_of(near_1), named_of(near_2)
        placed_1, placed_2 = placed_of(keys_1, named_1), placed_of(keys_2, named_2)

        def pack(placed, near, send):
            out = []
            for d, s in enumerate((0, 1, -1, 2)):
                packed = lax.dot_general(
                    placed[:, d * block : (d + 1) * block],
                    near[:, :half],
                    (((0,), (0,)), ((), ())),
                    preferred_element_type=jnp.float32,
                ).astype(jnp.bfloat16)
                out.append((send(packed, s) if s else packed).reshape(2, 4, CAP, half))
            return out

        held_1 = pack(placed_1, near_1, to_y)
        held_2 = pack(placed_2, near_2, to_z)

        def joined(core):
            return jnp.concatenate(
                [
                    jnp.stack([a[core] for a in held_1], axis=0),
                    jnp.stack([a[core] for a in held_2], axis=1),
                ],
                axis=-1,
            ).reshape(16 * CAP, width)

        passed = swap_core(joined(1))
        kept = joined(0)

    with jax.named_scope("mix"):

        def mix_of(keys, named, near):
            def weighted(first):
                return sum(
                    jnp.where(
                        named[:, k : k + 1] == keys,
                        near[:, half + first + k : half + first + k + 1].astype(jnp.float32),
                        0.0,
                    )
                    for k in range(top)
                ).astype(jnp.bfloat16)

            return jnp.concatenate([weighted(2 * top), weighted(3 * top)], axis=0)

        mix_1 = mix_of(keys_1, named_1, near_1)
        mix_2 = mix_of(keys_2, named_2, near_2)

    with jax.named_scope("experts"):
        inner_dim = expert_out.shape[1]

        def expert(rows):
            inner = jnp.dot(rows, expert_in[0], preferred_element_type=jnp.float32)
            active = (jnp.maximum(inner[:, :inner_dim], 0.0) * inner[:, inner_dim:]).astype(
                jnp.bfloat16
            )
            return jnp.dot(active, expert_out[0], preferred_element_type=jnp.float32).astype(
                jnp.bfloat16
            )

        shape = (4, 4, CAP, width)
        passed_back = swap_core(expert(passed)).reshape(shape)
        kept_back = expert(kept).reshape(shape)

    with jax.named_scope("combine"):

        def give_back(parts, send):
            out = []
            for d, s in enumerate((0, -1, 1, -2)):
                out.append(send(parts[d], s) if s else parts[d])
            return out

        parts_1 = [
            jnp.stack([kept_back[i, :, :, :half], passed_back[i, :, :, :half]]).reshape(block, half)
            for i in range(4)
        ]
        parts_2 = [
            jnp.stack([kept_back[:, j, :, half:], passed_back[:, j, :, half:]]).reshape(block, half)
            for j in range(4)
        ]

        def summed(mix, parts, send, back):
            rows = jnp.concatenate(give_back(parts, send), axis=0)
            both_sums = jnp.dot(mix, rows, preferred_element_type=jnp.float32)
            sums = both_sums[: 4 * rows_dev] + both_sums[4 * rows_dev :]
            mine = sums[:rows_dev]
            away = [
                sums[d * rows_dev : (d + 1) * rows_dev].astype(jnp.bfloat16) for d in range(4)
            ]
            return [mine] + give_back(away, back)[1:]

        total_1 = summed(mix_1, parts_1, to_y, to_z)
        total_2 = summed(mix_2, parts_2, to_z, to_y)
        mixed = jnp.concatenate(
            [sum(a.astype(jnp.float32) for a in t) for t in (total_1, total_2)], axis=1
        )
        hidden_out = (mid.astype(jnp.float32) + mixed).astype(jnp.bfloat16)
    return (hidden_out, new_cache)


def solution(mesh):
    axes = ("x", "zh", "y", "zl", "c")
    split = Mesh(mesh.devices.reshape(X, ZH, Y, ZL, C), axes)
    placed = (
        P(axes, None),
        P(axes, None),
        P(),
        P(None, None, ("x", "zh", "y"), None),
        P(),
        P(None, ("zl", "c")),
        P(),
        P(("zl", "c"), None),
        P(),
        P(),
        P(("y", "zl", "c"), None, None),
        P(("y", "zl", "c"), None, None),
    )
    return jax.shard_map(
        body,
        mesh=split,
        in_specs=placed,
        out_specs=(P(axes, None), P(("x", "zh", "y"), ("zl", "c"))),
        check_vma=False,
    )
```

```python
import jax
import jax.numpy as jnp
from jax import lax
from jax.experimental import pallas as pl
from jax.experimental.pallas import tpu as pltpu
from jax.sharding import Mesh
from jax.sharding import PartitionSpec as P

CAP = 24
epsilon = 1e-06
masked_score = -1e30
log2e = 1.4426950408889634

X, ZH, Y, ZL, C = 4, 2, 4, 4, 2


def rms_scale(rows, gain):
    values = rows.astype(jnp.float32)
    inverse = lax.rsqrt(jnp.mean(values * values, axis=-1, keepdims=True) + epsilon)
    return (values * inverse * gain).astype(jnp.bfloat16)


def swap_core(a):
    return lax.ppermute(a, "c", [(0, 1), (1, 0)])


def shift_line(a, s):
    return lax.ppermute(a, "zl", [(i, (i + s) % ZL) for i in range(ZL)])


def shift_y(a, s):
    pairs = []
    for y in range(Y):
        for c in range(C):
            t = (y + (s if c == 0 else -s)) % Y
            pairs.append((y * C + c, t * C + c))
    return lax.ppermute(a, ("y", "c"), pairs)


def shift_z(a, s):
    pairs = []
    n = ZH * ZL
    for z in range(n):
        for c in range(C):
            t = (z + (s if c == 0 else -s)) % n
            pairs.append((z * C + c, t * C + c))
    return lax.ppermute(a, ("zh", "zl", "c"), pairs)


def spread_out(a, send):
    return [a, send(a, 1), send(a, -1), send(a, 2)]


def attention_kernel(meta, q_ref, *refs, sources, first, last, pages, heads):
    refs = list(refs)
    shards = [refs.pop(0) for _ in sources]
    before = None if first else (refs.pop(0), refs.pop(0))
    outs = [refs.pop(0)] if last else [refs.pop(0), refs.pop(0)]
    keys_ref, values_ref, m_ref, sum_ref = refs
    span = keys_ref.shape[0]
    rows = q_ref.shape[0] // heads
    scale = log2e / float(128) ** 0.5
    y, zl, c, length = meta[0], meta[1], meta[2], meta[3]
    if first:
        m_ref[...] = jnp.full(m_ref.shape, masked_score, jnp.float32)
        sum_ref[...] = jnp.zeros(sum_ref.shape, jnp.float32)
    else:
        m_ref[...] = before[0][...]
        sum_ref[...] = before[1][...]
    values_ref[:, 128:] = jnp.ones((span, 128), jnp.bfloat16)

    def half_of(index):
        return ((index % 256) // 128) * (1 - 2 * c) + c

    key = lax.broadcasted_iota(jnp.int32, (1, span), 1)
    fresh = key - pages

    def fold(index, _):
        away = 0
        for i, ref in enumerate(shards):
            away = jnp.where(index == i, sources[i], away)

            @pl.when(index == i)
            def _(ref=ref):
                keys_ref[...] = ref[:, :128]
                values_ref[:, :128] = ref[:, 128:]

        source = lax.rem(y + away * (1 - 2 * c) + 4, 4)
        position = (key // 64 * 4 + source) * 64 + key % 64
        if first:
            place = ((zl - fresh // 256 + 4) % 4) * 256 + half_of(fresh) * 128 + fresh % 128
            bound = jnp.where(key < pages, jnp.where(position < length, -1, 2**20), place)
            row = lax.broadcasted_iota(jnp.int32, (rows, 1), 0)
            row_place = zl * 256 + half_of(row) * 128 + row % 128
            visible = bound <= row_place
        else:
            visible = jnp.where(key < pages, position, source) < jnp.where(key < pages, length, y)
        for h in range(heads):
            part = pl.ds(h * rows, rows)
            scores = lax.dot_general(
                q_ref[part, :],
                keys_ref[...],
                (((1,), (1,)), ((), ())),
                preferred_element_type=jnp.float32,
            )
            scores = jnp.where(visible, scores, masked_score)
            old = m_ref[part, :]
            new = jnp.maximum(old, jnp.max(scores, axis=1, keepdims=True))
            m_ref[part, :] = new
            weights = jnp.exp2(scores * scale - new[:, :1] * scale)
            factor = jnp.exp2((old - new) * scale)
            sum_ref[part, :] = sum_ref[part, :] * jnp.concatenate([factor, factor], axis=1) + jnp.dot(
                weights.astype(jnp.bfloat16), values_ref[...], preferred_element_type=jnp.float32
            )
        return 0

    lax.fori_loop(0, len(shards), fold, 0)
    if last:
        done = (sum_ref[:, :128] / sum_ref[:, 128:]).astype(jnp.bfloat16)
        for h in range(heads):
            outs[0][:, h * 128 : (h + 1) * 128] = done[h * rows : (h + 1) * rows, :]
    else:
        outs[0][...] = m_ref[...]
        outs[1][...] = sum_ref[...]


def attention(meta, queries, shards, sources, state, last, pages):
    heads = 4
    n, span = queries.shape[0], shards[0].shape[0]
    vmem = pl.BlockSpec(memory_space=pltpu.VMEM)
    kinds = (
        [jax.ShapeDtypeStruct((n // heads, heads * 128), jnp.bfloat16)]
        if last
        else [
            jax.ShapeDtypeStruct((n, 128), jnp.float32),
            jax.ShapeDtypeStruct((n, 256), jnp.float32),
        ]
    )
    return pl.pallas_call(
        lambda *refs: attention_kernel(
            *refs, sources=sources, first=not state, last=last, pages=pages, heads=heads
        ),
        out_shape=kinds,
        in_specs=[pl.BlockSpec(memory_space=pltpu.SMEM)]
        + [vmem] * (1 + len(shards) + len(state)),
        out_specs=[vmem] * len(kinds),
        scratch_shapes=[
            pltpu.VMEM((span, 128), jnp.bfloat16),
            pltpu.VMEM((span, 256), jnp.bfloat16),
            pltpu.VMEM((n, 128), jnp.float32),
            pltpu.VMEM((n, 256), jnp.float32),
        ],
        compiler_params=pltpu.CompilerParams(vmem_limit_bytes=40 * 2**20),
        cost_estimate=pl.CostEstimate(
            flops=6 * n * span * 128 * len(shards),
            bytes_accessed=4 * 2**20,
            transcendentals=n * span * len(shards),
        ),
        name="attention",
    )(meta, queries, *shards, *state)


def gate_kernel(
    hidden_ref, partial_ref, received_ref, gain_ref, router_ref, routes_ref, base_ref, mid_ref, a_ref, b_ref
):
    half = hidden_ref.shape[1] // 2
    rows, top = routes_ref.shape
    total = hidden_ref[...].astype(jnp.float32) + (partial_ref[...] + received_ref[...])
    mid = total.astype(jnp.bfloat16)
    mid_ref[...] = mid
    values = mid.astype(jnp.float32)
    inverse = lax.rsqrt(jnp.mean(values * values, axis=-1, keepdims=True) + epsilon)
    normed = (values * inverse * gain_ref[...]).astype(jnp.bfloat16)
    logits = jnp.dot(normed, router_ref[...], preferred_element_type=jnp.float32)
    expert = lax.broadcasted_iota(jnp.int32, logits.shape, 1)
    raised = [
        jnp.exp(
            jnp.sum(
                jnp.where(routes_ref[:, k : k + 1] == expert, logits, 0.0), axis=1, keepdims=True
            )
        )
        for k in range(top)
    ]
    whole = sum(raised[1:], raised[0])
    lane = lax.broadcasted_iota(jnp.int32, (rows, 128), 1)
    table = base_ref[...]
    for k in range(top):
        gate = raised[k] / whole
        high = gate.astype(jnp.bfloat16).astype(jnp.float32)
        table = jnp.where(lane == 2 * top + k, high, table)
        table = jnp.where(lane == 3 * top + k, gate - high, table)
    table = table.astype(jnp.bfloat16)
    a_ref[:, :half] = normed[:, :half]
    a_ref[:, half:] = table
    b_ref[:, :half] = normed[:, half:]
    b_ref[:, half:] = table


def order_kernel(meta, x_ref, o_ref):
    zl, c = meta[1], meta[2]
    col = pl.multiple_of(lax.rem(zl, 2) * 128, 128)
    for z in range(ZL):
        slot = lax.rem(zl - z + 4, 4)
        for half in range(2):
            inner = half * (1 - 2 * c) + c
            start = pl.multiple_of(slot * 256 + inner * 128, 128)
            o_ref[z * 256 + half * 128 : z * 256 + half * 128 + 128, :] = x_ref[
                pl.ds(start, 128), pl.ds(col, 128)
            ]


def body(
    hidden_in,
    routes,
    prefix_len,
    cache,
    attn_gain,
    w_query,
    w_keyval,
    w_out,
    moe_gain,
    w_router,
    expert_in,
    expert_out,
):
    y, zl, c = lax.axis_index("y"), lax.axis_index("zl"), lax.axis_index("c")
    rep = lax.axis_index(("x", "zh"))
    rows_dev, width = hidden_in.shape
    length = lax.dynamic_index_in_dim(prefix_len, rep, 0, keepdims=False)
    meta = jnp.stack([y, zl, c, length]).astype(jnp.int32)
    smem = pl.BlockSpec(memory_space=pltpu.SMEM)
    vmem = pl.BlockSpec(memory_space=pltpu.VMEM)

    group_size = 4
    to_group = []
    for z in range(ZH * ZL):
        for k in range(C):
            t = (z + k * (2 * (z % 2) - 1)) % (ZH * ZL)
            to_group.append((z * C + k, t * C + (z % ZL) // 2))

    def line_of(a):
        return [a] + [shift_line(a, s) for s in (1, 2, 3)]

    with jax.named_scope("weights"):
        wq_here = lax.ppermute(w_query, ("zh", "zl", "c"), to_group)
        wo_here = lax.ppermute(w_out, ("zh", "zl", "c"), to_group)

    with jax.named_scope("keys"):
        normed = rms_scale(hidden_in, attn_gain)
        both = jnp.concatenate([normed, swap_core(normed)], axis=0)
        w_kv = lax.dynamic_index_in_dim(w_keyval, c, 0, keepdims=False)
        kv = jnp.dot(both, w_kv, preferred_element_type=jnp.float32).astype(jnp.bfloat16)
        line = line_of(kv)
        own_pages = lax.dynamic_index_in_dim(cache, c, 1, keepdims=True)
        line[1], own_pages = lax.optimization_barrier((line[1], own_pages))
        fetched = lax.all_to_all(own_pages, ("x", "zh"), split_axis=0, concat_axis=2, tiled=True)
        pages = fetched.reshape(-1, 256)
        shard = jnp.concatenate([pages] + line, axis=0)
        up = shift_y(shard, 1)
        down = shift_y(shard, -1)
        far = shift_y(up, 1)

    with jax.named_scope("new_cache"):
        ordered = pl.pallas_call(
            order_kernel,
            out_shape=jax.ShapeDtypeStruct((1024, 128), jnp.bfloat16),
            in_specs=[smem, vmem],
            out_specs=vmem,
        )(meta, jnp.concatenate(line, axis=0))
        other, wq_here, wo_here = lax.optimization_barrier((swap_core(ordered), wq_here, wo_here))
        held = jnp.where(c == zl // 2, ordered, other)
        new_cache = jnp.where(c == 0, held[:, :64], held[:, 64:])

    with jax.named_scope("weights"):
        wq = spread_out(wq_here, shift_z)
        wq, wo_here = lax.optimization_barrier((wq, wo_here))
        wo = jnp.concatenate(spread_out(wo_here, shift_z), axis=0)

    with jax.named_scope("routing"):
        experts_all = w_router.shape[1]
        top = routes.shape[1]
        matches = routes[:, :, None] == jnp.arange(experts_all, dtype=jnp.int32)[None, None, :]
        named = jnp.sum(matches.astype(jnp.float32), axis=1)
        lower = (jnp.arange(rows_dev)[:, None] > jnp.arange(rows_dev)[None, :]).astype(jnp.float32)
        before = jnp.dot(lower, named, preferred_element_type=jnp.float32)
        slot = jnp.sum(jnp.where(matches, before[:, None, :], 0.0), axis=2)
        lane = jnp.arange(128, dtype=jnp.int32)[None, :]
        base = sum(
            jnp.where(lane == k, routes[:, k : k + 1].astype(jnp.float32), 0.0)
            + jnp.where(lane == top + k, slot[:, k : k + 1], 0.0)
            for k in range(top)
        )

    with jax.named_scope("queries"):
        queries = jnp.concatenate(
            [jnp.dot(both, wq[h], preferred_element_type=jnp.float32) for h in range(group_size)],
            axis=0,
        ).astype(jnp.bfloat16)

    with jax.named_scope("attention"):
        n_pages = pages.shape[0]
        queries, new_cache, base = lax.optimization_barrier((queries, new_cache, base))
        state = attention(meta, queries, [shard], [0], (), False, n_pages)
        state = attention(meta, queries, [up, down], [-1, 1], state, False, n_pages)
        (attended,) = attention(meta, queries, [far], [2], state, True, n_pages)

    with jax.named_scope("out_projection"):
        half = width // 2
        received = swap_core(
            jnp.dot(attended[rows_dev:], wo, preferred_element_type=jnp.float32)
        )
        partial = jnp.dot(attended[:rows_dev], wo, preferred_element_type=jnp.float32)
        wide = jax.ShapeDtypeStruct((rows_dev, half + 128), jnp.bfloat16)
        mid, send_1, send_2 = pl.pallas_call(
            gate_kernel,
            out_shape=[jax.ShapeDtypeStruct((rows_dev, width), jnp.bfloat16), wide, wide],
            in_specs=[vmem] * 7,
            out_specs=[vmem] * 3,
            compiler_params=pltpu.CompilerParams(vmem_limit_bytes=16 * 2**20),
            name="gate",
        )(hidden_in, partial, received, moe_gain[None], w_router, routes, base)

    with jax.named_scope("routing"):
        step = 1 - 2 * c
        z = lax.axis_index(("zh", "zl"))
        y_goals = jnp.stack([y, y + step, y - step, y + 2]) % Y
        z_goals = jnp.stack([z, z + step, z - step, z + 2 * step]) % ZL
        cores = jnp.stack([c, 1 - c])
        half = width // 2
        spread = experts_all * CAP

        def keys_of(first):
            inner = jnp.arange(4, dtype=jnp.int32)[:, None] * spread + jnp.arange(CAP, dtype=jnp.int32)
            return (first[:, :, None, None] * CAP + inner[None, None]).reshape(1, -1)

        keys_1 = keys_of(y_goals[:, None] * 8 + (z % ZL) * 2 + cores[None, :])
        keys_2 = keys_of(y * 8 + z_goals[:, None] * 2 + cores[None, :])

    def to_y(a, s):
        return shift_y(a, s)

    def to_z(a, s):
        return shift_z(a, s)

    block = 2 * 4 * CAP

    with jax.named_scope("dispatch"):
        near_1 = jnp.concatenate(spread_out(send_1, to_z), axis=0)
        near_2 = jnp.concatenate(spread_out(send_2, to_y), axis=0)

        def named_of(near):
            ids = near[:, half : half + top].astype(jnp.int32)
            slots = near[:, half + top : half + 2 * top].astype(jnp.int32)
            source = lax.broadcasted_iota(jnp.int32, ids.shape, 0) // rows_dev
            return ids * CAP + slots + source * spread

        def placed_of(keys, named):
            return sum((named[:, k : k + 1] == keys) for k in range(top)).astype(jnp.bfloat16)

        named_1, named_2 = named_of(near_1), named_of(near_2)
        placed_1, placed_2 = placed_of(keys_1, named_1), placed_of(keys_2, named_2)

        def pack(placed, near, send):
            out = []
            for d, s in enumerate((0, 1, -1, 2)):
                packed = lax.dot_general(
                    placed[:, d * block : (d + 1) * block],
                    near[:, :half],
                    (((0,), (0,)), ((), ())),
                    preferred_element_type=jnp.float32,
                ).astype(jnp.bfloat16)
                out.append((send(packed, s) if s else packed).reshape(2, 4, CAP, half))
            return out

        held_1 = pack(placed_1, near_1, to_y)
        held_2 = pack(placed_2, near_2, to_z)

        def joined(core):
            return jnp.concatenate(
                [
                    jnp.stack([a[core] for a in held_1], axis=0),
                    jnp.stack([a[core] for a in held_2], axis=1),
                ],
                axis=-1,
            ).reshape(16 * CAP, width)

        passed = swap_core(joined(1))
        kept = joined(0)

    with jax.named_scope("mix"):

        def mix_of(keys, named, near):
            def weighted(first):
                return sum(
                    jnp.where(
                        named[:, k : k + 1] == keys,
                        near[:, half + first + k : half + first + k + 1].astype(jnp.float32),
                        0.0,
                    )
                    for k in range(top)
                ).astype(jnp.bfloat16)

            return jnp.concatenate([weighted(2 * top), weighted(3 * top)], axis=0)

        mix_1 = mix_of(keys_1, named_1, near_1)
        mix_2 = mix_of(keys_2, named_2, near_2)

    with jax.named_scope("experts"):
        inner_dim = expert_out.shape[1]

        def expert(rows):
            inner = jnp.dot(rows, expert_in[0], preferred_element_type=jnp.float32)
            active = (jnp.maximum(inner[:, :inner_dim], 0.0) * inner[:, inner_dim:]).astype(
                jnp.bfloat16
            )
            return jnp.dot(active, expert_out[0], preferred_element_type=jnp.float32).astype(
                jnp.bfloat16
            )

        shape = (4, 4, CAP, width)
        passed_back = swap_core(expert(passed)).reshape(shape)
        kept_back = expert(kept).reshape(shape)

    with jax.named_scope("combine"):

        def give_back(parts, send):
            out = []
            for d, s in enumerate((0, -1, 1, -2)):
                out.append(send(parts[d], s) if s else parts[d])
            return out

        parts_1 = [
            jnp.stack([kept_back[i, :, :, :half], passed_back[i, :, :, :half]]).reshape(block, half)
            for i in range(4)
        ]
        parts_2 = [
            jnp.stack([kept_back[:, j, :, half:], passed_back[:, j, :, half:]]).reshape(block, half)
            for j in range(4)
        ]

        def summed(mix, parts, send, back):
            rows = jnp.concatenate(give_back(parts, send), axis=0)
            both_sums = jnp.dot(mix, rows, preferred_element_type=jnp.float32)
            sums = both_sums[: 4 * rows_dev] + both_sums[4 * rows_dev :]
            mine = sums[:rows_dev]
            away = [
                sums[d * rows_dev : (d + 1) * rows_dev].astype(jnp.bfloat16) for d in range(4)
            ]
            return [mine] + give_back(away, back)[1:]

        total_1 = summed(mix_1, parts_1, to_y, to_z)
        total_2 = summed(mix_2, parts_2, to_z, to_y)
        mixed = jnp.concatenate(
            [sum(a.astype(jnp.float32) for a in t) for t in (total_1, total_2)], axis=1
        )
        hidden_out = (mid.astype(jnp.float32) + mixed).astype(jnp.bfloat16)
    return (hidden_out, new_cache)


def solution(mesh):
    axes = ("x", "zh", "y", "zl", "c")
    split = Mesh(mesh.devices.reshape(X, ZH, Y, ZL, C), axes)
    placed = (
        P(axes, None),
        P(axes, None),
        P(),
        P(None, None, ("x", "zh", "y"), None),
        P(),
        P(None, ("zl", "c")),
        P(),
        P(("zl", "c"), None),
        P(),
        P(),
        P(("y", "zl", "c"), None, None),
        P(("y", "zl", "c"), None, None),
    )
    return jax.shard_map(
        body,
        mesh=split,
        in_specs=placed,
        out_specs=(P(axes, None), P(("x", "zh", "y"), ("zl", "c"))),
        check_vma=False,
    )
```

```python
import jax
import jax.numpy as jnp
from jax import lax
from jax.experimental import pallas as pl
from jax.experimental.pallas import tpu as pltpu
from jax.sharding import Mesh
from jax.sharding import PartitionSpec as P

CAP = 24
epsilon = 1e-06
masked_score = -1e30
log2e = 1.4426950408889634

X, ZH, Y, ZL, C = 4, 2, 4, 4, 2


def rms_scale(rows, gain):
    values = rows.astype(jnp.float32)
    inverse = lax.rsqrt(jnp.mean(values * values, axis=-1, keepdims=True) + epsilon)
    return (values * inverse * gain).astype(jnp.bfloat16)


def swap_core(a):
    return lax.ppermute(a, "c", [(0, 1), (1, 0)])


def shift_line(a, s):
    return lax.ppermute(a, "zl", [(i, (i + s) % ZL) for i in range(ZL)])


def shift_y(a, s):
    pairs = []
    for y in range(Y):
        for c in range(C):
            t = (y + (s if c == 0 else -s)) % Y
            pairs.append((y * C + c, t * C + c))
    return lax.ppermute(a, ("y", "c"), pairs)


def shift_z(a, s):
    pairs = []
    n = ZH * ZL
    for z in range(n):
        for c in range(C):
            t = (z + (s if c == 0 else -s)) % n
            pairs.append((z * C + c, t * C + c))
    return lax.ppermute(a, ("zh", "zl", "c"), pairs)


def spread_out(a, send):
    return [a, send(a, 1), send(a, -1), send(a, 2)]


def attention_kernel(meta, q_ref, *refs, sources, first, last, pages, heads):
    refs = list(refs)
    shards = [refs.pop(0) for _ in sources]
    before = None if first else (refs.pop(0), refs.pop(0))
    projections = [refs.pop(0) for _ in range(heads)] if last else None
    outs = [refs.pop(0), refs.pop(0)]
    keys_ref, values_ref, m_ref, sum_ref = refs
    span = keys_ref.shape[0]
    rows = q_ref.shape[0] // heads
    scale = log2e / float(128) ** 0.5
    y, zl, c, length = meta[0], meta[1], meta[2], meta[3]
    if first:
        m_ref[...] = jnp.full(m_ref.shape, masked_score, jnp.float32)
        sum_ref[...] = jnp.zeros(sum_ref.shape, jnp.float32)
    else:
        m_ref[...] = before[0][...]
        sum_ref[...] = before[1][...]
    values_ref[:, 128:] = jnp.ones((span, 128), jnp.bfloat16)

    def half_of(index):
        return ((index % 256) // 128) * (1 - 2 * c) + c

    key = lax.broadcasted_iota(jnp.int32, (1, span), 1)
    fresh = key - pages

    def fold(index, _):
        away = 0
        for i, ref in enumerate(shards):
            away = jnp.where(index == i, sources[i], away)

            @pl.when(index == i)
            def _(ref=ref):
                keys_ref[...] = ref[:, :128]
                values_ref[:, :128] = ref[:, 128:]

        source = lax.rem(y + away * (1 - 2 * c) + 4, 4)
        position = (key // 64 * 4 + source) * 64 + key % 64
        if first:
            place = ((zl - fresh // 256 + 4) % 4) * 256 + half_of(fresh) * 128 + fresh % 128
            bound = jnp.where(key < pages, jnp.where(position < length, -1, 2**20), place)
            row = lax.broadcasted_iota(jnp.int32, (rows, 1), 0)
            row_place = zl * 256 + half_of(row) * 128 + row % 128
            visible = bound <= row_place
        else:
            visible = jnp.where(key < pages, position, source) < jnp.where(key < pages, length, y)
        for h in range(heads):
            part = pl.ds(h * rows, rows)
            scores = lax.dot_general(
                q_ref[part, :],
                keys_ref[...],
                (((1,), (1,)), ((), ())),
                preferred_element_type=jnp.float32,
            )
            scores = jnp.where(visible, scores, masked_score)
            old = m_ref[part, :]
            new = jnp.maximum(old, jnp.max(scores, axis=1, keepdims=True))
            m_ref[part, :] = new
            weights = jnp.exp2(scores * scale - new[:, :1] * scale)
            factor = jnp.exp2((old - new) * scale)
            sum_ref[part, :] = sum_ref[part, :] * jnp.concatenate([factor, factor], axis=1) + jnp.dot(
                weights.astype(jnp.bfloat16), values_ref[...], preferred_element_type=jnp.float32
            )
        return 0

    lax.fori_loop(0, len(shards), fold, 0)
    if last:
        done = (sum_ref[:, :128] / sum_ref[:, 128:]).astype(jnp.bfloat16)
        for out, first_row in ((outs[0], 0), (outs[1], rows // 2)):
            out[...] = sum(
                jnp.dot(
                    done[h * rows + first_row : h * rows + first_row + rows // 2],
                    projections[h][...],
                    preferred_element_type=jnp.float32,
                )
                for h in range(heads)
            )
    else:
        outs[0][...] = m_ref[...]
        outs[1][...] = sum_ref[...]


def attention(meta, queries, shards, sources, state, projections, pages):
    heads = 4
    n, span = queries.shape[0], shards[0].shape[0]
    vmem = pl.BlockSpec(memory_space=pltpu.VMEM)
    last = bool(projections)
    kinds = (
        [jax.ShapeDtypeStruct((n // heads // 2, projections[0].shape[1]), jnp.float32)] * 2
        if last
        else [
            jax.ShapeDtypeStruct((n, 128), jnp.float32),
            jax.ShapeDtypeStruct((n, 256), jnp.float32),
        ]
    )
    return pl.pallas_call(
        lambda *refs: attention_kernel(
            *refs, sources=sources, first=not state, last=last, pages=pages, heads=heads
        ),
        out_shape=kinds,
        in_specs=[pl.BlockSpec(memory_space=pltpu.SMEM)]
        + [vmem] * (1 + len(shards) + len(state) + len(projections)),
        out_specs=[vmem] * len(kinds),
        scratch_shapes=[
            pltpu.VMEM((span, 128), jnp.bfloat16),
            pltpu.VMEM((span, 256), jnp.bfloat16),
            pltpu.VMEM((n, 128), jnp.float32),
            pltpu.VMEM((n, 256), jnp.float32),
        ],
        compiler_params=pltpu.CompilerParams(vmem_limit_bytes=40 * 2**20),
        cost_estimate=pl.CostEstimate(
            flops=6 * n * span * 128 * len(shards),
            bytes_accessed=4 * 2**20,
            transcendentals=n * span * len(shards),
        ),
        name="attention",
    )(meta, queries, *shards, *state, *projections)


def gate_kernel(
    hidden_ref, partial_ref, received_ref, gain_ref, router_ref, routes_ref, base_ref, mid_ref, a_ref, b_ref
):
    half = hidden_ref.shape[1] // 2
    rows, top = routes_ref.shape
    total = hidden_ref[...].astype(jnp.float32) + (partial_ref[...] + received_ref[...])
    mid = total.astype(jnp.bfloat16)
    mid_ref[...] = mid
    values = mid.astype(jnp.float32)
    inverse = lax.rsqrt(jnp.mean(values * values, axis=-1, keepdims=True) + epsilon)
    normed = (values * inverse * gain_ref[...]).astype(jnp.bfloat16)
    logits = jnp.dot(normed, router_ref[...], preferred_element_type=jnp.float32)
    expert = lax.broadcasted_iota(jnp.int32, logits.shape, 1)
    raised = [
        jnp.exp(
            jnp.sum(
                jnp.where(routes_ref[:, k : k + 1] == expert, logits, 0.0), axis=1, keepdims=True
            )
        )
        for k in range(top)
    ]
    whole = sum(raised[1:], raised[0])
    lane = lax.broadcasted_iota(jnp.int32, (rows, 128), 1)
    table = base_ref[...]
    for k in range(top):
        gate = raised[k] / whole
        high = gate.astype(jnp.bfloat16).astype(jnp.float32)
        table = jnp.where(lane == 2 * top + k, high, table)
        table = jnp.where(lane == 3 * top + k, gate - high, table)
    table = table.astype(jnp.bfloat16)
    a_ref[:, :half] = normed[:, :half]
    a_ref[:, half:] = table
    b_ref[:, :half] = normed[:, half:]
    b_ref[:, half:] = table


def order_kernel(meta, x_ref, o_ref):
    zl, c = meta[1], meta[2]
    col = pl.multiple_of(lax.rem(zl, 2) * 128, 128)
    for z in range(ZL):
        slot = lax.rem(zl - z + 4, 4)
        for half in range(2):
            inner = half * (1 - 2 * c) + c
            start = pl.multiple_of(slot * 256 + inner * 128, 128)
            o_ref[z * 256 + half * 128 : z * 256 + half * 128 + 128, :] = x_ref[
                pl.ds(start, 128), pl.ds(col, 128)
            ]


def body(
    hidden_in,
    routes,
    prefix_len,
    cache,
    attn_gain,
    w_query,
    w_keyval,
    w_out,
    moe_gain,
    w_router,
    expert_in,
    expert_out,
):
    y, zl, c = lax.axis_index("y"), lax.axis_index("zl"), lax.axis_index("c")
    rep = lax.axis_index(("x", "zh"))
    rows_dev, width = hidden_in.shape
    length = lax.dynamic_index_in_dim(prefix_len, rep, 0, keepdims=False)
    meta = jnp.stack([y, zl, c, length]).astype(jnp.int32)
    smem = pl.BlockSpec(memory_space=pltpu.SMEM)
    vmem = pl.BlockSpec(memory_space=pltpu.VMEM)

    group_size = 4
    to_group = []
    for z in range(ZH * ZL):
        for k in range(C):
            t = (z + k * (2 * (z % 2) - 1)) % (ZH * ZL)
            to_group.append((z * C + k, t * C + (z % ZL) // 2))

    def line_of(a):
        return [a] + [shift_line(a, s) for s in (1, 2, 3)]

    with jax.named_scope("weights"):
        wq_here = lax.ppermute(w_query, ("zh", "zl", "c"), to_group)
        wo_here = lax.ppermute(w_out, ("zh", "zl", "c"), to_group)

    with jax.named_scope("keys"):
        normed = rms_scale(hidden_in, attn_gain)
        own_pages = lax.dynamic_index_in_dim(cache, c, 1, keepdims=True)
        normed, own_pages = lax.optimization_barrier((normed, own_pages))
        both = jnp.concatenate([normed, swap_core(normed)], axis=0)
        w_kv = lax.dynamic_index_in_dim(w_keyval, c, 0, keepdims=False)
        kv = jnp.dot(both, w_kv, preferred_element_type=jnp.float32).astype(jnp.bfloat16)
        line = line_of(kv)
        line, wq_here, wo_here, routes = lax.optimization_barrier((line, wq_here, wo_here, routes))
        fetched = lax.all_to_all(own_pages, ("x", "zh"), split_axis=0, concat_axis=2, tiled=True)
        pages = fetched.reshape(-1, 256)
        shard = jnp.concatenate([pages] + line, axis=0)
        up = shift_y(shard, 1)
        down = shift_y(shard, -1)

    with jax.named_scope("new_cache"):
        ordered = pl.pallas_call(
            order_kernel,
            out_shape=jax.ShapeDtypeStruct((1024, 128), jnp.bfloat16),
            in_specs=[smem, vmem],
            out_specs=vmem,
        )(meta, jnp.concatenate(line, axis=0))
        ordered, down = lax.optimization_barrier((ordered, down))
        other = swap_core(ordered)
        held = jnp.where(c == zl // 2, ordered, other)
        new_cache = jnp.where(c == 0, held[:, :64], held[:, 64:])

    with jax.named_scope("weights"):
        wq = spread_out(wq_here, shift_z)
        wq, wo_here = lax.optimization_barrier((wq, wo_here))
        wo = spread_out(wo_here, shift_z)
        wq, up = lax.optimization_barrier((wq, up))
        far = shift_y(up, 1)

    with jax.named_scope("routing"):
        experts_all = w_router.shape[1]
        top = routes.shape[1]
        matches = routes[:, :, None] == jnp.arange(experts_all, dtype=jnp.int32)[None, None, :]
        named = jnp.sum(matches.astype(jnp.float32), axis=1)
        lower = (jnp.arange(rows_dev)[:, None] > jnp.arange(rows_dev)[None, :]).astype(jnp.float32)
        before = jnp.dot(lower, named, preferred_element_type=jnp.float32)
        slot = jnp.sum(jnp.where(matches, before[:, None, :], 0.0), axis=2)
        lane = jnp.arange(128, dtype=jnp.int32)[None, :]
        base = sum(
            jnp.where(lane == k, routes[:, k : k + 1].astype(jnp.float32), 0.0)
            + jnp.where(lane == top + k, slot[:, k : k + 1], 0.0)
            for k in range(top)
        )

    with jax.named_scope("queries"):
        queries = jnp.concatenate(
            [jnp.dot(both, wq[h], preferred_element_type=jnp.float32) for h in range(group_size)],
            axis=0,
        ).astype(jnp.bfloat16)

    with jax.named_scope("attention"):
        n_pages = pages.shape[0]
        queries, base = lax.optimization_barrier((queries, base))
        state = attention(meta, queries, [shard], [0], (), (), n_pages)
        state = attention(meta, queries, [up, down], [-1, 1], state, (), n_pages)
        partial, leaving = attention(meta, queries, [far], [2], state, wo, n_pages)

    with jax.named_scope("out_projection"):
        half = width // 2
        received = swap_core(leaving)
        wide = jax.ShapeDtypeStruct((rows_dev, half + 128), jnp.bfloat16)
        mid, send_1, send_2 = pl.pallas_call(
            gate_kernel,
            out_shape=[jax.ShapeDtypeStruct((rows_dev, width), jnp.bfloat16), wide, wide],
            in_specs=[vmem] * 7,
            out_specs=[vmem] * 3,
            compiler_params=pltpu.CompilerParams(vmem_limit_bytes=16 * 2**20),
            name="gate",
        )(hidden_in, partial, received, moe_gain[None], w_router, routes, base)

    with jax.named_scope("routing"):
        step = 1 - 2 * c
        z = lax.axis_index(("zh", "zl"))
        y_goals = jnp.stack([y, y + step, y - step, y + 2]) % Y
        z_goals = jnp.stack([z, z + step, z - step, z + 2 * step]) % ZL
        cores = jnp.stack([c, 1 - c])
        half = width // 2
        spread = experts_all * CAP

        def keys_of(first):
            inner = jnp.arange(4, dtype=jnp.int32)[:, None] * spread + jnp.arange(CAP, dtype=jnp.int32)
            return (first[:, :, None, None] * CAP + inner[None, None]).reshape(1, -1)

        keys_1 = keys_of(y_goals[:, None] * 8 + (z % ZL) * 2 + cores[None, :])
        keys_2 = keys_of(y * 8 + z_goals[:, None] * 2 + cores[None, :])

    def to_y(a, s):
        return shift_y(a, s)

    def to_z(a, s):
        return shift_z(a, s)

    block = 2 * 4 * CAP

    with jax.named_scope("dispatch"):
        near_1 = jnp.concatenate(spread_out(send_1, to_z), axis=0)
        near_2 = jnp.concatenate(spread_out(send_2, to_y), axis=0)

        def named_of(near):
            ids = near[:, half : half + top].astype(jnp.int32)
            slots = near[:, half + top : half + 2 * top].astype(jnp.int32)
            source = lax.broadcasted_iota(jnp.int32, ids.shape, 0) // rows_dev
            return ids * CAP + slots + source * spread

        def placed_of(keys, named):
            return sum((named[:, k : k + 1] == keys) for k in range(top)).astype(jnp.bfloat16)

        named_1, named_2 = named_of(near_1), named_of(near_2)
        placed_1, placed_2 = placed_of(keys_1, named_1), placed_of(keys_2, named_2)

        def pack(placed, near, send):
            out = []
            for d, s in enumerate((0, 1, -1, 2)):
                packed = lax.dot_general(
                    placed[:, d * block : (d + 1) * block],
                    near[:, :half],
                    (((0,), (0,)), ((), ())),
                    preferred_element_type=jnp.float32,
                ).astype(jnp.bfloat16)
                out.append((send(packed, s) if s else packed).reshape(2, 4, CAP, half))
            return out

        held_1 = pack(placed_1, near_1, to_y)
        held_2 = pack(placed_2, near_2, to_z)

        def joined(core):
            return jnp.concatenate(
                [
                    jnp.stack([a[core] for a in held_1], axis=0),
                    jnp.stack([a[core] for a in held_2], axis=1),
                ],
                axis=-1,
            ).reshape(16 * CAP, width)

        passed = swap_core(joined(1))
        kept = joined(0)

    with jax.named_scope("mix"):

        def mix_of(keys, named, near):
            def weighted(first):
                return sum(
                    jnp.where(
                        named[:, k : k + 1] == keys,
                        near[:, half + first + k : half + first + k + 1].astype(jnp.float32),
                        0.0,
                    )
                    for k in range(top)
                ).astype(jnp.bfloat16)

            return jnp.concatenate([weighted(2 * top), weighted(3 * top)], axis=0)

        mix_1 = mix_of(keys_1, named_1, near_1)
        mix_2 = mix_of(keys_2, named_2, near_2)

    with jax.named_scope("experts"):
        inner_dim = expert_out.shape[1]

        def expert(rows):
            inner = jnp.dot(rows, expert_in[0], preferred_element_type=jnp.float32)
            active = (jnp.maximum(inner[:, :inner_dim], 0.0) * inner[:, inner_dim:]).astype(
                jnp.bfloat16
            )
            return jnp.dot(active, expert_out[0], preferred_element_type=jnp.float32).astype(
                jnp.bfloat16
            )

        shape = (4, 4, CAP, width)
        passed_back = swap_core(expert(passed)).reshape(shape)
        kept_back = expert(kept).reshape(shape)

    with jax.named_scope("combine"):

        def give_back(parts, send):
            out = []
            for d, s in enumerate((0, -1, 1, -2)):
                out.append(send(parts[d], s) if s else parts[d])
            return out

        parts_1 = [
            jnp.stack([kept_back[i, :, :, :half], passed_back[i, :, :, :half]]).reshape(block, half)
            for i in range(4)
        ]
        parts_2 = [
            jnp.stack([kept_back[:, j, :, half:], passed_back[:, j, :, half:]]).reshape(block, half)
            for j in range(4)
        ]

        def summed(mix, parts, send, back):
            rows = jnp.concatenate(give_back(parts, send), axis=0)
            both_sums = jnp.dot(mix, rows, preferred_element_type=jnp.float32)
            sums = both_sums[: 4 * rows_dev] + both_sums[4 * rows_dev :]
            mine = sums[:rows_dev]
            away = [
                sums[d * rows_dev : (d + 1) * rows_dev].astype(jnp.bfloat16) for d in range(4)
            ]
            return [mine] + give_back(away, back)[1:]

        total_1 = summed(mix_1, parts_1, to_y, to_z)
        total_2 = summed(mix_2, parts_2, to_z, to_y)
        mixed = jnp.concatenate(
            [sum(a.astype(jnp.float32) for a in t) for t in (total_1, total_2)], axis=1
        )
        hidden_out = (mid.astype(jnp.float32) + mixed).astype(jnp.bfloat16)
    return (hidden_out, new_cache)


def solution(mesh):
    axes = ("x", "zh", "y", "zl", "c")
    split = Mesh(mesh.devices.reshape(X, ZH, Y, ZL, C), axes)
    placed = (
        P(axes, None),
        P(axes, None),
        P(),
        P(None, None, ("x", "zh", "y"), None),
        P(),
        P(None, ("zl", "c")),
        P(),
        P(("zl", "c"), None),
        P(),
        P(),
        P(("y", "zl", "c"), None, None),
        P(("y", "zl", "c"), None, None),
    )
    return jax.shard_map(
        body,
        mesh=split,
        in_specs=placed,
        out_specs=(P(axes, None), P(("x", "zh", "y"), ("zl", "c"))),
        check_vma=False,
    )
```

```python
import jax
import jax.numpy as jnp
from jax import lax
from jax.experimental import pallas as pl
from jax.experimental.pallas import tpu as pltpu
from jax.sharding import Mesh
from jax.sharding import PartitionSpec as P

CAP = 24
epsilon = 1e-06
masked_score = -1e30
log2e = 1.4426950408889634

X, ZH, Y, ZL, C = 4, 2, 4, 4, 2


def rms_scale(rows, gain):
    values = rows.astype(jnp.float32)
    inverse = lax.rsqrt(jnp.mean(values * values, axis=-1, keepdims=True) + epsilon)
    return (values * inverse * gain).astype(jnp.bfloat16)


def swap_core(a):
    return lax.ppermute(a, "c", [(0, 1), (1, 0)])


def shift_line(a, s):
    return lax.ppermute(a, "zl", [(i, (i + s) % ZL) for i in range(ZL)])


def shift_y(a, s):
    pairs = []
    for y in range(Y):
        for c in range(C):
            t = (y + (s if c == 0 else -s)) % Y
            pairs.append((y * C + c, t * C + c))
    return lax.ppermute(a, ("y", "c"), pairs)


def shift_z(a, s):
    pairs = []
    n = ZH * ZL
    for z in range(n):
        for c in range(C):
            t = (z + (s if c == 0 else -s)) % n
            pairs.append((z * C + c, t * C + c))
    return lax.ppermute(a, ("zh", "zl", "c"), pairs)


def spread_out(a, send):
    return [a, send(a, 1), send(a, -1), send(a, 2)]


def attention_kernel(meta, q_ref, *refs, sources, first, last, pages, heads):
    refs = list(refs)
    shards = [refs.pop(0) for _ in sources]
    before = None if first else (refs.pop(0), refs.pop(0))
    projections = [refs.pop(0) for _ in range(heads)] if last else None
    outs = [refs.pop(0), refs.pop(0)]
    keys_ref, values_ref, m_ref, sum_ref = refs
    span = keys_ref.shape[0]
    rows = q_ref.shape[0] // heads
    scale = log2e / float(128) ** 0.5
    y, zl, c, length = meta[0], meta[1], meta[2], meta[3]
    if first:
        m_ref[...] = jnp.full(m_ref.shape, masked_score, jnp.float32)
        sum_ref[...] = jnp.zeros(sum_ref.shape, jnp.float32)
    else:
        m_ref[...] = before[0][...]
        sum_ref[...] = before[1][...]
    values_ref[:, 128:] = jnp.ones((span, 128), jnp.bfloat16)

    def half_of(index):
        return ((index % 256) // 128) * (1 - 2 * c) + c

    key = lax.broadcasted_iota(jnp.int32, (1, span), 1)
    fresh = key - pages

    def fold(index, _):
        away = 0
        for i, ref in enumerate(shards):
            away = jnp.where(index == i, sources[i], away)

            @pl.when(index == i)
            def _(ref=ref):
                keys_ref[...] = ref[:, :128]
                values_ref[:, :128] = ref[:, 128:]

        source = lax.rem(y + away * (1 - 2 * c) + 4, 4)
        position = (key // 64 * 4 + source) * 64 + key % 64
        if first:
            place = ((zl - fresh // 256 + 4) % 4) * 256 + half_of(fresh) * 128 + fresh % 128
            bound = jnp.where(key < pages, jnp.where(position < length, -1, 2**20), place)
            row = lax.broadcasted_iota(jnp.int32, (rows, 1), 0)
            row_place = zl * 256 + half_of(row) * 128 + row % 128
            visible = bound <= row_place
        else:
            visible = jnp.where(key < pages, position, source) < jnp.where(key < pages, length, y)
        for h in range(heads):
            part = pl.ds(h * rows, rows)
            scores = lax.dot_general(
                q_ref[part, :],
                keys_ref[...],
                (((1,), (1,)), ((), ())),
                preferred_element_type=jnp.float32,
            )
            scores = jnp.where(visible, scores, masked_score)
            old = m_ref[part, :]
            new = jnp.maximum(old, jnp.max(scores, axis=1, keepdims=True))
            m_ref[part, :] = new
            weights = jnp.exp2(scores * scale - new[:, :1] * scale)
            factor = jnp.exp2((old - new) * scale)
            sum_ref[part, :] = sum_ref[part, :] * jnp.concatenate([factor, factor], axis=1) + jnp.dot(
                weights.astype(jnp.bfloat16), values_ref[...], preferred_element_type=jnp.float32
            )
        return 0

    lax.fori_loop(0, len(shards), fold, 0)
    if last:
        done = (sum_ref[:, :128] / sum_ref[:, 128:]).astype(jnp.bfloat16)
        for out, first_row in ((outs[0], 0), (outs[1], rows // 2)):
            out[...] = sum(
                jnp.dot(
                    done[h * rows + first_row : h * rows + first_row + rows // 2],
                    projections[h][...],
                    preferred_element_type=jnp.float32,
                )
                for h in range(heads)
            )
    else:
        outs[0][...] = m_ref[...]
        outs[1][...] = sum_ref[...]


def attention(meta, queries, shards, sources, state, projections, pages):
    heads = 4
    n, span = queries.shape[0], shards[0].shape[0]
    vmem = pl.BlockSpec(memory_space=pltpu.VMEM)
    last = bool(projections)
    kinds = (
        [jax.ShapeDtypeStruct((n // heads // 2, projections[0].shape[1]), jnp.float32)] * 2
        if last
        else [
            jax.ShapeDtypeStruct((n, 128), jnp.float32),
            jax.ShapeDtypeStruct((n, 256), jnp.float32),
        ]
    )
    return pl.pallas_call(
        lambda *refs: attention_kernel(
            *refs, sources=sources, first=not state, last=last, pages=pages, heads=heads
        ),
        out_shape=kinds,
        in_specs=[pl.BlockSpec(memory_space=pltpu.SMEM)]
        + [vmem] * (1 + len(shards) + len(state) + len(projections)),
        out_specs=[vmem] * len(kinds),
        scratch_shapes=[
            pltpu.VMEM((span, 128), jnp.bfloat16),
            pltpu.VMEM((span, 256), jnp.bfloat16),
            pltpu.VMEM((n, 128), jnp.float32),
            pltpu.VMEM((n, 256), jnp.float32),
        ],
        compiler_params=pltpu.CompilerParams(vmem_limit_bytes=40 * 2**20),
        cost_estimate=pl.CostEstimate(
            flops=6 * n * span * 128 * len(shards),
            bytes_accessed=4 * 2**20,
            transcendentals=n * span * len(shards),
        ),
        name="attention",
    )(meta, queries, *shards, *state, *projections)


def gate_kernel(
    hidden_ref, partial_ref, received_ref, gain_ref, router_ref, base_ref, mid_ref, a_ref, b_ref
):
    half = hidden_ref.shape[1] // 2
    rows, top = hidden_ref.shape[0], 4
    total = hidden_ref[...].astype(jnp.float32) + (partial_ref[...] + received_ref[...])
    mid = total.astype(jnp.bfloat16)
    mid_ref[...] = mid
    values = mid.astype(jnp.float32)
    inverse = lax.rsqrt(jnp.mean(values * values, axis=-1, keepdims=True) + epsilon)
    normed = (values * inverse * gain_ref[...]).astype(jnp.bfloat16)
    logits = jnp.dot(normed, router_ref[...], preferred_element_type=jnp.float32)
    expert = lax.broadcasted_iota(jnp.int32, logits.shape, 1).astype(jnp.float32)
    raised = [
        jnp.exp(
            jnp.sum(
                jnp.where(base_ref[:, k : k + 1] == expert, logits, 0.0), axis=1, keepdims=True
            )
        )
        for k in range(top)
    ]
    whole = sum(raised[1:], raised[0])
    lane = lax.broadcasted_iota(jnp.int32, (rows, 128), 1)
    table = base_ref[...]
    for k in range(top):
        gate = raised[k] / whole
        high = gate.astype(jnp.bfloat16).astype(jnp.float32)
        table = jnp.where(lane == 2 * top + k, high, table)
        table = jnp.where(lane == 3 * top + k, gate - high, table)
    table = table.astype(jnp.bfloat16)
    a_ref[:, :half] = normed[:, :half]
    a_ref[:, half:] = table
    b_ref[:, :half] = normed[:, half:]
    b_ref[:, half:] = table


def table_kernel(routes_ref, o_ref):
    rows, top = routes_ref.shape
    expert = lax.broadcasted_iota(jnp.int32, (rows, 32), 1)
    named = [(routes_ref[:, k : k + 1] == expert).astype(jnp.float32) for k in range(top)]
    later = lax.broadcasted_iota(jnp.int32, (rows, rows), 0)
    earlier = lax.broadcasted_iota(jnp.int32, (rows, rows), 1)
    before = jnp.dot(
        (later > earlier).astype(jnp.float32),
        sum(named[1:], named[0]),
        preferred_element_type=jnp.float32,
    )
    lane = lax.broadcasted_iota(jnp.int32, (rows, 128), 1)
    table = jnp.zeros((rows, 128), jnp.float32)
    for k in range(top):
        slot = jnp.sum(named[k] * before, axis=1, keepdims=True)
        table = jnp.where(lane == k, routes_ref[:, k : k + 1].astype(jnp.float32), table)
        table = jnp.where(lane == top + k, slot, table)
    o_ref[...] = table


def key_kernel(meta, own_ref, other_ref, w_ref, o_ref):
    half = own_ref.shape[0]
    for i, ref in enumerate((own_ref, other_ref)):
        o_ref[i * half : (i + 1) * half, :] = jnp.dot(
            ref[...], w_ref[0], preferred_element_type=jnp.float32
        ).astype(jnp.bfloat16)


def query_kernel(own_ref, other_ref, *refs):
    half = own_ref.shape[0]
    for h, w_ref in enumerate(refs[:-1]):
        for i, ref in enumerate((own_ref, other_ref)):
            start = (2 * h + i) * half
            refs[-1][start : start + half, :] = jnp.dot(
                ref[...], w_ref[...], preferred_element_type=jnp.float32
            ).astype(jnp.bfloat16)


def shard_kernel(meta, pages_ref, *refs):
    line, shard_ref, ordered_ref = refs[:ZL], refs[ZL], refs[ZL + 1]
    zl, c = meta[1], meta[2]
    pages = pages_ref.shape[0]
    shard_ref[:pages, :] = pages_ref[...]
    for i, ref in enumerate(line):
        shard_ref[pages + i * 256 : pages + (i + 1) * 256, :] = ref[...]
    col = pl.multiple_of(lax.rem(zl, 2) * 128, 128)
    for z in range(ZL):
        slot = lax.rem(zl - z + 4, 4)
        for half in range(2):
            inner = half * (1 - 2 * c) + c
            start = pl.multiple_of(pages + slot * 256 + inner * 128, 128)
            ordered_ref[z * 256 + half * 128 : z * 256 + half * 128 + 128, :] = shard_ref[
                pl.ds(start, 128), pl.ds(col, 128)
            ]


def goal_keys(meta, d, along_y, shape, spread):
    y, zl, c = meta[0], meta[1], meta[2]
    step = 1 - 2 * c
    away = (0, step, -step, 2)[d]
    goal = lax.rem((y if along_y else zl) + away + 4, 4)
    first = goal * 8 + zl * 2 if along_y else y * 8 + goal * 2
    row = lax.broadcasted_iota(jnp.int32, shape, 0)
    core = jnp.where(row < 4 * CAP, c, 1 - c)
    source = row % (4 * CAP) // CAP
    return ((first + core) * CAP + row % CAP + source * spread).astype(jnp.float32)


def columns_of(near_ref, half, source, spread):
    flat = jnp.transpose(near_ref[:, half:].astype(jnp.float32))
    top = 4
    names = [
        flat[k : k + 1] * CAP + flat[top + k : top + k + 1] + source * spread for k in range(top)
    ]
    return names, [flat[i : i + 1] for i in range(2 * top, 4 * top)]


def pack_kernel(meta, *refs, along_y):
    near, outs, rows_ref = refs[:4], refs[4:8], refs[8]
    rows, half = near[0].shape[0], near[0].shape[1] - 128
    spread = 32 * CAP
    names = []
    for j, ref in enumerate(near):
        rows_ref[j * rows : (j + 1) * rows, :] = ref[:, :half]
        names.append(columns_of(ref, half, j, spread)[0])
    for d in range(4):
        keys = goal_keys(meta, d, along_y, (8 * CAP, rows), spread)
        placed = jnp.concatenate(
            [sum((keys == name).astype(jnp.float32) for name in names[j]) for j in range(4)], axis=1
        ).astype(jnp.bfloat16)
        outs[d][...] = jnp.dot(placed, rows_ref[...], preferred_element_type=jnp.float32).astype(
            jnp.bfloat16
        )


def mix_kernel(meta, *refs, along_y):
    near, out = refs[:4], refs[4]
    rows, half = near[0].shape[0], near[0].shape[1] - 128
    spread = 32 * CAP
    tables = [columns_of(ref, half, j, spread) for j, ref in enumerate(near)]
    for d in range(4):
        keys = goal_keys(meta, d, along_y, (8 * CAP, rows), spread)
        for j in range(4):
            names, gates = tables[j]
            hits = [keys == name for name in names]
            for part in range(2):
                weight = sum(
                    jnp.where(hits[k], gates[4 * part + k], 0.0) for k in range(len(names))
                )
                out[
                    d * 8 * CAP : (d + 1) * 8 * CAP,
                    (4 * part + j) * rows : (4 * part + j + 1) * rows,
                ] = weight.astype(jnp.bfloat16)


def body(
    hidden_in,
    routes,
    prefix_len,
    cache,
    attn_gain,
    w_query,
    w_keyval,
    w_out,
    moe_gain,
    w_router,
    expert_in,
    expert_out,
):
    y, zl, c = lax.axis_index("y"), lax.axis_index("zl"), lax.axis_index("c")
    rep = lax.axis_index(("x", "zh"))
    rows_dev, width = hidden_in.shape
    length = lax.dynamic_index_in_dim(prefix_len, rep, 0, keepdims=False)
    meta = jnp.stack([y, zl, c, length]).astype(jnp.int32)
    smem = pl.BlockSpec(memory_space=pltpu.SMEM)
    vmem = pl.BlockSpec(memory_space=pltpu.VMEM)

    group_size = 4
    to_group = []
    for z in range(ZH * ZL):
        for k in range(C):
            t = (z + k * (2 * (z % 2) - 1)) % (ZH * ZL)
            to_group.append((z * C + k, t * C + (z % ZL) // 2))

    def line_of(a):
        return [a] + [shift_line(a, s) for s in (1, 2, 3)]

    with jax.named_scope("weights"):
        wq_here = lax.ppermute(w_query, ("zh", "zl", "c"), to_group)
        wo_here = lax.ppermute(w_out, ("zh", "zl", "c"), to_group)

    with jax.named_scope("keys"):
        normed = rms_scale(hidden_in, attn_gain)
        own_pages = lax.dynamic_index_in_dim(cache, c, 1, keepdims=True)
        normed, own_pages = lax.optimization_barrier((normed, own_pages))
        beside = swap_core(normed)
        whole = pl.BlockSpec((rows_dev, width), lambda i, meta: (0, 0))
        kv = pl.pallas_call(
            key_kernel,
            out_shape=jax.ShapeDtypeStruct((2 * rows_dev, 256), jnp.bfloat16),
            grid_spec=pltpu.PrefetchScalarGridSpec(
                num_scalar_prefetch=1,
                grid=(1,),
                in_specs=[whole, whole, pl.BlockSpec((1, width, 256), lambda i, meta: (meta[2], 0, 0))],
                out_specs=pl.BlockSpec((2 * rows_dev, 256), lambda i, meta: (0, 0)),
            ),
            name="key",
        )(meta, normed, beside, w_keyval)
        line = line_of(kv)
        line, wq_here, wo_here, routes = lax.optimization_barrier((line, wq_here, wo_here, routes))
        fetched = lax.all_to_all(own_pages, ("x", "zh"), split_axis=0, concat_axis=2, tiled=True)
        pages = fetched.reshape(-1, 256)
        shard, ordered = pl.pallas_call(
            shard_kernel,
            out_shape=[
                jax.ShapeDtypeStruct((1536, 256), jnp.bfloat16),
                jax.ShapeDtypeStruct((1024, 128), jnp.bfloat16),
            ],
            in_specs=[smem] + [vmem] * 5,
            out_specs=[vmem] * 2,
            name="shard",
        )(meta, pages, *line)
        up = shift_y(shard, 1)
        down = shift_y(shard, -1)

    with jax.named_scope("new_cache"):
        ordered, down = lax.optimization_barrier((ordered, down))
        other = swap_core(ordered)
        held = jnp.where(c == zl // 2, ordered, other)
        new_cache = jnp.where(c == 0, held[:, :64], held[:, 64:])

    with jax.named_scope("weights"):
        wq = spread_out(wq_here, shift_z)
        wq, wo_here = lax.optimization_barrier((wq, wo_here))
        wo = spread_out(wo_here, shift_z)
        wq, up = lax.optimization_barrier((wq, up))
        far = shift_y(up, 1)

    with jax.named_scope("routing"):
        experts_all = w_router.shape[1]
        top = routes.shape[1]
        base = pl.pallas_call(
            table_kernel,
            out_shape=jax.ShapeDtypeStruct((rows_dev, 128), jnp.float32),
            in_specs=[vmem],
            out_specs=vmem,
            name="table",
        )(routes)

    with jax.named_scope("queries"):
        queries = pl.pallas_call(
            query_kernel,
            out_shape=jax.ShapeDtypeStruct((2 * rows_dev * group_size, 128), jnp.bfloat16),
            in_specs=[vmem] * (2 + group_size),
            out_specs=vmem,
            name="query",
        )(normed, beside, *wq)

    with jax.named_scope("attention"):
        n_pages = pages.shape[0]
        queries, base = lax.optimization_barrier((queries, base))
        state = attention(meta, queries, [shard], [0], (), (), n_pages)
        state = attention(meta, queries, [up, down], [-1, 1], state, (), n_pages)
        partial, leaving = attention(meta, queries, [far], [2], state, wo, n_pages)

    with jax.named_scope("out_projection"):
        half = width // 2
        received = swap_core(leaving)
        wide = jax.ShapeDtypeStruct((rows_dev, half + 128), jnp.bfloat16)
        mid, send_1, send_2 = pl.pallas_call(
            gate_kernel,
            out_shape=[jax.ShapeDtypeStruct((rows_dev, width), jnp.bfloat16), wide, wide],
            in_specs=[vmem] * 6,
            out_specs=[vmem] * 3,
            compiler_params=pltpu.CompilerParams(vmem_limit_bytes=16 * 2**20),
            name="gate",
        )(hidden_in, partial, received, moe_gain[None], w_router, base)

    def to_y(a, s):
        return shift_y(a, s)

    def to_z(a, s):
        return shift_z(a, s)

    block = 2 * 4 * CAP

    with jax.named_scope("dispatch"):
        near_1 = spread_out(send_1, to_z)
        near_2 = spread_out(send_2, to_y)
        packed_rows = jax.ShapeDtypeStruct((block, half), jnp.bfloat16)

        def pack(near, send, along_y):
            packed = pl.pallas_call(
                lambda *refs: pack_kernel(*refs, along_y=along_y),
                out_shape=[packed_rows] * 4,
                in_specs=[smem] + [vmem] * 4,
                out_specs=[vmem] * 4,
                scratch_shapes=[pltpu.VMEM((4 * rows_dev, half), jnp.bfloat16)],
                cost_estimate=pl.CostEstimate(
                    flops=2 * 4 * block * 4 * rows_dev * half, bytes_accessed=2**21, transcendentals=0
                ),
                name="pack",
            )(meta, *near)
            return [
                (send(a, s) if s else a).reshape(2, 4, CAP, half)
                for a, s in zip(packed, (0, 1, -1, 2))
            ]

        held_1 = pack(near_1, to_y, True)
        held_2 = pack(near_2, to_z, False)

        def joined(core):
            return jnp.concatenate(
                [
                    jnp.stack([a[core] for a in held_1], axis=0),
                    jnp.stack([a[core] for a in held_2], axis=1),
                ],
                axis=-1,
            ).reshape(16 * CAP, width)

        passed = swap_core(joined(1))
        kept = joined(0)

    with jax.named_scope("mix"):

        def mix_of(near, along_y):
            return pl.pallas_call(
                lambda *refs: mix_kernel(*refs, along_y=along_y),
                out_shape=jax.ShapeDtypeStruct((4 * block, 8 * rows_dev), jnp.bfloat16),
                in_specs=[smem] + [vmem] * 4,
                out_specs=vmem,
                cost_estimate=pl.CostEstimate(
                    flops=2**22, bytes_accessed=2**22, transcendentals=0
                ),
                name="mix",
            )(meta, *near)

        mix_1 = mix_of(near_1, True)
        mix_2 = mix_of(near_2, False)

    with jax.named_scope("experts"):
        inner_dim = expert_out.shape[1]

        def expert(rows):
            inner = jnp.dot(rows, expert_in[0], preferred_element_type=jnp.float32)
            active = (jnp.maximum(inner[:, :inner_dim], 0.0) * inner[:, inner_dim:]).astype(
                jnp.bfloat16
            )
            return jnp.dot(active, expert_out[0], preferred_element_type=jnp.float32).astype(
                jnp.bfloat16
            )

        shape = (4, 4, CAP, width)
        passed_back = swap_core(expert(passed)).reshape(shape)
        kept_back = expert(kept).reshape(shape)

    with jax.named_scope("combine"):

        def give_back(parts, send):
            out = []
            for d, s in enumerate((0, -1, 1, -2)):
                out.append(send(parts[d], s) if s else parts[d])
            return out

        parts_1 = [
            jnp.stack([kept_back[i, :, :, :half], passed_back[i, :, :, :half]]).reshape(block, half)
            for i in range(4)
        ]
        parts_2 = [
            jnp.stack([kept_back[:, j, :, half:], passed_back[:, j, :, half:]]).reshape(block, half)
            for j in range(4)
        ]

        def summed(mix, parts, send, back):
            rows = jnp.concatenate(give_back(parts, send), axis=0)
            both_sums = lax.dot_general(
                mix, rows, (((0,), (0,)), ((), ())), preferred_element_type=jnp.float32
            )
            sums = both_sums[: 4 * rows_dev] + both_sums[4 * rows_dev :]
            mine = sums[:rows_dev]
            away = [
                sums[d * rows_dev : (d + 1) * rows_dev].astype(jnp.bfloat16) for d in range(4)
            ]
            return [mine] + give_back(away, back)[1:]

        total_1 = summed(mix_1, parts_1, to_y, to_z)
        total_2 = summed(mix_2, parts_2, to_z, to_y)
        mixed = jnp.concatenate(
            [sum(a.astype(jnp.float32) for a in t) for t in (total_1, total_2)], axis=1
        )
        hidden_out = (mid.astype(jnp.float32) + mixed).astype(jnp.bfloat16)
    return (hidden_out, new_cache)


def solution(mesh):
    axes = ("x", "zh", "y", "zl", "c")
    split = Mesh(mesh.devices.reshape(X, ZH, Y, ZL, C), axes)
    placed = (
        P(axes, None),
        P(axes, None),
        P(),
        P(None, None, ("x", "zh", "y"), None),
        P(),
        P(None, ("zl", "c")),
        P(),
        P(("zl", "c"), None),
        P(),
        P(),
        P(("y", "zl", "c"), None, None),
        P(("y", "zl", "c"), None, None),
    )
    return jax.shard_map(
        body,
        mesh=split,
        in_specs=placed,
        out_specs=(P(axes, None), P(("x", "zh", "y"), ("zl", "c"))),
        check_vma=False,
    )
```

```python
import jax
import jax.numpy as jnp
from jax import lax
from jax.experimental import pallas as pl
from jax.experimental.pallas import tpu as pltpu
from jax.sharding import Mesh
from jax.sharding import PartitionSpec as P

CAP = 24
epsilon = 1e-06
masked_score = -1e30
log2e = 1.4426950408889634

X, ZH, Y, ZL, C = 4, 2, 4, 4, 2


def rms_scale(rows, gain):
    values = rows.astype(jnp.float32)
    inverse = lax.rsqrt(jnp.mean(values * values, axis=-1, keepdims=True) + epsilon)
    return (values * inverse * gain).astype(jnp.bfloat16)


def swap_core(a):
    return lax.ppermute(a, "c", [(0, 1), (1, 0)])


def shift_line(a, s):
    return lax.ppermute(a, "zl", [(i, (i + s) % ZL) for i in range(ZL)])


def shift_y(a, s):
    pairs = []
    for y in range(Y):
        for c in range(C):
            t = (y + (s if c == 0 else -s)) % Y
            pairs.append((y * C + c, t * C + c))
    return lax.ppermute(a, ("y", "c"), pairs)


def shift_z(a, s):
    pairs = []
    n = ZH * ZL
    for z in range(n):
        for c in range(C):
            t = (z + (s if c == 0 else -s)) % n
            pairs.append((z * C + c, t * C + c))
    return lax.ppermute(a, ("zh", "zl", "c"), pairs)


def spread_out(a, send):
    return [a, send(a, 1), send(a, -1), send(a, 2)]


def attention_kernel(meta, q_ref, *refs, sources, first, last, pages, heads):
    refs = list(refs)
    shards = [refs.pop(0) for _ in sources]
    before = None if first else (refs.pop(0), refs.pop(0))
    projections = [refs.pop(0) for _ in range(heads)] if last else None
    outs = [refs.pop(0), refs.pop(0)]
    keys_ref, values_ref, m_ref, sum_ref = refs[:4]
    span = keys_ref.shape[0]
    rows = q_ref.shape[0] // heads
    scale = log2e / float(128) ** 0.5
    y, zl, c, length = meta[0], meta[1], meta[2], meta[3]
    if first:
        m_ref[...] = jnp.full(m_ref.shape, masked_score, jnp.float32)
        sum_ref[...] = jnp.zeros(sum_ref.shape, jnp.float32)
    else:
        m_ref[...] = before[0][...]
        sum_ref[...] = before[1][...]
    values_ref[:, 128:] = jnp.ones((span, 128), jnp.bfloat16)

    def half_of(index):
        return ((index % 256) // 128) * (1 - 2 * c) + c

    key = lax.broadcasted_iota(jnp.int32, (1, span), 1)
    fresh = key - pages

    def fold(index, _):
        away = 0
        for i, ref in enumerate(shards):
            away = jnp.where(index == i, sources[i], away)

            @pl.when(index == i)
            def _(ref=ref):
                keys_ref[...] = ref[:, :128]
                values_ref[:, :128] = ref[:, 128:]

        source = lax.rem(y + away * (1 - 2 * c) + 4, 4)
        position = (key // 64 * 4 + source) * 64 + key % 64
        if first:
            place = ((zl - fresh // 256 + 4) % 4) * 256 + half_of(fresh) * 128 + fresh % 128
            bound = jnp.where(key < pages, jnp.where(position < length, -1, 2**20), place)
            row = lax.broadcasted_iota(jnp.int32, (rows, 1), 0)
            row_place = zl * 256 + half_of(row) * 128 + row % 128
            visible = bound <= row_place
        else:
            visible = jnp.where(key < pages, position, source) < jnp.where(key < pages, length, y)
        for h in range(heads):
            part = pl.ds(h * rows, rows)
            scores = lax.dot_general(
                q_ref[part, :],
                keys_ref[...],
                (((1,), (1,)), ((), ())),
                preferred_element_type=jnp.float32,
            )
            scores = jnp.where(visible, scores, masked_score)
            old = m_ref[part, :]
            new = jnp.maximum(old, jnp.max(scores, axis=1, keepdims=True))
            m_ref[part, :] = new
            weights = jnp.exp2(scores * scale - new[:, :1] * scale)
            factor = jnp.exp2((old - new) * scale)
            sum_ref[part, :] = sum_ref[part, :] * jnp.concatenate([factor, factor], axis=1) + jnp.dot(
                weights.astype(jnp.bfloat16), values_ref[...], preferred_element_type=jnp.float32
            )
        return 0

    lax.fori_loop(0, len(shards), fold, 0)
    if last:
        done = (sum_ref[:, :128] / sum_ref[:, 128:]).astype(jnp.bfloat16)
        whole = refs[4]
        width = whole.shape[1]
        for h in range(heads):
            for i in range(width // 128):
                whole[h * 128 : (h + 1) * 128, i * 128 : (i + 1) * 128] = projections[h][
                    width + i * 128 : width + (i + 1) * 128
                ]
        joined = jnp.concatenate([done[h * rows : (h + 1) * rows] for h in range(heads)], axis=1)
        for out, first_row in ((outs[0], 0), (outs[1], rows // 2)):
            out[...] = jnp.dot(
                joined[first_row : first_row + rows // 2],
                whole[...],
                preferred_element_type=jnp.float32,
            )
    else:
        outs[0][...] = m_ref[...]
        outs[1][...] = sum_ref[...]


def attention(meta, queries, shards, sources, state, projections, pages):
    heads = 4
    n, span = queries.shape[0], shards[0].shape[0]
    vmem = pl.BlockSpec(memory_space=pltpu.VMEM)
    last = bool(projections)
    kinds = (
        [jax.ShapeDtypeStruct((n // heads // 2, projections[0].shape[0] // 2), jnp.float32)] * 2
        if last
        else [
            jax.ShapeDtypeStruct((n, 128), jnp.float32),
            jax.ShapeDtypeStruct((n, 256), jnp.float32),
        ]
    )
    return pl.pallas_call(
        lambda *refs: attention_kernel(
            *refs, sources=sources, first=not state, last=last, pages=pages, heads=heads
        ),
        out_shape=kinds,
        in_specs=[pl.BlockSpec(memory_space=pltpu.SMEM)]
        + [vmem] * (1 + len(shards) + len(state) + len(projections)),
        out_specs=[vmem] * len(kinds),
        scratch_shapes=[
            pltpu.VMEM((span, 128), jnp.bfloat16),
            pltpu.VMEM((span, 256), jnp.bfloat16),
            pltpu.VMEM((n, 128), jnp.float32),
            pltpu.VMEM((n, 256), jnp.float32),
        ]
        + [pltpu.VMEM((heads * 128, p.shape[0] // 2), jnp.bfloat16) for p in projections[:1]],
        compiler_params=pltpu.CompilerParams(vmem_limit_bytes=40 * 2**20),
        cost_estimate=pl.CostEstimate(
            flops=6 * n * span * 128 * len(shards),
            bytes_accessed=4 * 2**20,
            transcendentals=n * span * len(shards),
        ),
        name="attention",
    )(meta, queries, *shards, *state, *projections)


def gate_kernel(
    hidden_ref, partial_ref, received_ref, gain_ref, router_ref, base_ref, mid_ref, a_ref, b_ref
):
    half = hidden_ref.shape[1] // 2
    rows, top = hidden_ref.shape[0], 4
    total = hidden_ref[...].astype(jnp.float32) + (partial_ref[...] + received_ref[...])
    mid = total.astype(jnp.bfloat16)
    mid_ref[...] = mid
    values = mid.astype(jnp.float32)
    inverse = lax.rsqrt(jnp.mean(values * values, axis=-1, keepdims=True) + epsilon)
    normed = (values * inverse * gain_ref[...]).astype(jnp.bfloat16)
    logits = jnp.dot(normed, router_ref[...], preferred_element_type=jnp.float32)
    expert = lax.broadcasted_iota(jnp.int32, logits.shape, 1).astype(jnp.float32)
    raised = [
        jnp.exp(
            jnp.sum(
                jnp.where(base_ref[:, k : k + 1] == expert, logits, 0.0), axis=1, keepdims=True
            )
        )
        for k in range(top)
    ]
    whole = sum(raised[1:], raised[0])
    lane = lax.broadcasted_iota(jnp.int32, (rows, 128), 1)
    table = base_ref[...]
    for k in range(top):
        gate = raised[k] / whole
        high = gate.astype(jnp.bfloat16).astype(jnp.float32)
        table = jnp.where(lane == 2 * top + k, high, table)
        table = jnp.where(lane == 3 * top + k, gate - high, table)
    table = table.astype(jnp.bfloat16)
    a_ref[:, :half] = normed[:, :half]
    a_ref[:, half:] = table
    b_ref[:, :half] = normed[:, half:]
    b_ref[:, half:] = table


def table_kernel(routes_ref, o_ref):
    rows, top = routes_ref.shape
    expert = lax.broadcasted_iota(jnp.int32, (rows, 32), 1)
    named = [(routes_ref[:, k : k + 1] == expert).astype(jnp.float32) for k in range(top)]
    later = lax.broadcasted_iota(jnp.int32, (rows, rows), 0)
    earlier = lax.broadcasted_iota(jnp.int32, (rows, rows), 1)
    before = jnp.dot(
        (later > earlier).astype(jnp.float32),
        sum(named[1:], named[0]),
        preferred_element_type=jnp.float32,
    )
    lane = lax.broadcasted_iota(jnp.int32, (rows, 128), 1)
    table = jnp.zeros((rows, 128), jnp.float32)
    for k in range(top):
        slot = jnp.sum(named[k] * before, axis=1, keepdims=True)
        table = jnp.where(lane == k, routes_ref[:, k : k + 1].astype(jnp.float32), table)
        table = jnp.where(lane == top + k, slot, table)
    o_ref[...] = table


def key_kernel(meta, own_ref, other_ref, w_ref, o_ref):
    half = own_ref.shape[0]
    for i, ref in enumerate((own_ref, other_ref)):
        o_ref[i * half : (i + 1) * half, :] = jnp.dot(
            ref[...], w_ref[0], preferred_element_type=jnp.float32
        ).astype(jnp.bfloat16)


def query_kernel(own_ref, other_ref, *refs):
    half = own_ref.shape[0]
    for h, w_ref in enumerate(refs[:-1]):
        for i, ref in enumerate((own_ref, other_ref)):
            start = (2 * h + i) * half
            refs[-1][start : start + half, :] = jnp.dot(
                ref[...], w_ref[: ref.shape[1]], preferred_element_type=jnp.float32
            ).astype(jnp.bfloat16)


def stack_kernel(wq_ref, wo_ref, o_ref):
    width = wq_ref.shape[0]
    o_ref[:width] = wq_ref[...]
    for i in range(width // 128):
        o_ref[width + i * 128 : width + (i + 1) * 128] = wo_ref[:, i * 128 : (i + 1) * 128]


def shard_kernel(meta, pages_ref, *refs):
    line, shard_ref, ordered_ref = refs[:ZL], refs[ZL], refs[ZL + 1]
    zl, c = meta[1], meta[2]
    pages = pages_ref.shape[0]
    shard_ref[:pages, :] = pages_ref[...]
    for i, ref in enumerate(line):
        shard_ref[pages + i * 256 : pages + (i + 1) * 256, :] = ref[...]
    col = pl.multiple_of(lax.rem(zl, 2) * 128, 128)
    for z in range(ZL):
        slot = lax.rem(zl - z + 4, 4)
        for half in range(2):
            inner = half * (1 - 2 * c) + c
            start = pl.multiple_of(pages + slot * 256 + inner * 128, 128)
            ordered_ref[z * 256 + half * 128 : z * 256 + half * 128 + 128, :] = shard_ref[
                pl.ds(start, 128), pl.ds(col, 128)
            ]


def body(
    hidden_in,
    routes,
    prefix_len,
    cache,
    attn_gain,
    w_query,
    w_keyval,
    w_out,
    moe_gain,
    w_router,
    expert_in,
    expert_out,
):
    y, zl, c = lax.axis_index("y"), lax.axis_index("zl"), lax.axis_index("c")
    rep = lax.axis_index(("x", "zh"))
    rows_dev, width = hidden_in.shape
    length = lax.dynamic_index_in_dim(prefix_len, rep, 0, keepdims=False)
    meta = jnp.stack([y, zl, c, length]).astype(jnp.int32)
    smem = pl.BlockSpec(memory_space=pltpu.SMEM)
    vmem = pl.BlockSpec(memory_space=pltpu.VMEM)

    group_size = 4
    to_group = []
    for z in range(ZH * ZL):
        for k in range(C):
            t = (z + k * (2 * (z % 2) - 1)) % (ZH * ZL)
            to_group.append((z * C + k, t * C + (z % ZL) // 2))

    def line_of(a):
        return [a] + [shift_line(a, s) for s in (1, 2, 3)]

    with jax.named_scope("weights"):
        stacked = pl.pallas_call(
            stack_kernel,
            out_shape=jax.ShapeDtypeStruct((2 * width, 128), jnp.bfloat16),
            in_specs=[vmem] * 2,
            out_specs=vmem,
            name="stack",
        )(w_query, w_out)
        weights = spread_out(lax.ppermute(stacked, ("zh", "zl", "c"), to_group), shift_z)

    with jax.named_scope("keys"):
        normed = rms_scale(hidden_in, attn_gain)
        own_pages = lax.dynamic_index_in_dim(cache, c, 1, keepdims=True)
        normed, own_pages = lax.optimization_barrier((normed, own_pages))
        beside = swap_core(normed)
        whole = pl.BlockSpec((rows_dev, width), lambda i, meta: (0, 0))
        kv = pl.pallas_call(
            key_kernel,
            out_shape=jax.ShapeDtypeStruct((2 * rows_dev, 256), jnp.bfloat16),
            grid_spec=pltpu.PrefetchScalarGridSpec(
                num_scalar_prefetch=1,
                grid=(1,),
                in_specs=[whole, whole, pl.BlockSpec((1, width, 256), lambda i, meta: (meta[2], 0, 0))],
                out_specs=pl.BlockSpec((2 * rows_dev, 256), lambda i, meta: (0, 0)),
            ),
            name="key",
        )(meta, normed, beside, w_keyval)
        kv, routes = lax.optimization_barrier((kv, routes))
        line = line_of(kv)
        fetched = lax.all_to_all(own_pages, ("x", "zh"), split_axis=0, concat_axis=2, tiled=True)
        pages = fetched.reshape(-1, 256)
        shard, ordered = pl.pallas_call(
            shard_kernel,
            out_shape=[
                jax.ShapeDtypeStruct((1536, 256), jnp.bfloat16),
                jax.ShapeDtypeStruct((1024, 128), jnp.bfloat16),
            ],
            in_specs=[smem] + [vmem] * 5,
            out_specs=[vmem] * 2,
            name="shard",
        )(meta, pages, *line)
        up = shift_y(shard, 1)
        down = shift_y(shard, -1)

    with jax.named_scope("new_cache"):
        ordered, down = lax.optimization_barrier((ordered, down))
        other = swap_core(ordered)
        held = jnp.where(c == zl // 2, ordered, other)
        new_cache = jnp.where(c == 0, held[:, :64], held[:, 64:])

    with jax.named_scope("routing"):
        experts_all = w_router.shape[1]
        top = routes.shape[1]
        base = pl.pallas_call(
            table_kernel,
            out_shape=jax.ShapeDtypeStruct((rows_dev, 128), jnp.float32),
            in_specs=[vmem],
            out_specs=vmem,
            name="table",
        )(routes)

    with jax.named_scope("queries"):
        queries = pl.pallas_call(
            query_kernel,
            out_shape=jax.ShapeDtypeStruct((2 * rows_dev * group_size, 128), jnp.bfloat16),
            in_specs=[vmem] * (2 + group_size),
            out_specs=vmem,
            name="query",
        )(normed, beside, *weights)

    with jax.named_scope("attention"):
        n_pages = pages.shape[0]
        far = shift_y(up, 1)
        state = attention(meta, queries, [shard], [0], (), (), n_pages)
        state = attention(meta, queries, [up, down], [-1, 1], state, (), n_pages)
        partial, leaving = attention(meta, queries, [far], [2], state, weights, n_pages)

    with jax.named_scope("out_projection"):
        half = width // 2
        received = swap_core(leaving)
        wide = jax.ShapeDtypeStruct((rows_dev, half + 128), jnp.bfloat16)
        mid, send_1, send_2 = pl.pallas_call(
            gate_kernel,
            out_shape=[jax.ShapeDtypeStruct((rows_dev, width), jnp.bfloat16), wide, wide],
            in_specs=[vmem] * 6,
            out_specs=[vmem] * 3,
            compiler_params=pltpu.CompilerParams(vmem_limit_bytes=16 * 2**20),
            name="gate",
        )(hidden_in, partial, received, moe_gain[None], w_router, base)

    with jax.named_scope("routing"):
        step = 1 - 2 * c
        z = lax.axis_index(("zh", "zl"))
        y_goals = jnp.stack([y, y + step, y - step, y + 2]) % Y
        z_goals = jnp.stack([z, z + step, z - step, z + 2 * step]) % ZL
        cores = jnp.stack([c, 1 - c])
        half = width // 2
        spread = experts_all * CAP

        def keys_of(first):
            inner = jnp.arange(4, dtype=jnp.int32)[:, None] * spread + jnp.arange(CAP, dtype=jnp.int32)
            return (first[:, :, None, None] * CAP + inner[None, None]).reshape(1, -1)

        keys_1 = keys_of(y_goals[:, None] * 8 + (z % ZL) * 2 + cores[None, :])
        keys_2 = keys_of(y * 8 + z_goals[:, None] * 2 + cores[None, :])

    def to_y(a, s):
        return shift_y(a, s)

    def to_z(a, s):
        return shift_z(a, s)

    block = 2 * 4 * CAP

    with jax.named_scope("dispatch"):
        near_1 = jnp.concatenate(spread_out(send_1, to_z), axis=0)
        near_2 = jnp.concatenate(spread_out(send_2, to_y), axis=0)

        def named_of(near):
            ids = near[:, half : half + top].astype(jnp.int32)
            slots = near[:, half + top : half + 2 * top].astype(jnp.int32)
            source = lax.broadcasted_iota(jnp.int32, ids.shape, 0) // rows_dev
            return ids * CAP + slots + source * spread

        def placed_of(keys, named):
            return sum((named[:, k : k + 1] == keys) for k in range(top)).astype(jnp.bfloat16)

        named_1, named_2 = named_of(near_1), named_of(near_2)
        placed_1, placed_2 = placed_of(keys_1, named_1), placed_of(keys_2, named_2)

        def pack(placed, near, send):
            out = []
            for d, s in enumerate((0, 1, -1, 2)):
                packed = lax.dot_general(
                    placed[:, d * block : (d + 1) * block],
                    near[:, :half],
                    (((0,), (0,)), ((), ())),
                    preferred_element_type=jnp.float32,
                ).astype(jnp.bfloat16)
                out.append((send(packed, s) if s else packed).reshape(2, 4, CAP, half))
            return out

        held_1 = pack(placed_1, near_1, to_y)
        held_2 = pack(placed_2, near_2, to_z)

        def joined(core):
            return jnp.concatenate(
                [
                    jnp.stack([a[core] for a in held_1], axis=0),
                    jnp.stack([a[core] for a in held_2], axis=1),
                ],
                axis=-1,
            ).reshape(16 * CAP, width)

        passed = swap_core(joined(1))
        kept = joined(0)

    with jax.named_scope("mix"):

        def mix_of(keys, named, near):
            def weighted(first):
                return sum(
                    jnp.where(
                        named[:, k : k + 1] == keys,
                        near[:, half + first + k : half + first + k + 1].astype(jnp.float32),
                        0.0,
                    )
                    for k in range(top)
                ).astype(jnp.bfloat16)

            return jnp.concatenate([weighted(2 * top), weighted(3 * top)], axis=0)

        mix_1 = mix_of(keys_1, named_1, near_1)
        mix_2 = mix_of(keys_2, named_2, near_2)

    with jax.named_scope("experts"):
        inner_dim = expert_out.shape[1]

        def expert(rows):
            inner = jnp.dot(rows, expert_in[0], preferred_element_type=jnp.float32)
            active = (jnp.maximum(inner[:, :inner_dim], 0.0) * inner[:, inner_dim:]).astype(
                jnp.bfloat16
            )
            return jnp.dot(active, expert_out[0], preferred_element_type=jnp.float32).astype(
                jnp.bfloat16
            )

        shape = (4, 4, CAP, width)
        passed_back = swap_core(expert(passed)).reshape(shape)
        kept_back = expert(kept).reshape(shape)

    with jax.named_scope("combine"):

        def give_back(parts, send):
            out = []
            for d, s in enumerate((0, -1, 1, -2)):
                out.append(send(parts[d], s) if s else parts[d])
            return out

        parts_1 = [
            jnp.stack([kept_back[i, :, :, :half], passed_back[i, :, :, :half]]).reshape(block, half)
            for i in range(4)
        ]
        parts_2 = [
            jnp.stack([kept_back[:, j, :, half:], passed_back[:, j, :, half:]]).reshape(block, half)
            for j in range(4)
        ]

        def summed(mix, parts, send, back):
            rows = jnp.concatenate(give_back(parts, send), axis=0)
            both_sums = jnp.dot(mix, rows, preferred_element_type=jnp.float32)
            sums = both_sums[: 4 * rows_dev] + both_sums[4 * rows_dev :]
            mine = sums[:rows_dev]
            away = [
                sums[d * rows_dev : (d + 1) * rows_dev].astype(jnp.bfloat16) for d in range(4)
            ]
            return [mine] + give_back(away, back)[1:]

        total_1 = summed(mix_1, parts_1, to_y, to_z)
        total_2 = summed(mix_2, parts_2, to_z, to_y)
        mixed = jnp.concatenate(
            [sum(a.astype(jnp.float32) for a in t) for t in (total_1, total_2)], axis=1
        )
        hidden_out = (mid.astype(jnp.float32) + mixed).astype(jnp.bfloat16)
    return (hidden_out, new_cache)


def solution(mesh):
    axes = ("x", "zh", "y", "zl", "c")
    split = Mesh(mesh.devices.reshape(X, ZH, Y, ZL, C), axes)
    placed = (
        P(axes, None),
        P(axes, None),
        P(),
        P(None, None, ("x", "zh", "y"), None),
        P(),
        P(None, ("zl", "c")),
        P(),
        P(("zl", "c"), None),
        P(),
        P(),
        P(("y", "zl", "c"), None, None),
        P(("y", "zl", "c"), None, None),
    )
    return jax.shard_map(
        body,
        mesh=split,
        in_specs=placed,
        out_specs=(P(axes, None), P(("x", "zh", "y"), ("zl", "c"))),
        check_vma=False,
    )
```

```python
import jax
import jax.numpy as jnp
from jax import lax
from jax.experimental import pallas as pl
from jax.experimental.pallas import tpu as pltpu
from jax.sharding import Mesh
from jax.sharding import PartitionSpec as P

CAP = 24
epsilon = 1e-06
masked_score = -1e30
log2e = 1.4426950408889634

X, ZH, Y, ZL, C = 4, 2, 4, 4, 2


def rms_scale(rows, gain):
    values = rows.astype(jnp.float32)
    inverse = lax.rsqrt(jnp.mean(values * values, axis=-1, keepdims=True) + epsilon)
    return (values * inverse * gain).astype(jnp.bfloat16)


def swap_core(a):
    return lax.ppermute(a, "c", [(0, 1), (1, 0)])


def shift_line(a, s):
    return lax.ppermute(a, "zl", [(i, (i + s) % ZL) for i in range(ZL)])


def shift_y(a, s):
    pairs = []
    for y in range(Y):
        for c in range(C):
            t = (y + (s if c == 0 else -s)) % Y
            pairs.append((y * C + c, t * C + c))
    return lax.ppermute(a, ("y", "c"), pairs)


def shift_z(a, s):
    pairs = []
    n = ZH * ZL
    for z in range(n):
        for c in range(C):
            t = (z + (s if c == 0 else -s)) % n
            pairs.append((z * C + c, t * C + c))
    return lax.ppermute(a, ("zh", "zl", "c"), pairs)


def spread_out(a, send):
    return [a, send(a, 1), send(a, -1), send(a, 2)]


def attention_kernel(meta, q_ref, *refs, sources, first, last, pages, heads):
    refs = list(refs)
    shards = [refs.pop(0) for _ in sources]
    before = None if first else (refs.pop(0), refs.pop(0))
    projections = [refs.pop(0) for _ in range(heads)] if last else None
    outs = [refs.pop(0), refs.pop(0)]
    keys_ref, values_ref, m_ref, sum_ref = refs
    span = keys_ref.shape[0]
    rows = q_ref.shape[0] // heads
    scale = log2e / float(128) ** 0.5
    y, zl, c, length = meta[0], meta[1], meta[2], meta[3]
    if first:
        m_ref[...] = jnp.full(m_ref.shape, masked_score, jnp.float32)
        sum_ref[...] = jnp.zeros(sum_ref.shape, jnp.float32)
    else:
        m_ref[...] = before[0][...]
        sum_ref[...] = before[1][...]
    values_ref[:, 128:] = jnp.ones((span, 128), jnp.bfloat16)

    def half_of(index):
        return ((index % 256) // 128) * (1 - 2 * c) + c

    key = lax.broadcasted_iota(jnp.int32, (1, span), 1)
    fresh = key - pages

    def fold(index, _):
        away = 0
        for i, ref in enumerate(shards):
            away = jnp.where(index == i, sources[i], away)

            @pl.when(index == i)
            def _(ref=ref):
                keys_ref[...] = ref[:, :128]
                values_ref[:, :128] = ref[:, 128:]

        source = lax.rem(y + away * (1 - 2 * c) + 4, 4)
        position = (key // 64 * 4 + source) * 64 + key % 64
        if first:
            place = ((zl - fresh // 256 + 4) % 4) * 256 + half_of(fresh) * 128 + fresh % 128
            bound = jnp.where(key < pages, jnp.where(position < length, -1, 2**20), place)
            row = lax.broadcasted_iota(jnp.int32, (rows, 1), 0)
            row_place = zl * 256 + half_of(row) * 128 + row % 128
            visible = bound <= row_place
        else:
            visible = jnp.where(key < pages, position, source) < jnp.where(key < pages, length, y)
        for h in range(heads):
            part = pl.ds(h * rows, rows)
            scores = lax.dot_general(
                q_ref[part, :],
                keys_ref[...],
                (((1,), (1,)), ((), ())),
                preferred_element_type=jnp.float32,
            )
            scores = jnp.where(visible, scores, masked_score)
            old = m_ref[part, :]
            new = jnp.maximum(old, jnp.max(scores, axis=1, keepdims=True))
            m_ref[part, :] = new
            weights = jnp.exp2(scores * scale - new[:, :1] * scale)
            factor = jnp.exp2((old - new) * scale)
            sum_ref[part, :] = sum_ref[part, :] * jnp.concatenate([factor, factor], axis=1) + jnp.dot(
                weights.astype(jnp.bfloat16), values_ref[...], preferred_element_type=jnp.float32
            )
        return 0

    lax.fori_loop(0, len(shards), fold, 0)
    if last:
        done = (sum_ref[:, :128] / sum_ref[:, 128:]).astype(jnp.bfloat16)
        for out, first_row in ((outs[0], 0), (outs[1], rows // 2)):
            out[...] = sum(
                jnp.dot(
                    done[h * rows + first_row : h * rows + first_row + rows // 2],
                    projections[h][...],
                    preferred_element_type=jnp.float32,
                )
                for h in range(heads)
            )
    else:
        outs[0][...] = m_ref[...]
        outs[1][...] = sum_ref[...]


def attention(meta, queries, shards, sources, state, projections, pages):
    heads = 4
    n, span = queries.shape[0], shards[0].shape[0]
    vmem = pl.BlockSpec(memory_space=pltpu.VMEM)
    last = bool(projections)
    kinds = (
        [jax.ShapeDtypeStruct((n // heads // 2, projections[0].shape[1]), jnp.float32)] * 2
        if last
        else [
            jax.ShapeDtypeStruct((n, 128), jnp.float32),
            jax.ShapeDtypeStruct((n, 256), jnp.float32),
        ]
    )
    return pl.pallas_call(
        lambda *refs: attention_kernel(
            *refs, sources=sources, first=not state, last=last, pages=pages, heads=heads
        ),
        out_shape=kinds,
        in_specs=[pl.BlockSpec(memory_space=pltpu.SMEM)]
        + [vmem] * (1 + len(shards) + len(state) + len(projections)),
        out_specs=[vmem] * len(kinds),
        scratch_shapes=[
            pltpu.VMEM((span, 128), jnp.bfloat16),
            pltpu.VMEM((span, 256), jnp.bfloat16),
            pltpu.VMEM((n, 128), jnp.float32),
            pltpu.VMEM((n, 256), jnp.float32),
        ],
        compiler_params=pltpu.CompilerParams(vmem_limit_bytes=40 * 2**20),
        cost_estimate=pl.CostEstimate(
            flops=6 * n * span * 128 * len(shards),
            bytes_accessed=4 * 2**20,
            transcendentals=n * span * len(shards),
        ),
        name="attention",
    )(meta, queries, *shards, *state, *projections)


def gate_kernel(
    hidden_ref, partial_ref, received_ref, gain_ref, router_ref, base_ref, mid_ref, a_ref, b_ref
):
    half = hidden_ref.shape[1] // 2
    rows, top = hidden_ref.shape[0], 4
    total = hidden_ref[...].astype(jnp.float32) + (partial_ref[...] + received_ref[...])
    mid = total.astype(jnp.bfloat16)
    mid_ref[...] = mid
    values = mid.astype(jnp.float32)
    inverse = lax.rsqrt(jnp.mean(values * values, axis=-1, keepdims=True) + epsilon)
    normed = (values * inverse * gain_ref[...]).astype(jnp.bfloat16)
    logits = jnp.dot(normed, router_ref[...], preferred_element_type=jnp.float32)
    expert = lax.broadcasted_iota(jnp.int32, logits.shape, 1).astype(jnp.float32)
    raised = [
        jnp.exp(
            jnp.sum(
                jnp.where(base_ref[:, k : k + 1] == expert, logits, 0.0), axis=1, keepdims=True
            )
        )
        for k in range(top)
    ]
    whole = sum(raised[1:], raised[0])
    lane = lax.broadcasted_iota(jnp.int32, (rows, 128), 1)
    table = base_ref[...]
    for k in range(top):
        gate = raised[k] / whole
        high = gate.astype(jnp.bfloat16).astype(jnp.float32)
        table = jnp.where(lane == 2 * top + k, high, table)
        table = jnp.where(lane == 3 * top + k, gate - high, table)
    table = table.astype(jnp.bfloat16)
    a_ref[:, :half] = normed[:, :half]
    a_ref[:, half:] = table
    b_ref[:, :half] = normed[:, half:]
    b_ref[:, half:] = table


def table_kernel(routes_ref, o_ref):
    rows, top = routes_ref.shape
    expert = lax.broadcasted_iota(jnp.int32, (rows, 32), 1)
    named = [(routes_ref[:, k : k + 1] == expert).astype(jnp.float32) for k in range(top)]
    later = lax.broadcasted_iota(jnp.int32, (rows, rows), 0)
    earlier = lax.broadcasted_iota(jnp.int32, (rows, rows), 1)
    before = jnp.dot(
        (later > earlier).astype(jnp.float32),
        sum(named[1:], named[0]),
        preferred_element_type=jnp.float32,
    )
    lane = lax.broadcasted_iota(jnp.int32, (rows, 128), 1)
    table = jnp.zeros((rows, 128), jnp.float32)
    for k in range(top):
        slot = jnp.sum(named[k] * before, axis=1, keepdims=True)
        table = jnp.where(lane == k, routes_ref[:, k : k + 1].astype(jnp.float32), table)
        table = jnp.where(lane == top + k, slot, table)
    o_ref[...] = table


def key_kernel(meta, own_ref, other_ref, w_ref, o_ref):
    half = own_ref.shape[0]
    for i, ref in enumerate((own_ref, other_ref)):
        o_ref[i * half : (i + 1) * half, :] = jnp.dot(
            ref[...], w_ref[0], preferred_element_type=jnp.float32
        ).astype(jnp.bfloat16)


def query_kernel(own_ref, other_ref, *refs):
    half = own_ref.shape[0]
    for h, w_ref in enumerate(refs[:-1]):
        for i, ref in enumerate((own_ref, other_ref)):
            start = (2 * h + i) * half
            refs[-1][start : start + half, :] = jnp.dot(
                ref[...], w_ref[...], preferred_element_type=jnp.float32
            ).astype(jnp.bfloat16)


def shard_kernel(meta, pages_ref, *refs):
    line, shard_ref, ordered_ref = refs[:ZL], refs[ZL], refs[ZL + 1]
    zl, c = meta[1], meta[2]
    pages = pages_ref.shape[0]
    shard_ref[:pages, :] = pages_ref[...]
    for i, ref in enumerate(line):
        shard_ref[pages + i * 256 : pages + (i + 1) * 256, :] = ref[...]
    col = pl.multiple_of(lax.rem(zl, 2) * 128, 128)
    for z in range(ZL):
        slot = lax.rem(zl - z + 4, 4)
        for half in range(2):
            inner = half * (1 - 2 * c) + c
            start = pl.multiple_of(pages + slot * 256 + inner * 128, 128)
            ordered_ref[z * 256 + half * 128 : z * 256 + half * 128 + 128, :] = shard_ref[
                pl.ds(start, 128), pl.ds(col, 128)
            ]


def body(
    hidden_in,
    routes,
    prefix_len,
    cache,
    attn_gain,
    w_query,
    w_keyval,
    w_out,
    moe_gain,
    w_router,
    expert_in,
    expert_out,
):
    y, zl, c = lax.axis_index("y"), lax.axis_index("zl"), lax.axis_index("c")
    rep = lax.axis_index(("x", "zh"))
    rows_dev, width = hidden_in.shape
    length = lax.dynamic_index_in_dim(prefix_len, rep, 0, keepdims=False)
    meta = jnp.stack([y, zl, c, length]).astype(jnp.int32)
    smem = pl.BlockSpec(memory_space=pltpu.SMEM)
    vmem = pl.BlockSpec(memory_space=pltpu.VMEM)

    group_size = 4
    def to_group(a):
        out = []
        for s in range(ZL):
            pairs = []
            for z in range(ZH * ZL):
                for k in range(C):
                    goal = 2 * (z % 2) + k + s
                    hops = (goal - z + 1) % ZL - 1
                    if hops == 2 and k:
                        hops = -2
                    t = (z + hops) % (ZH * ZL)
                    pairs.append((z * C + k, t * C + (z % ZL) // 2))
            out.append(lax.ppermute(a, ("zh", "zl", "c"), pairs))
        return out

    def line_of(a):
        return [a] + [shift_line(a, s) for s in (1, 2, 3)]

    with jax.named_scope("weights"):
        wq = to_group(w_query)

    with jax.named_scope("keys"):
        normed = rms_scale(hidden_in, attn_gain)
        own_pages = lax.dynamic_index_in_dim(cache, c, 1, keepdims=True)
        normed, own_pages = lax.optimization_barrier((normed, own_pages))
        beside = swap_core(normed)
        whole = pl.BlockSpec((rows_dev, width), lambda i, meta: (0, 0))
        kv = pl.pallas_call(
            key_kernel,
            out_shape=jax.ShapeDtypeStruct((2 * rows_dev, 256), jnp.bfloat16),
            grid_spec=pltpu.PrefetchScalarGridSpec(
                num_scalar_prefetch=1,
                grid=(1,),
                in_specs=[whole, whole, pl.BlockSpec((1, width, 256), lambda i, meta: (meta[2], 0, 0))],
                out_specs=pl.BlockSpec((2 * rows_dev, 256), lambda i, meta: (0, 0)),
            ),
            name="key",
        )(meta, normed, beside, w_keyval)
        kv, wq = lax.optimization_barrier((kv, wq))
        line = line_of(kv)
        fetched = lax.all_to_all(own_pages, ("x", "zh"), split_axis=0, concat_axis=2, tiled=True)
        pages = fetched.reshape(-1, 256)
        shard, ordered = pl.pallas_call(
            shard_kernel,
            out_shape=[
                jax.ShapeDtypeStruct((1536, 256), jnp.bfloat16),
                jax.ShapeDtypeStruct((1024, 128), jnp.bfloat16),
            ],
            in_specs=[smem] + [vmem] * 5,
            out_specs=[vmem] * 2,
            name="shard",
        )(meta, pages, *line)
        up = shift_y(shard, 1)
        down = shift_y(shard, -1)

    with jax.named_scope("new_cache"):
        other, w_out = lax.optimization_barrier((swap_core(ordered), w_out))
        held = jnp.where(c == zl // 2, ordered, other)
        new_cache = jnp.where(c == 0, held[:, :64], held[:, 64:])

    with jax.named_scope("weights"):
        wo = to_group(w_out)

    with jax.named_scope("routing"):
        experts_all = w_router.shape[1]
        top = routes.shape[1]
        base = pl.pallas_call(
            table_kernel,
            out_shape=jax.ShapeDtypeStruct((rows_dev, 128), jnp.float32),
            in_specs=[vmem],
            out_specs=vmem,
            name="table",
        )(routes)

    with jax.named_scope("queries"):
        queries = pl.pallas_call(
            query_kernel,
            out_shape=jax.ShapeDtypeStruct((2 * rows_dev * group_size, 128), jnp.bfloat16),
            in_specs=[vmem] * (2 + group_size),
            out_specs=vmem,
            name="query",
        )(normed, beside, *wq)

    with jax.named_scope("attention"):
        n_pages = pages.shape[0]
        queries, base = lax.optimization_barrier((queries, base))
        state = attention(meta, queries, [shard], [0], (), (), n_pages)
        state, up, down = lax.optimization_barrier((state, up, down))
        far = shift_y(up, 1)
        state = attention(meta, queries, [up, down], [-1, 1], state, (), n_pages)
        partial, leaving = attention(meta, queries, [far], [2], state, wo, n_pages)

    with jax.named_scope("out_projection"):
        half = width // 2
        received = swap_core(leaving)
        wide = jax.ShapeDtypeStruct((rows_dev, half + 128), jnp.bfloat16)
        mid, send_1, send_2 = pl.pallas_call(
            gate_kernel,
            out_shape=[jax.ShapeDtypeStruct((rows_dev, width), jnp.bfloat16), wide, wide],
            in_specs=[vmem] * 6,
            out_specs=[vmem] * 3,
            compiler_params=pltpu.CompilerParams(vmem_limit_bytes=16 * 2**20),
            name="gate",
        )(hidden_in, partial, received, moe_gain[None], w_router, base)

    with jax.named_scope("routing"):
        step = 1 - 2 * c
        z = lax.axis_index(("zh", "zl"))
        y_goals = jnp.stack([y, y + step, y - step, y + 2]) % Y
        z_goals = jnp.stack([z, z + step, z - step, z + 2 * step]) % ZL
        cores = jnp.stack([c, 1 - c])
        half = width // 2
        spread = experts_all * CAP

        def keys_of(first):
            inner = jnp.arange(4, dtype=jnp.int32)[:, None] * spread + jnp.arange(CAP, dtype=jnp.int32)
            return (first[:, :, None, None] * CAP + inner[None, None]).reshape(1, -1)

        keys_1 = keys_of(y_goals[:, None] * 8 + (z % ZL) * 2 + cores[None, :])
        keys_2 = keys_of(y * 8 + z_goals[:, None] * 2 + cores[None, :])

    def to_y(a, s):
        return shift_y(a, s)

    def to_z(a, s):
        return shift_z(a, s)

    block = 2 * 4 * CAP

    with jax.named_scope("dispatch"):
        near_1 = jnp.concatenate(spread_out(send_1, to_z), axis=0)
        near_2 = jnp.concatenate(spread_out(send_2, to_y), axis=0)

        def named_of(near):
            ids = near[:, half : half + top].astype(jnp.int32)
            slots = near[:, half + top : half + 2 * top].astype(jnp.int32)
            source = lax.broadcasted_iota(jnp.int32, ids.shape, 0) // rows_dev
            return ids * CAP + slots + source * spread

        def placed_of(keys, named):
            return sum((named[:, k : k + 1] == keys) for k in range(top)).astype(jnp.bfloat16)

        named_1, named_2 = named_of(near_1), named_of(near_2)
        placed_1, placed_2 = placed_of(keys_1, named_1), placed_of(keys_2, named_2)

        def pack(placed, near, send):
            out = []
            for d, s in enumerate((0, 1, -1, 2)):
                packed = lax.dot_general(
                    placed[:, d * block : (d + 1) * block],
                    near[:, :half],
                    (((0,), (0,)), ((), ())),
                    preferred_element_type=jnp.float32,
                ).astype(jnp.bfloat16)
                out.append((send(packed, s) if s else packed).reshape(2, 4, CAP, half))
            return out

        held_1 = pack(placed_1, near_1, to_y)
        held_2 = pack(placed_2, near_2, to_z)

        def joined(core):
            return jnp.concatenate(
                [
                    jnp.stack([a[core] for a in held_1], axis=0),
                    jnp.stack([a[core] for a in held_2], axis=1),
                ],
                axis=-1,
            ).reshape(16 * CAP, width)

        passed = swap_core(joined(1))
        kept = joined(0)

    with jax.named_scope("mix"):

        def mix_of(keys, named, near):
            def weighted(first):
                return sum(
                    jnp.where(
                        named[:, k : k + 1] == keys,
                        near[:, half + first + k : half + first + k + 1].astype(jnp.float32),
                        0.0,
                    )
                    for k in range(top)
                ).astype(jnp.bfloat16)

            return jnp.concatenate([weighted(2 * top), weighted(3 * top)], axis=0)

        mix_1 = mix_of(keys_1, named_1, near_1)
        mix_2 = mix_of(keys_2, named_2, near_2)

    with jax.named_scope("experts"):
        inner_dim = expert_out.shape[1]

        def expert(rows):
            inner = jnp.dot(rows, expert_in[0], preferred_element_type=jnp.float32)
            active = (jnp.maximum(inner[:, :inner_dim], 0.0) * inner[:, inner_dim:]).astype(
                jnp.bfloat16
            )
            return jnp.dot(active, expert_out[0], preferred_element_type=jnp.float32).astype(
                jnp.bfloat16
            )

        shape = (4, 4, CAP, width)
        passed_back = swap_core(expert(passed)).reshape(shape)
        kept_back = expert(kept).reshape(shape)

    with jax.named_scope("combine"):

        def give_back(parts, send):
            out = []
            for d, s in enumerate((0, -1, 1, -2)):
                out.append(send(parts[d], s) if s else parts[d])
            return out

        parts_1 = [
            jnp.stack([kept_back[i, :, :, :half], passed_back[i, :, :, :half]]).reshape(block, half)
            for i in range(4)
        ]
        parts_2 = [
            jnp.stack([kept_back[:, j, :, half:], passed_back[:, j, :, half:]]).reshape(block, half)
            for j in range(4)
        ]

        def summed(mix, parts, send, back):
            rows = jnp.concatenate(give_back(parts, send), axis=0)
            both_sums = jnp.dot(mix, rows, preferred_element_type=jnp.float32)
            sums = both_sums[: 4 * rows_dev] + both_sums[4 * rows_dev :]
            mine = sums[:rows_dev]
            away = [
                sums[d * rows_dev : (d + 1) * rows_dev].astype(jnp.bfloat16) for d in range(4)
            ]
            return [mine] + give_back(away, back)[1:]

        total_1 = summed(mix_1, parts_1, to_y, to_z)
        total_2 = summed(mix_2, parts_2, to_z, to_y)
        mixed = jnp.concatenate(
            [sum(a.astype(jnp.float32) for a in t) for t in (total_1, total_2)], axis=1
        )
        hidden_out = (mid.astype(jnp.float32) + mixed).astype(jnp.bfloat16)
    return (hidden_out, new_cache)


def solution(mesh):
    axes = ("x", "zh", "y", "zl", "c")
    split = Mesh(mesh.devices.reshape(X, ZH, Y, ZL, C), axes)
    placed = (
        P(axes, None),
        P(axes, None),
        P(),
        P(None, None, ("x", "zh", "y"), None),
        P(),
        P(None, ("zl", "c")),
        P(),
        P(("zl", "c"), None),
        P(),
        P(),
        P(("y", "zl", "c"), None, None),
        P(("y", "zl", "c"), None, None),
    )
    return jax.shard_map(
        body,
        mesh=split,
        in_specs=placed,
        out_specs=(P(axes, None), P(("x", "zh", "y"), ("zl", "c"))),
        check_vma=False,
    )
```

```python
import jax
import jax.numpy as jnp
from jax import lax
from jax.experimental import pallas as pl
from jax.experimental.pallas import tpu as pltpu
from jax.sharding import Mesh
from jax.sharding import PartitionSpec as P

CAP = 24
epsilon = 1e-06
masked_score = -1e30
log2e = 1.4426950408889634

X, ZH, Y, ZL, C = 4, 2, 4, 4, 2


def rms_scale(rows, gain):
    values = rows.astype(jnp.float32)
    inverse = lax.rsqrt(jnp.mean(values * values, axis=-1, keepdims=True) + epsilon)
    return (values * inverse * gain).astype(jnp.bfloat16)


def swap_core(a):
    return lax.ppermute(a, "c", [(0, 1), (1, 0)])


def shift_line(a, s):
    return lax.ppermute(a, "zl", [(i, (i + s) % ZL) for i in range(ZL)])


def shift_y(a, s):
    pairs = []
    for y in range(Y):
        for c in range(C):
            t = (y + (s if c == 0 else -s)) % Y
            pairs.append((y * C + c, t * C + c))
    return lax.ppermute(a, ("y", "c"), pairs)


def shift_z(a, s):
    pairs = []
    n = ZH * ZL
    for z in range(n):
        for c in range(C):
            t = (z + (s if c == 0 else -s)) % n
            pairs.append((z * C + c, t * C + c))
    return lax.ppermute(a, ("zh", "zl", "c"), pairs)


def spread_out(a, send):
    return [a, send(a, 1), send(a, -1), send(a, 2)]


def attention_kernel(meta, q_ref, *refs, sources, first, last, pages, heads):
    refs = list(refs)
    shards = [refs.pop(0) for _ in sources]
    before = None if first else (refs.pop(0), refs.pop(0))
    projection = refs.pop(0) if last else None
    outs = [refs.pop(0), refs.pop(0)]
    keys_ref, values_ref, m_ref, sum_ref = refs[:4]
    span = keys_ref.shape[0]
    rows = q_ref.shape[0] // heads
    scale = log2e / float(128) ** 0.5
    y, zl, c, length = meta[0], meta[1], meta[2], meta[3]
    if first:
        m_ref[...] = jnp.full(m_ref.shape, masked_score, jnp.float32)
        sum_ref[...] = jnp.zeros(sum_ref.shape, jnp.float32)
    else:
        m_ref[...] = before[0][...]
        sum_ref[...] = before[1][...]
    values_ref[:, 128:] = jnp.ones((span, 128), jnp.bfloat16)

    def half_of(index):
        return ((index % 256) // 128) * (1 - 2 * c) + c

    key = lax.broadcasted_iota(jnp.int32, (1, span), 1)
    fresh = key - pages

    def fold(index, _):
        away = 0
        for i, ref in enumerate(shards):
            away = jnp.where(index == i, sources[i], away)

            @pl.when(index == i)
            def _(ref=ref):
                keys_ref[...] = ref[:, :128]
                values_ref[:, :128] = ref[:, 128:]

        source = lax.rem(y + away * (1 - 2 * c) + 4, 4)
        position = (key // 64 * 4 + source) * 64 + key % 64
        if first:
            place = ((zl - fresh // 256 + 4) % 4) * 256 + half_of(fresh) * 128 + fresh % 128
            bound = jnp.where(key < pages, jnp.where(position < length, -1, 2**20), place)
            row = lax.broadcasted_iota(jnp.int32, (rows, 1), 0)
            row_place = zl * 256 + half_of(row) * 128 + row % 128
            visible = bound <= row_place
        else:
            visible = jnp.where(key < pages, position, source) < jnp.where(key < pages, length, y)
        for h in range(heads):
            part = pl.ds(h * rows, rows)
            scores = lax.dot_general(
                q_ref[part, :],
                keys_ref[...],
                (((1,), (1,)), ((), ())),
                preferred_element_type=jnp.float32,
            )
            scores = jnp.where(visible, scores, masked_score)
            old = m_ref[part, :]
            new = jnp.maximum(old, jnp.max(scores, axis=1, keepdims=True))
            m_ref[part, :] = new
            weights = jnp.exp2(scores * scale - new[:, :1] * scale)
            factor = jnp.exp2((old - new) * scale)
            sum_ref[part, :] = sum_ref[part, :] * jnp.concatenate([factor, factor], axis=1) + jnp.dot(
                weights.astype(jnp.bfloat16), values_ref[...], preferred_element_type=jnp.float32
            )
        return 0

    lax.fori_loop(0, len(shards), fold, 0)
    if last:
        done = (sum_ref[:, :128] / sum_ref[:, 128:]).astype(jnp.bfloat16)
        whole = refs[4]
        for h in range(heads):
            for i in range(whole.shape[1] // 128):
                whole[h * 128 : (h + 1) * 128, i * 128 : (i + 1) * 128] = projection[
                    h, i * 128 : (i + 1) * 128
                ]
        joined = jnp.concatenate([done[h * rows : (h + 1) * rows] for h in range(heads)], axis=1)
        for out, first_row in ((outs[0], 0), (outs[1], rows // 2)):
            out[...] = jnp.dot(
                joined[first_row : first_row + rows // 2],
                whole[...],
                preferred_element_type=jnp.float32,
            )
    else:
        outs[0][...] = m_ref[...]
        outs[1][...] = sum_ref[...]


def attention(meta, queries, shards, sources, state, projections, pages):
    heads = 4
    n, span = queries.shape[0], shards[0].shape[0]
    vmem = pl.BlockSpec(memory_space=pltpu.VMEM)
    last = bool(projections)
    kinds = (
        [jax.ShapeDtypeStruct((n // heads // 2, projections[0].shape[1]), jnp.float32)] * 2
        if last
        else [
            jax.ShapeDtypeStruct((n, 128), jnp.float32),
            jax.ShapeDtypeStruct((n, 256), jnp.float32),
        ]
    )
    return pl.pallas_call(
        lambda *refs: attention_kernel(
            *refs, sources=sources, first=not state, last=last, pages=pages, heads=heads
        ),
        out_shape=kinds,
        in_specs=[pl.BlockSpec(memory_space=pltpu.SMEM)]
        + [vmem] * (1 + len(shards) + len(state) + len(projections)),
        out_specs=[vmem] * len(kinds),
        scratch_shapes=[
            pltpu.VMEM((span, 128), jnp.bfloat16),
            pltpu.VMEM((span, 256), jnp.bfloat16),
            pltpu.VMEM((n, 128), jnp.float32),
            pltpu.VMEM((n, 256), jnp.float32),
        ]
        + [pltpu.VMEM((heads * 128, p.shape[1]), jnp.bfloat16) for p in projections],
        compiler_params=pltpu.CompilerParams(vmem_limit_bytes=40 * 2**20),
        cost_estimate=pl.CostEstimate(
            flops=6 * n * span * 128 * len(shards),
            bytes_accessed=4 * 2**20,
            transcendentals=n * span * len(shards),
        ),
        name="attention",
    )(meta, queries, *shards, *state, *projections)


def gate_kernel(
    hidden_ref, partial_ref, received_ref, gain_ref, router_ref, base_ref, mid_ref, a_ref, b_ref
):
    half = hidden_ref.shape[1] // 2
    rows, top = hidden_ref.shape[0], 4
    total = hidden_ref[...].astype(jnp.float32) + (partial_ref[...] + received_ref[...])
    mid = total.astype(jnp.bfloat16)
    mid_ref[...] = mid
    values = mid.astype(jnp.float32)
    inverse = lax.rsqrt(jnp.mean(values * values, axis=-1, keepdims=True) + epsilon)
    normed = (values * inverse * gain_ref[...]).astype(jnp.bfloat16)
    logits = jnp.dot(normed, router_ref[...], preferred_element_type=jnp.float32)
    expert = lax.broadcasted_iota(jnp.int32, logits.shape, 1).astype(jnp.float32)
    raised = [
        jnp.exp(
            jnp.sum(
                jnp.where(base_ref[:, k : k + 1] == expert, logits, 0.0), axis=1, keepdims=True
            )
        )
        for k in range(top)
    ]
    whole = sum(raised[1:], raised[0])
    lane = lax.broadcasted_iota(jnp.int32, (rows, 128), 1)
    table = base_ref[...]
    for k in range(top):
        gate = raised[k] / whole
        high = gate.astype(jnp.bfloat16).astype(jnp.float32)
        table = jnp.where(lane == 2 * top + k, high, table)
        table = jnp.where(lane == 3 * top + k, gate - high, table)
    table = table.astype(jnp.bfloat16)
    a_ref[:, :half] = normed[:, :half]
    a_ref[:, half:] = table
    b_ref[:, :half] = normed[:, half:]
    b_ref[:, half:] = table


def table_kernel(routes_ref, o_ref):
    rows, top = routes_ref.shape
    expert = lax.broadcasted_iota(jnp.int32, (rows, 32), 1)
    named = [(routes_ref[:, k : k + 1] == expert).astype(jnp.float32) for k in range(top)]
    later = lax.broadcasted_iota(jnp.int32, (rows, rows), 0)
    earlier = lax.broadcasted_iota(jnp.int32, (rows, rows), 1)
    before = jnp.dot(
        (later > earlier).astype(jnp.float32),
        sum(named[1:], named[0]),
        preferred_element_type=jnp.float32,
    )
    lane = lax.broadcasted_iota(jnp.int32, (rows, 128), 1)
    table = jnp.zeros((rows, 128), jnp.float32)
    for k in range(top):
        slot = jnp.sum(named[k] * before, axis=1, keepdims=True)
        table = jnp.where(lane == k, routes_ref[:, k : k + 1].astype(jnp.float32), table)
        table = jnp.where(lane == top + k, slot, table)
    o_ref[...] = table


def key_kernel(meta, own_ref, other_ref, w_ref, o_ref):
    half = own_ref.shape[0]
    for i, ref in enumerate((own_ref, other_ref)):
        o_ref[i * half : (i + 1) * half, :] = jnp.dot(
            ref[...], w_ref[0], preferred_element_type=jnp.float32
        ).astype(jnp.bfloat16)


def query_kernel(own_ref, other_ref, *refs):
    half = own_ref.shape[0]
    for h, w_ref in enumerate(refs[:-1]):
        for i, ref in enumerate((own_ref, other_ref)):
            start = (2 * h + i) * half
            refs[-1][start : start + half, :] = jnp.dot(
                ref[...], w_ref[: ref.shape[1]], preferred_element_type=jnp.float32
            ).astype(jnp.bfloat16)


def stack_kernel(wq_ref, wo_ref, o_ref):
    width = wq_ref.shape[0]
    o_ref[:width] = wq_ref[...]
    for i in range(wo_ref.shape[1] // 128):
        o_ref[width + i * 128 : width + (i + 1) * 128] = wo_ref[:, i * 128 : (i + 1) * 128]


def shard_kernel(meta, pages_ref, *refs):
    line, shard_ref, ordered_ref = refs[:ZL], refs[ZL], refs[ZL + 1]
    zl, c = meta[1], meta[2]
    pages = pages_ref.shape[0]
    shard_ref[:pages, :] = pages_ref[...]
    for i, ref in enumerate(line):
        shard_ref[pages + i * 256 : pages + (i + 1) * 256, :] = ref[...]
    col = pl.multiple_of(lax.rem(zl, 2) * 128, 128)
    for z in range(ZL):
        slot = lax.rem(zl - z + 4, 4)
        for half in range(2):
            inner = half * (1 - 2 * c) + c
            start = pl.multiple_of(pages + slot * 256 + inner * 128, 128)
            ordered_ref[z * 256 + half * 128 : z * 256 + half * 128 + 128, :] = shard_ref[
                pl.ds(start, 128), pl.ds(col, 128)
            ]


def body(
    hidden_in,
    routes,
    prefix_len,
    cache,
    attn_gain,
    w_query,
    w_keyval,
    w_out,
    moe_gain,
    w_router,
    expert_in,
    expert_out,
):
    y, zl, c = lax.axis_index("y"), lax.axis_index("zl"), lax.axis_index("c")
    rep = lax.axis_index(("x", "zh"))
    rows_dev, width = hidden_in.shape
    length = lax.dynamic_index_in_dim(prefix_len, rep, 0, keepdims=False)
    meta = jnp.stack([y, zl, c, length]).astype(jnp.int32)
    smem = pl.BlockSpec(memory_space=pltpu.SMEM)
    vmem = pl.BlockSpec(memory_space=pltpu.VMEM)

    group_size = 4
    def to_group(a):
        out = []
        for s in range(ZL):
            pairs = []
            for z in range(ZH * ZL):
                for k in range(C):
                    goal = 2 * (z % 2) + k + s
                    hops = (goal - z + 1) % ZL - 1
                    if hops == 2 and k:
                        hops = -2
                    t = (z + hops) % (ZH * ZL)
                    pairs.append((z * C + k, t * C + (z % ZL) // 2))
            out.append(lax.ppermute(a, ("zh", "zl", "c"), pairs))
        return out

    def line_of(a):
        return [a] + [shift_line(a, s) for s in (1, 2, 3)]

    with jax.named_scope("weights"):
        share = width // X
        columns = lax.dynamic_slice_in_dim(w_out, lax.axis_index("x") * share, share, 1)
        stacked = pl.pallas_call(
            stack_kernel,
            out_shape=jax.ShapeDtypeStruct((width + share, 128), jnp.bfloat16),
            in_specs=[vmem] * 2,
            out_specs=vmem,
            name="stack",
        )(w_query, columns)
        wq = to_group(stacked)

    with jax.named_scope("keys"):
        normed = rms_scale(hidden_in, attn_gain)
        own_pages = lax.dynamic_index_in_dim(cache, c, 1, keepdims=True)
        normed, own_pages = lax.optimization_barrier((normed, own_pages))
        beside = swap_core(normed)
        whole = pl.BlockSpec((rows_dev, width), lambda i, meta: (0, 0))
        kv = pl.pallas_call(
            key_kernel,
            out_shape=jax.ShapeDtypeStruct((2 * rows_dev, 256), jnp.bfloat16),
            grid_spec=pltpu.PrefetchScalarGridSpec(
                num_scalar_prefetch=1,
                grid=(1,),
                in_specs=[whole, whole, pl.BlockSpec((1, width, 256), lambda i, meta: (meta[2], 0, 0))],
                out_specs=pl.BlockSpec((2 * rows_dev, 256), lambda i, meta: (0, 0)),
            ),
            name="key",
        )(meta, normed, beside, w_keyval)
        kv, wq = lax.optimization_barrier((kv, wq))
        wo = lax.all_gather(jnp.stack([w[width:] for w in wq]), "x", axis=1, tiled=True)
        line = line_of(kv)
        fetched = lax.all_to_all(own_pages, ("x", "zh"), split_axis=0, concat_axis=2, tiled=True)
        pages = fetched.reshape(-1, 256)
        shard, ordered = pl.pallas_call(
            shard_kernel,
            out_shape=[
                jax.ShapeDtypeStruct((1536, 256), jnp.bfloat16),
                jax.ShapeDtypeStruct((1024, 128), jnp.bfloat16),
            ],
            in_specs=[smem] + [vmem] * 5,
            out_specs=[vmem] * 2,
            name="shard",
        )(meta, pages, *line)
        up = shift_y(shard, 1)
        down = shift_y(shard, -1)

    with jax.named_scope("new_cache"):
        ordered, down = lax.optimization_barrier((ordered, down))
        other = swap_core(ordered)
        held = jnp.where(c == zl // 2, ordered, other)
        new_cache = jnp.where(c == 0, held[:, :64], held[:, 64:])

    with jax.named_scope("routing"):
        experts_all = w_router.shape[1]
        top = routes.shape[1]
        base = pl.pallas_call(
            table_kernel,
            out_shape=jax.ShapeDtypeStruct((rows_dev, 128), jnp.float32),
            in_specs=[vmem],
            out_specs=vmem,
            name="table",
        )(routes)

    with jax.named_scope("queries"):
        queries = pl.pallas_call(
            query_kernel,
            out_shape=jax.ShapeDtypeStruct((2 * rows_dev * group_size, 128), jnp.bfloat16),
            in_specs=[vmem] * (2 + group_size),
            out_specs=vmem,
            name="query",
        )(normed, beside, *wq)

    with jax.named_scope("attention"):
        n_pages = pages.shape[0]
        queries, base = lax.optimization_barrier((queries, base))
        state = attention(meta, queries, [shard], [0], (), (), n_pages)
        state, up, down = lax.optimization_barrier((state, up, down))
        far = shift_y(up, 1)
        state = attention(meta, queries, [up, down], [-1, 1], state, (), n_pages)
        partial, leaving = attention(meta, queries, [far], [2], state, [wo], n_pages)

    with jax.named_scope("out_projection"):
        half = width // 2
        received = swap_core(leaving)
        wide = jax.ShapeDtypeStruct((rows_dev, half + 128), jnp.bfloat16)
        mid, send_1, send_2 = pl.pallas_call(
            gate_kernel,
            out_shape=[jax.ShapeDtypeStruct((rows_dev, width), jnp.bfloat16), wide, wide],
            in_specs=[vmem] * 6,
            out_specs=[vmem] * 3,
            compiler_params=pltpu.CompilerParams(vmem_limit_bytes=16 * 2**20),
            name="gate",
        )(hidden_in, partial, received, moe_gain[None], w_router, base)

    with jax.named_scope("routing"):
        step = 1 - 2 * c
        z = lax.axis_index(("zh", "zl"))
        y_goals = jnp.stack([y, y + step, y - step, y + 2]) % Y
        z_goals = jnp.stack([z, z + step, z - step, z + 2 * step]) % ZL
        cores = jnp.stack([c, 1 - c])
        half = width // 2
        spread = experts_all * CAP

        def keys_of(first):
            inner = jnp.arange(4, dtype=jnp.int32)[:, None] * spread + jnp.arange(CAP, dtype=jnp.int32)
            return (first[:, :, None, None] * CAP + inner[None, None]).reshape(1, -1)

        keys_1 = keys_of(y_goals[:, None] * 8 + (z % ZL) * 2 + cores[None, :])
        keys_2 = keys_of(y * 8 + z_goals[:, None] * 2 + cores[None, :])

    def to_y(a, s):
        return shift_y(a, s)

    def to_z(a, s):
        return shift_z(a, s)

    block = 2 * 4 * CAP

    with jax.named_scope("dispatch"):
        near_1 = jnp.concatenate(spread_out(send_1, to_z), axis=0)
        near_2 = jnp.concatenate(spread_out(send_2, to_y), axis=0)

        def named_of(near):
            ids = near[:, half : half + top].astype(jnp.int32)
            slots = near[:, half + top : half + 2 * top].astype(jnp.int32)
            source = lax.broadcasted_iota(jnp.int32, ids.shape, 0) // rows_dev
            return ids * CAP + slots + source * spread

        def placed_of(keys, named):
            return sum((named[:, k : k + 1] == keys) for k in range(top)).astype(jnp.bfloat16)

        named_1, named_2 = named_of(near_1), named_of(near_2)
        placed_1, placed_2 = placed_of(keys_1, named_1), placed_of(keys_2, named_2)

        def pack(placed, near, send):
            out = []
            for d, s in enumerate((0, 1, -1, 2)):
                packed = lax.dot_general(
                    placed[:, d * block : (d + 1) * block],
                    near[:, :half],
                    (((0,), (0,)), ((), ())),
                    preferred_element_type=jnp.float32,
                ).astype(jnp.bfloat16)
                out.append((send(packed, s) if s else packed).reshape(2, 4, CAP, half))
            return out

        held_1 = pack(placed_1, near_1, to_y)
        held_2 = pack(placed_2, near_2, to_z)

        def joined(core):
            return jnp.concatenate(
                [
                    jnp.stack([a[core] for a in held_1], axis=0),
                    jnp.stack([a[core] for a in held_2], axis=1),
                ],
                axis=-1,
            ).reshape(16 * CAP, width)

        passed = swap_core(joined(1))
        kept = joined(0)

    with jax.named_scope("mix"):

        def mix_of(keys, named, near):
            def weighted(first):
                return sum(
                    jnp.where(
                        named[:, k : k + 1] == keys,
                        near[:, half + first + k : half + first + k + 1].astype(jnp.float32),
                        0.0,
                    )
                    for k in range(top)
                ).astype(jnp.bfloat16)

            return jnp.concatenate([weighted(2 * top), weighted(3 * top)], axis=0)

        mix_1 = mix_of(keys_1, named_1, near_1)
        mix_2 = mix_of(keys_2, named_2, near_2)

    with jax.named_scope("experts"):
        inner_dim = expert_out.shape[1]

        def expert(rows):
            inner = jnp.dot(rows, expert_in[0], preferred_element_type=jnp.float32)
            active = (jnp.maximum(inner[:, :inner_dim], 0.0) * inner[:, inner_dim:]).astype(
                jnp.bfloat16
            )
            return jnp.dot(active, expert_out[0], preferred_element_type=jnp.float32).astype(
                jnp.bfloat16
            )

        shape = (4, 4, CAP, width)
        passed_back = swap_core(expert(passed)).reshape(shape)
        kept_back = expert(kept).reshape(shape)

    with jax.named_scope("combine"):

        def give_back(parts, send):
            out = []
            for d, s in enumerate((0, -1, 1, -2)):
                out.append(send(parts[d], s) if s else parts[d])
            return out

        parts_1 = [
            jnp.stack([kept_back[i, :, :, :half], passed_back[i, :, :, :half]]).reshape(block, half)
            for i in range(4)
        ]
        parts_2 = [
            jnp.stack([kept_back[:, j, :, half:], passed_back[:, j, :, half:]]).reshape(block, half)
            for j in range(4)
        ]

        def summed(mix, parts, send, back):
            rows = jnp.concatenate(give_back(parts, send), axis=0)
            both_sums = jnp.dot(mix, rows, preferred_element_type=jnp.float32)
            sums = both_sums[: 4 * rows_dev] + both_sums[4 * rows_dev :]
            mine = sums[:rows_dev]
            away = [
                sums[d * rows_dev : (d + 1) * rows_dev].astype(jnp.bfloat16) for d in range(4)
            ]
            return [mine] + give_back(away, back)[1:]

        total_1 = summed(mix_1, parts_1, to_y, to_z)
        total_2 = summed(mix_2, parts_2, to_z, to_y)
        mixed = jnp.concatenate(
            [sum(a.astype(jnp.float32) for a in t) for t in (total_1, total_2)], axis=1
        )
        hidden_out = (mid.astype(jnp.float32) + mixed).astype(jnp.bfloat16)
    return (hidden_out, new_cache)


def solution(mesh):
    axes = ("x", "zh", "y", "zl", "c")
    split = Mesh(mesh.devices.reshape(X, ZH, Y, ZL, C), axes)
    placed = (
        P(axes, None),
        P(axes, None),
        P(),
        P(None, None, ("x", "zh", "y"), None),
        P(),
        P(None, ("zl", "c")),
        P(),
        P(("zl", "c"), None),
        P(),
        P(),
        P(("y", "zl", "c"), None, None),
        P(("y", "zl", "c"), None, None),
    )
    return jax.shard_map(
        body,
        mesh=split,
        in_specs=placed,
        out_specs=(P(axes, None), P(("x", "zh", "y"), ("zl", "c"))),
        check_vma=False,
    )
```

```python
import jax
import jax.numpy as jnp
from jax import lax
from jax.experimental import pallas as pl
from jax.experimental.pallas import tpu as pltpu
from jax.sharding import Mesh
from jax.sharding import PartitionSpec as P

CAP = 24
epsilon = 1e-06
masked_score = -1e30
log2e = 1.4426950408889634

X, ZH, Y, ZL, C = 4, 2, 4, 4, 2


def rms_scale(rows, gain):
    values = rows.astype(jnp.float32)
    inverse = lax.rsqrt(jnp.mean(values * values, axis=-1, keepdims=True) + epsilon)
    return (values * inverse * gain).astype(jnp.bfloat16)


def swap_core(a):
    return lax.ppermute(a, "c", [(0, 1), (1, 0)])


def shift_line(a, s):
    return lax.ppermute(a, "zl", [(i, (i + s) % ZL) for i in range(ZL)])


def shift_y(a, s):
    pairs = []
    for y in range(Y):
        for c in range(C):
            t = (y + (s if c == 0 else -s)) % Y
            pairs.append((y * C + c, t * C + c))
    return lax.ppermute(a, ("y", "c"), pairs)


def shift_z(a, s):
    pairs = []
    n = ZH * ZL
    for z in range(n):
        for c in range(C):
            t = (z + (s if c == 0 else -s)) % n
            pairs.append((z * C + c, t * C + c))
    return lax.ppermute(a, ("zh", "zl", "c"), pairs)


def spread_out(a, send):
    return [a, send(a, 1), send(a, -1), send(a, 2)]


def attention_kernel(meta, q_ref, *refs, sources, first, last, pages, heads):
    refs = list(refs)
    shards = [refs.pop(0) for _ in sources]
    before = None if first else (refs.pop(0), refs.pop(0))
    projections = [refs.pop(0) for _ in range(heads)] if last else None
    outs = [refs.pop(0), refs.pop(0)]
    keys_ref, values_ref, m_ref, sum_ref = refs
    span = keys_ref.shape[0]
    rows = q_ref.shape[0] // heads
    scale = log2e / float(128) ** 0.5
    y, zl, c, length = meta[0], meta[1], meta[2], meta[3]
    if first:
        m_ref[...] = jnp.full(m_ref.shape, masked_score, jnp.float32)
        sum_ref[...] = jnp.zeros(sum_ref.shape, jnp.float32)
    else:
        m_ref[...] = before[0][...]
        sum_ref[...] = before[1][...]
    values_ref[:, 128:] = jnp.ones((span, 128), jnp.bfloat16)

    def half_of(index):
        return ((index % 256) // 128) * (1 - 2 * c) + c

    key = lax.broadcasted_iota(jnp.int32, (1, span), 1)
    fresh = key - pages

    def fold(index, _):
        away = 0
        for i, ref in enumerate(shards):
            away = jnp.where(index == i, sources[i], away)

            @pl.when(index == i)
            def _(ref=ref):
                keys_ref[...] = ref[:, :128]
                values_ref[:, :128] = ref[:, 128:]

        source = lax.rem(y + away * (1 - 2 * c) + 4, 4)
        position = (key // 64 * 4 + source) * 64 + key % 64
        if first:
            place = ((zl - fresh // 256 + 4) % 4) * 256 + half_of(fresh) * 128 + fresh % 128
            bound = jnp.where(key < pages, jnp.where(position < length, -1, 2**20), place)
            row = lax.broadcasted_iota(jnp.int32, (rows, 1), 0)
            row_place = zl * 256 + half_of(row) * 128 + row % 128
            visible = bound <= row_place
        else:
            visible = jnp.where(key < pages, position, source) < jnp.where(key < pages, length, y)
        for h in range(heads):
            part = pl.ds(h * rows, rows)
            scores = lax.dot_general(
                q_ref[part, :],
                keys_ref[...],
                (((1,), (1,)), ((), ())),
                preferred_element_type=jnp.float32,
            )
            scores = jnp.where(visible, scores, masked_score)
            old = m_ref[part, :]
            new = jnp.maximum(old, jnp.max(scores, axis=1, keepdims=True))
            m_ref[part, :] = new
            weights = jnp.exp2(scores * scale - new[:, :1] * scale)
            factor = jnp.exp2((old - new) * scale)
            sum_ref[part, :] = sum_ref[part, :] * jnp.concatenate([factor, factor], axis=1) + jnp.dot(
                weights.astype(jnp.bfloat16), values_ref[...], preferred_element_type=jnp.float32
            )
        return 0

    lax.fori_loop(0, len(shards), fold, 0)
    if last:
        done = (sum_ref[:, :128] / sum_ref[:, 128:]).astype(jnp.bfloat16)
        for out, first_row in ((outs[0], 0), (outs[1], rows // 2)):
            out[...] = sum(
                jnp.dot(
                    done[h * rows + first_row : h * rows + first_row + rows // 2],
                    projections[h][...],
                    preferred_element_type=jnp.float32,
                )
                for h in range(heads)
            )
    else:
        outs[0][...] = m_ref[...]
        outs[1][...] = sum_ref[...]


def attention(meta, queries, shards, sources, state, projections, pages):
    heads = 4
    n, span = queries.shape[0], shards[0].shape[0]
    vmem = pl.BlockSpec(memory_space=pltpu.VMEM)
    last = bool(projections)
    kinds = (
        [jax.ShapeDtypeStruct((n // heads // 2, projections[0].shape[1]), jnp.float32)] * 2
        if last
        else [
            jax.ShapeDtypeStruct((n, 128), jnp.float32),
            jax.ShapeDtypeStruct((n, 256), jnp.float32),
        ]
    )
    return pl.pallas_call(
        lambda *refs: attention_kernel(
            *refs, sources=sources, first=not state, last=last, pages=pages, heads=heads
        ),
        out_shape=kinds,
        in_specs=[pl.BlockSpec(memory_space=pltpu.SMEM)]
        + [vmem] * (1 + len(shards) + len(state) + len(projections)),
        out_specs=[vmem] * len(kinds),
        scratch_shapes=[
            pltpu.VMEM((span, 128), jnp.bfloat16),
            pltpu.VMEM((span, 256), jnp.bfloat16),
            pltpu.VMEM((n, 128), jnp.float32),
            pltpu.VMEM((n, 256), jnp.float32),
        ],
        compiler_params=pltpu.CompilerParams(vmem_limit_bytes=40 * 2**20),
        cost_estimate=pl.CostEstimate(
            flops=6 * n * span * 128 * len(shards),
            bytes_accessed=4 * 2**20,
            transcendentals=n * span * len(shards),
        ),
        name="attention",
    )(meta, queries, *shards, *state, *projections)


def gate_kernel(
    hidden_ref, partial_ref, received_ref, gain_ref, router_ref, base_ref, mid_ref, a_ref, b_ref
):
    half = hidden_ref.shape[1] // 2
    rows, top = hidden_ref.shape[0], 4
    total = hidden_ref[...].astype(jnp.float32) + (partial_ref[...] + received_ref[...])
    mid = total.astype(jnp.bfloat16)
    mid_ref[...] = mid
    values = mid.astype(jnp.float32)
    inverse = lax.rsqrt(jnp.mean(values * values, axis=-1, keepdims=True) + epsilon)
    normed = (values * inverse * gain_ref[...]).astype(jnp.bfloat16)
    logits = jnp.dot(normed, router_ref[...], preferred_element_type=jnp.float32)
    expert = lax.broadcasted_iota(jnp.int32, logits.shape, 1).astype(jnp.float32)
    raised = [
        jnp.exp(
            jnp.sum(
                jnp.where(base_ref[:, k : k + 1] == expert, logits, 0.0), axis=1, keepdims=True
            )
        )
        for k in range(top)
    ]
    whole = sum(raised[1:], raised[0])
    lane = lax.broadcasted_iota(jnp.int32, (rows, 128), 1)
    table = base_ref[...]
    for k in range(top):
        gate = raised[k] / whole
        high = gate.astype(jnp.bfloat16).astype(jnp.float32)
        table = jnp.where(lane == 2 * top + k, high, table)
        table = jnp.where(lane == 3 * top + k, gate - high, table)
    table = table.astype(jnp.bfloat16)
    a_ref[:, :half] = normed[:, :half]
    a_ref[:, half:] = table
    b_ref[:, :half] = normed[:, half:]
    b_ref[:, half:] = table


def table_kernel(routes_ref, o_ref):
    rows, top = routes_ref.shape
    expert = lax.broadcasted_iota(jnp.int32, (rows, 32), 1)
    named = [(routes_ref[:, k : k + 1] == expert).astype(jnp.float32) for k in range(top)]
    later = lax.broadcasted_iota(jnp.int32, (rows, rows), 0)
    earlier = lax.broadcasted_iota(jnp.int32, (rows, rows), 1)
    before = jnp.dot(
        (later > earlier).astype(jnp.float32),
        sum(named[1:], named[0]),
        preferred_element_type=jnp.float32,
    )
    lane = lax.broadcasted_iota(jnp.int32, (rows, 128), 1)
    table = jnp.zeros((rows, 128), jnp.float32)
    for k in range(top):
        slot = jnp.sum(named[k] * before, axis=1, keepdims=True)
        table = jnp.where(lane == k, routes_ref[:, k : k + 1].astype(jnp.float32), table)
        table = jnp.where(lane == top + k, slot, table)
    o_ref[...] = table


def key_kernel(meta, own_ref, other_ref, w_ref, o_ref):
    half = own_ref.shape[0]
    for i, ref in enumerate((own_ref, other_ref)):
        o_ref[i * half : (i + 1) * half, :] = jnp.dot(
            ref[...], w_ref[0], preferred_element_type=jnp.float32
        ).astype(jnp.bfloat16)


def query_kernel(own_ref, other_ref, *refs):
    half = own_ref.shape[0]
    for h, w_ref in enumerate(refs[:-1]):
        for i, ref in enumerate((own_ref, other_ref)):
            start = (2 * h + i) * half
            refs[-1][start : start + half, :] = jnp.dot(
                ref[...], w_ref[...], preferred_element_type=jnp.float32
            ).astype(jnp.bfloat16)


def shard_kernel(meta, pages_ref, *refs):
    line, shard_ref, ordered_ref = refs[:ZL], refs[ZL], refs[ZL + 1]
    zl, c = meta[1], meta[2]
    pages = pages_ref.shape[0]
    shard_ref[:pages, :] = pages_ref[...]
    for i, ref in enumerate(line):
        shard_ref[pages + i * 256 : pages + (i + 1) * 256, :] = ref[...]
    col = pl.multiple_of(lax.rem(zl, 2) * 128, 128)
    for z in range(ZL):
        slot = lax.rem(zl - z + 4, 4)
        for half in range(2):
            inner = half * (1 - 2 * c) + c
            start = pl.multiple_of(pages + slot * 256 + inner * 128, 128)
            ordered_ref[z * 256 + half * 128 : z * 256 + half * 128 + 128, :] = shard_ref[
                pl.ds(start, 128), pl.ds(col, 128)
            ]


def body(
    hidden_in,
    routes,
    prefix_len,
    cache,
    attn_gain,
    w_query,
    w_keyval,
    w_out,
    moe_gain,
    w_router,
    expert_in,
    expert_out,
):
    y, zl, c = lax.axis_index("y"), lax.axis_index("zl"), lax.axis_index("c")
    rep = lax.axis_index(("x", "zh"))
    rows_dev, width = hidden_in.shape
    length = lax.dynamic_index_in_dim(prefix_len, rep, 0, keepdims=False)
    meta = jnp.stack([y, zl, c, length]).astype(jnp.int32)
    smem = pl.BlockSpec(memory_space=pltpu.SMEM)
    vmem = pl.BlockSpec(memory_space=pltpu.VMEM)

    group_size = 4
    to_group = []
    for z in range(ZH * ZL):
        for k in range(C):
            t = (z + k * (2 * (z % 2) - 1)) % (ZH * ZL)
            to_group.append((z * C + k, t * C + (z % ZL) // 2))

    def line_of(a):
        return [a] + [shift_line(a, s) for s in (1, 2, 3)]

    with jax.named_scope("weights"):
        wq_here = lax.ppermute(w_query, ("zh", "zl", "c"), to_group)
        wo_here = lax.ppermute(w_out, ("zh", "zl", "c"), to_group)

    with jax.named_scope("keys"):
        normed = rms_scale(hidden_in, attn_gain)
        own_pages = lax.dynamic_index_in_dim(cache, c, 1, keepdims=True)
        normed, own_pages = lax.optimization_barrier((normed, own_pages))
        beside = swap_core(normed)
        whole = pl.BlockSpec((rows_dev, width), lambda i, meta: (0, 0))
        kv = pl.pallas_call(
            key_kernel,
            out_shape=jax.ShapeDtypeStruct((2 * rows_dev, 256), jnp.bfloat16),
            grid_spec=pltpu.PrefetchScalarGridSpec(
                num_scalar_prefetch=1,
                grid=(1,),
                in_specs=[whole, whole, pl.BlockSpec((1, width, 256), lambda i, meta: (meta[2], 0, 0))],
                out_specs=pl.BlockSpec((2 * rows_dev, 256), lambda i, meta: (0, 0)),
            ),
            name="key",
        )(meta, normed, beside, w_keyval)
        line = line_of(kv)
        line, wq_here, wo_here = lax.optimization_barrier((line, wq_here, wo_here))
        fetched = lax.all_to_all(own_pages, ("x", "zh"), split_axis=0, concat_axis=2, tiled=True)
        pages = fetched.reshape(-1, 256)
        shard, ordered = pl.pallas_call(
            shard_kernel,
            out_shape=[
                jax.ShapeDtypeStruct((1536, 256), jnp.bfloat16),
                jax.ShapeDtypeStruct((1024, 128), jnp.bfloat16),
            ],
            in_specs=[smem] + [vmem] * 5,
            out_specs=[vmem] * 2,
            name="shard",
        )(meta, pages, *line)
        up = shift_y(shard, 1)
        down = shift_y(shard, -1)

    with jax.named_scope("new_cache"):
        ordered, down = lax.optimization_barrier((ordered, down))
        other = swap_core(ordered)
        held = jnp.where(c == zl // 2, ordered, other)
        new_cache = jnp.where(c == 0, held[:, :64], held[:, 64:])

    with jax.named_scope("routing"):
        experts_all = w_router.shape[1]
        top = routes.shape[1]
        base = pl.pallas_call(
            table_kernel,
            out_shape=jax.ShapeDtypeStruct((rows_dev, 128), jnp.float32),
            in_specs=[vmem],
            out_specs=vmem,
            name="table",
        )(routes)

    with jax.named_scope("weights"):
        wq = spread_out(wq_here, shift_z)
        wq, wo_here = lax.optimization_barrier((wq, wo_here))
        wo = spread_out(wo_here, shift_z)
        wq, up, base = lax.optimization_barrier((wq, up, base))
        far = shift_y(up, 1)

    with jax.named_scope("queries"):
        queries = pl.pallas_call(
            query_kernel,
            out_shape=jax.ShapeDtypeStruct((2 * rows_dev * group_size, 128), jnp.bfloat16),
            in_specs=[vmem] * (2 + group_size),
            out_specs=vmem,
            name="query",
        )(normed, beside, *wq)

    with jax.named_scope("attention"):
        n_pages = pages.shape[0]
        state = attention(meta, queries, [shard], [0], (), (), n_pages)
        state = attention(meta, queries, [up, down], [-1, 1], state, (), n_pages)
        partial, leaving = attention(meta, queries, [far], [2], state, wo, n_pages)

    with jax.named_scope("out_projection"):
        half = width // 2
        received = swap_core(leaving)
        wide = jax.ShapeDtypeStruct((rows_dev, half + 128), jnp.bfloat16)
        mid, send_1, send_2 = pl.pallas_call(
            gate_kernel,
            out_shape=[jax.ShapeDtypeStruct((rows_dev, width), jnp.bfloat16), wide, wide],
            in_specs=[vmem] * 6,
            out_specs=[vmem] * 3,
            compiler_params=pltpu.CompilerParams(vmem_limit_bytes=16 * 2**20),
            name="gate",
        )(hidden_in, partial, received, moe_gain[None], w_router, base)

    with jax.named_scope("routing"):
        step = 1 - 2 * c
        z = lax.axis_index(("zh", "zl"))
        y_goals = jnp.stack([y, y + step, y - step, y + 2]) % Y
        z_goals = jnp.stack([z, z + step, z - step, z + 2 * step]) % ZL
        cores = jnp.stack([c, 1 - c])
        half = width // 2
        spread = experts_all * CAP

        def keys_of(first):
            inner = jnp.arange(4, dtype=jnp.int32)[:, None] * spread + jnp.arange(CAP, dtype=jnp.int32)
            return (first[:, :, None, None] * CAP + inner[None, None]).reshape(1, -1)

        keys_1 = keys_of(y_goals[:, None] * 8 + (z % ZL) * 2 + cores[None, :])
        keys_2 = keys_of(y * 8 + z_goals[:, None] * 2 + cores[None, :])

    def to_y(a, s):
        return shift_y(a, s)

    def to_z(a, s):
        return shift_z(a, s)

    block = 2 * 4 * CAP

    with jax.named_scope("dispatch"):
        near_1 = jnp.concatenate(spread_out(send_1, to_z), axis=0)
        near_2 = jnp.concatenate(spread_out(send_2, to_y), axis=0)

        def named_of(near):
            ids = near[:, half : half + top].astype(jnp.int32)
            slots = near[:, half + top : half + 2 * top].astype(jnp.int32)
            source = lax.broadcasted_iota(jnp.int32, ids.shape, 0) // rows_dev
            return ids * CAP + slots + source * spread

        def placed_of(keys, named):
            return sum((named[:, k : k + 1] == keys) for k in range(top)).astype(jnp.bfloat16)

        named_1, named_2 = named_of(near_1), named_of(near_2)
        placed_1, placed_2 = placed_of(keys_1, named_1), placed_of(keys_2, named_2)

        def pack(placed, near, send):
            out = []
            for d, s in enumerate((0, 1, -1, 2)):
                packed = lax.dot_general(
                    placed[:, d * block : (d + 1) * block],
                    near[:, :half],
                    (((0,), (0,)), ((), ())),
                    preferred_element_type=jnp.float32,
                ).astype(jnp.bfloat16)
                out.append((send(packed, s) if s else packed).reshape(2, 4, CAP, half))
            return out

        held_1 = pack(placed_1, near_1, to_y)
        held_2 = pack(placed_2, near_2, to_z)

        def joined(core):
            return jnp.concatenate(
                [
                    jnp.stack([a[core] for a in held_1], axis=0),
                    jnp.stack([a[core] for a in held_2], axis=1),
                ],
                axis=-1,
            ).reshape(16 * CAP, width)

        passed = swap_core(joined(1))
        kept = joined(0)

    with jax.named_scope("experts"):
        inner_dim = expert_out.shape[1]

        def expert(rows):
            inner = jnp.dot(rows, expert_in[0], preferred_element_type=jnp.float32)
            active = (jnp.maximum(inner[:, :inner_dim], 0.0) * inner[:, inner_dim:]).astype(
                jnp.bfloat16
            )
            return jnp.dot(active, expert_out[0], preferred_element_type=jnp.float32).astype(
                jnp.bfloat16
            )

        shape = (4, 4, CAP, width)
        passed_back = swap_core(expert(passed)).reshape(shape)
        kept_back, near_1, near_2 = lax.optimization_barrier((expert(kept), near_1, near_2))
        kept_back = kept_back.reshape(shape)
        named_1, named_2 = named_of(near_1), named_of(near_2)

    with jax.named_scope("mix"):

        def mix_of(keys, named, near):
            def weighted(first):
                return sum(
                    jnp.where(
                        named[:, k : k + 1] == keys,
                        near[:, half + first + k : half + first + k + 1].astype(jnp.float32),
                        0.0,
                    )
                    for k in range(top)
                ).astype(jnp.bfloat16)

            return jnp.concatenate([weighted(2 * top), weighted(3 * top)], axis=0)

        mix_1 = mix_of(keys_1, named_1, near_1)
        mix_2 = mix_of(keys_2, named_2, near_2)

    with jax.named_scope("combine"):

        def give_back(parts, send):
            out = []
            for d, s in enumerate((0, -1, 1, -2)):
                out.append(send(parts[d], s) if s else parts[d])
            return out

        parts_1 = [
            jnp.stack([kept_back[i, :, :, :half], passed_back[i, :, :, :half]]).reshape(block, half)
            for i in range(4)
        ]
        parts_2 = [
            jnp.stack([kept_back[:, j, :, half:], passed_back[:, j, :, half:]]).reshape(block, half)
            for j in range(4)
        ]

        def summed(mix, parts, send, back):
            rows = jnp.concatenate(give_back(parts, send), axis=0)
            both_sums = jnp.dot(mix, rows, preferred_element_type=jnp.float32)
            sums = both_sums[: 4 * rows_dev] + both_sums[4 * rows_dev :]
            mine = sums[:rows_dev]
            away = [
                sums[d * rows_dev : (d + 1) * rows_dev].astype(jnp.bfloat16) for d in range(4)
            ]
            return [mine] + give_back(away, back)[1:]

        total_1 = summed(mix_1, parts_1, to_y, to_z)
        total_2 = summed(mix_2, parts_2, to_z, to_y)
        mixed = jnp.concatenate(
            [sum(a.astype(jnp.float32) for a in t) for t in (total_1, total_2)], axis=1
        )
        hidden_out = (mid.astype(jnp.float32) + mixed).astype(jnp.bfloat16)
    return (hidden_out, new_cache)


def solution(mesh):
    axes = ("x", "zh", "y", "zl", "c")
    split = Mesh(mesh.devices.reshape(X, ZH, Y, ZL, C), axes)
    placed = (
        P(axes, None),
        P(axes, None),
        P(),
        P(None, None, ("x", "zh", "y"), None),
        P(),
        P(None, ("zl", "c")),
        P(),
        P(("zl", "c"), None),
        P(),
        P(),
        P(("y", "zl", "c"), None, None),
        P(("y", "zl", "c"), None, None),
    )
    return jax.shard_map(
        body,
        mesh=split,
        in_specs=placed,
        out_specs=(P(axes, None), P(("x", "zh", "y"), ("zl", "c"))),
        check_vma=False,
    )
```

```python
import jax
import jax.numpy as jnp
from jax import lax
from jax.experimental import pallas as pl
from jax.experimental.pallas import tpu as pltpu
from jax.sharding import Mesh
from jax.sharding import PartitionSpec as P

CAP = 24
epsilon = 1e-06
masked_score = -1e30
log2e = 1.4426950408889634

X, ZH, Y, ZL, C = 4, 2, 4, 4, 2


def rms_scale(rows, gain):
    values = rows.astype(jnp.float32)
    inverse = lax.rsqrt(jnp.mean(values * values, axis=-1, keepdims=True) + epsilon)
    return (values * inverse * gain).astype(jnp.bfloat16)


def swap_core(a):
    return lax.ppermute(a, "c", [(0, 1), (1, 0)])


def shift_line(a, s):
    return lax.ppermute(a, "zl", [(i, (i + s) % ZL) for i in range(ZL)])


def shift_y(a, s):
    pairs = []
    for y in range(Y):
        for c in range(C):
            t = (y + (s if c == 0 else -s)) % Y
            pairs.append((y * C + c, t * C + c))
    return lax.ppermute(a, ("y", "c"), pairs)


def shift_z(a, s):
    pairs = []
    n = ZH * ZL
    for z in range(n):
        for c in range(C):
            t = (z + (s if c == 0 else -s)) % n
            pairs.append((z * C + c, t * C + c))
    return lax.ppermute(a, ("zh", "zl", "c"), pairs)


def spread_out(a, send):
    return [a, send(a, 1), send(a, -1), send(a, 2)]


def attention_kernel(meta, q_ref, *refs, sources, first, last, pages, heads):
    refs = list(refs)
    shards = [refs.pop(0) for _ in sources]
    before = None if first else (refs.pop(0), refs.pop(0))
    projections = [refs.pop(0) for _ in range(heads)] if last else None
    outs = [refs.pop(0), refs.pop(0)]
    keys_ref, values_ref, m_ref, sum_ref = refs
    span = keys_ref.shape[0]
    rows = q_ref.shape[0] // heads
    scale = log2e / float(128) ** 0.5
    y, zl, c, length = meta[0], meta[1], meta[2], meta[3]
    if first:
        m_ref[...] = jnp.full(m_ref.shape, masked_score, jnp.float32)
        sum_ref[...] = jnp.zeros(sum_ref.shape, jnp.float32)
    else:
        m_ref[...] = before[0][...]
        sum_ref[...] = before[1][...]
    values_ref[:, 128:] = jnp.ones((span, 128), jnp.bfloat16)

    def half_of(index):
        return ((index % 256) // 128) * (1 - 2 * c) + c

    key = lax.broadcasted_iota(jnp.int32, (1, span), 1)
    fresh = key - pages

    def fold(index, _):
        away = 0
        for i, ref in enumerate(shards):
            away = jnp.where(index == i, sources[i], away)

            @pl.when(index == i)
            def _(ref=ref):
                keys_ref[...] = ref[:, :128]
                values_ref[:, :128] = ref[:, 128:]

        source = lax.rem(y + away * (1 - 2 * c) + 4, 4)
        position = (key // 64 * 4 + source) * 64 + key % 64
        if first:
            place = ((zl - fresh // 256 + 4) % 4) * 256 + half_of(fresh) * 128 + fresh % 128
            bound = jnp.where(key < pages, jnp.where(position < length, -1, 2**20), place)
            row = lax.broadcasted_iota(jnp.int32, (rows, 1), 0)
            row_place = zl * 256 + half_of(row) * 128 + row % 128
            visible = bound <= row_place
        else:
            visible = jnp.where(key < pages, position, source) < jnp.where(key < pages, length, y)
        for h in range(heads):
            part = pl.ds(h * rows, rows)
            scores = lax.dot_general(
                q_ref[part, :],
                keys_ref[...],
                (((1,), (1,)), ((), ())),
                preferred_element_type=jnp.float32,
            )
            scores = jnp.where(visible, scores, masked_score)
            old = m_ref[part, :]
            new = jnp.maximum(old, jnp.max(scores, axis=1, keepdims=True))
            m_ref[part, :] = new
            weights = jnp.exp2(scores * scale - new[:, :1] * scale)
            factor = jnp.exp2((old - new) * scale)
            sum_ref[part, :] = sum_ref[part, :] * jnp.concatenate([factor, factor], axis=1) + jnp.dot(
                weights.astype(jnp.bfloat16), values_ref[...], preferred_element_type=jnp.float32
            )
        return 0

    lax.fori_loop(0, len(shards), fold, 0)
    if last:
        done = (sum_ref[:, :128] / sum_ref[:, 128:]).astype(jnp.bfloat16)
        for out, first_row in ((outs[0], 0), (outs[1], rows // 2)):
            out[...] = sum(
                jnp.dot(
                    done[h * rows + first_row : h * rows + first_row + rows // 2],
                    projections[h][...],
                    preferred_element_type=jnp.float32,
                )
                for h in range(heads)
            )
    else:
        outs[0][...] = m_ref[...]
        outs[1][...] = sum_ref[...]


def attention(meta, queries, shards, sources, state, projections, pages):
    heads = 4
    n, span = queries.shape[0], shards[0].shape[0]
    vmem = pl.BlockSpec(memory_space=pltpu.VMEM)
    last = bool(projections)
    kinds = (
        [jax.ShapeDtypeStruct((n // heads // 2, projections[0].shape[1]), jnp.float32)] * 2
        if last
        else [
            jax.ShapeDtypeStruct((n, 128), jnp.float32),
            jax.ShapeDtypeStruct((n, 256), jnp.float32),
        ]
    )
    return pl.pallas_call(
        lambda *refs: attention_kernel(
            *refs, sources=sources, first=not state, last=last, pages=pages, heads=heads
        ),
        out_shape=kinds,
        in_specs=[pl.BlockSpec(memory_space=pltpu.SMEM)]
        + [vmem] * (1 + len(shards) + len(state) + len(projections)),
        out_specs=[vmem] * len(kinds),
        scratch_shapes=[
            pltpu.VMEM((span, 128), jnp.bfloat16),
            pltpu.VMEM((span, 256), jnp.bfloat16),
            pltpu.VMEM((n, 128), jnp.float32),
            pltpu.VMEM((n, 256), jnp.float32),
        ],
        compiler_params=pltpu.CompilerParams(vmem_limit_bytes=40 * 2**20),
        cost_estimate=pl.CostEstimate(
            flops=6 * n * span * 128 * len(shards),
            bytes_accessed=4 * 2**20,
            transcendentals=n * span * len(shards),
        ),
        name="attention",
    )(meta, queries, *shards, *state, *projections)


def gate_kernel(
    hidden_ref, partial_ref, received_ref, gain_ref, router_ref, base_ref, mid_ref, a_ref, b_ref
):
    half = hidden_ref.shape[1] // 2
    rows, top = hidden_ref.shape[0], 4
    total = hidden_ref[...].astype(jnp.float32) + (partial_ref[...] + received_ref[...])
    mid = total.astype(jnp.bfloat16)
    mid_ref[...] = mid
    values = mid.astype(jnp.float32)
    inverse = lax.rsqrt(jnp.mean(values * values, axis=-1, keepdims=True) + epsilon)
    normed = (values * inverse * gain_ref[...]).astype(jnp.bfloat16)
    logits = jnp.dot(normed, router_ref[...], preferred_element_type=jnp.float32)
    expert = lax.broadcasted_iota(jnp.int32, logits.shape, 1).astype(jnp.float32)
    raised = [
        jnp.exp(
            jnp.sum(
                jnp.where(base_ref[:, k : k + 1] == expert, logits, 0.0), axis=1, keepdims=True
            )
        )
        for k in range(top)
    ]
    whole = sum(raised[1:], raised[0])
    lane = lax.broadcasted_iota(jnp.int32, (rows, 128), 1)
    table = base_ref[...]
    for k in range(top):
        gate = raised[k] / whole
        high = gate.astype(jnp.bfloat16).astype(jnp.float32)
        table = jnp.where(lane == 2 * top + k, high, table)
        table = jnp.where(lane == 3 * top + k, gate - high, table)
    table = table.astype(jnp.bfloat16)
    a_ref[:, :half] = normed[:, :half]
    a_ref[:, half:] = table
    b_ref[:, :half] = normed[:, half:]
    b_ref[:, half:] = table


def table_kernel(routes_ref, o_ref):
    rows, top = routes_ref.shape
    expert = lax.broadcasted_iota(jnp.int32, (rows, 32), 1)
    named = [(routes_ref[:, k : k + 1] == expert).astype(jnp.float32) for k in range(top)]
    later = lax.broadcasted_iota(jnp.int32, (rows, rows), 0)
    earlier = lax.broadcasted_iota(jnp.int32, (rows, rows), 1)
    before = jnp.dot(
        (later > earlier).astype(jnp.float32),
        sum(named[1:], named[0]),
        preferred_element_type=jnp.float32,
    )
    lane = lax.broadcasted_iota(jnp.int32, (rows, 128), 1)
    table = jnp.zeros((rows, 128), jnp.float32)
    for k in range(top):
        slot = jnp.sum(named[k] * before, axis=1, keepdims=True)
        table = jnp.where(lane == k, routes_ref[:, k : k + 1].astype(jnp.float32), table)
        table = jnp.where(lane == top + k, slot, table)
    o_ref[...] = table


def key_kernel(meta, own_ref, other_ref, w_ref, o_ref):
    half = own_ref.shape[0]
    for i, ref in enumerate((own_ref, other_ref)):
        o_ref[i * half : (i + 1) * half, :] = jnp.dot(
            ref[...], w_ref[0], preferred_element_type=jnp.float32
        ).astype(jnp.bfloat16)


def query_kernel(own_ref, other_ref, *refs):
    half = own_ref.shape[0]
    for h, w_ref in enumerate(refs[:-1]):
        for i, ref in enumerate((own_ref, other_ref)):
            start = (2 * h + i) * half
            refs[-1][start : start + half, :] = jnp.dot(
                ref[...], w_ref[...], preferred_element_type=jnp.float32
            ).astype(jnp.bfloat16)


def shard_kernel(meta, pages_ref, *refs):
    line, shard_ref, ordered_ref = refs[:ZL], refs[ZL], refs[ZL + 1]
    zl, c = meta[1], meta[2]
    pages = pages_ref.shape[0]
    shard_ref[:pages, :] = pages_ref[...]
    for i, ref in enumerate(line):
        shard_ref[pages + i * 256 : pages + (i + 1) * 256, :] = ref[...]
    col = pl.multiple_of(lax.rem(zl, 2) * 128, 128)
    for z in range(ZL):
        slot = lax.rem(zl - z + 4, 4)
        for half in range(2):
            inner = half * (1 - 2 * c) + c
            start = pl.multiple_of(pages + slot * 256 + inner * 128, 128)
            ordered_ref[z * 256 + half * 128 : z * 256 + half * 128 + 128, :] = shard_ref[
                pl.ds(start, 128), pl.ds(col, 128)
            ]


def body(
    hidden_in,
    routes,
    prefix_len,
    cache,
    attn_gain,
    w_query,
    w_keyval,
    w_out,
    moe_gain,
    w_router,
    expert_in,
    expert_out,
):
    y, zl, c = lax.axis_index("y"), lax.axis_index("zl"), lax.axis_index("c")
    rep = lax.axis_index(("x", "zh"))
    rows_dev, width = hidden_in.shape
    length = lax.dynamic_index_in_dim(prefix_len, rep, 0, keepdims=False)
    meta = jnp.stack([y, zl, c, length]).astype(jnp.int32)
    smem = pl.BlockSpec(memory_space=pltpu.SMEM)
    vmem = pl.BlockSpec(memory_space=pltpu.VMEM)

    group_size = 4
    to_group = []
    for z in range(ZH * ZL):
        for k in range(C):
            t = (z + k * (2 * (z % 2) - 1)) % (ZH * ZL)
            to_group.append((z * C + k, t * C + (z % ZL) // 2))

    def line_of(a):
        return [a] + [shift_line(a, s) for s in (1, 2, 3)]

    with jax.named_scope("weights"):
        wq_here = lax.ppermute(w_query, ("zh", "zl", "c"), to_group)
        wo_here = lax.ppermute(w_out, ("zh", "zl", "c"), to_group)

    with jax.named_scope("keys"):
        normed = rms_scale(hidden_in, attn_gain)
        own_pages = lax.dynamic_index_in_dim(cache, c, 1, keepdims=True)
        normed, own_pages = lax.optimization_barrier((normed, own_pages))
        beside = swap_core(normed)
        whole = pl.BlockSpec((rows_dev, width), lambda i, meta: (0, 0))
        kv = pl.pallas_call(
            key_kernel,
            out_shape=jax.ShapeDtypeStruct((2 * rows_dev, 256), jnp.bfloat16),
            grid_spec=pltpu.PrefetchScalarGridSpec(
                num_scalar_prefetch=1,
                grid=(1,),
                in_specs=[whole, whole, pl.BlockSpec((1, width, 256), lambda i, meta: (meta[2], 0, 0))],
                out_specs=pl.BlockSpec((2 * rows_dev, 256), lambda i, meta: (0, 0)),
            ),
            name="key",
        )(meta, normed, beside, w_keyval)
        line = line_of(kv)
        line, wq_here, wo_here = lax.optimization_barrier((line, wq_here, wo_here))
        fetched = lax.all_to_all(own_pages, ("x", "zh"), split_axis=0, concat_axis=2, tiled=True)
        pages = fetched.reshape(-1, 256)
        shard, ordered = pl.pallas_call(
            shard_kernel,
            out_shape=[
                jax.ShapeDtypeStruct((1536, 256), jnp.bfloat16),
                jax.ShapeDtypeStruct((1024, 128), jnp.bfloat16),
            ],
            in_specs=[smem] + [vmem] * 5,
            out_specs=[vmem] * 2,
            name="shard",
        )(meta, pages, *line)
        up = shift_y(shard, 1)
        down = shift_y(shard, -1)

    with jax.named_scope("new_cache"):
        ordered, down = lax.optimization_barrier((ordered, down))
        other = swap_core(ordered)
        held = jnp.where(c == zl // 2, ordered, other)
        new_cache = jnp.where(c == 0, held[:, :64], held[:, 64:])

    with jax.named_scope("routing"):
        experts_all = w_router.shape[1]
        top = routes.shape[1]
        base = pl.pallas_call(
            table_kernel,
            out_shape=jax.ShapeDtypeStruct((rows_dev, 128), jnp.float32),
            in_specs=[vmem],
            out_specs=vmem,
            name="table",
        )(routes)

    with jax.named_scope("weights"):
        wq = spread_out(wq_here, shift_z)
        wq, wo_here = lax.optimization_barrier((wq, wo_here))
        wo = spread_out(wo_here, shift_z)
        wq, up, base = lax.optimization_barrier((wq, up, base))
        far = shift_y(up, 1)

    with jax.named_scope("queries"):
        queries = pl.pallas_call(
            query_kernel,
            out_shape=jax.ShapeDtypeStruct((2 * rows_dev * group_size, 128), jnp.bfloat16),
            in_specs=[vmem] * (2 + group_size),
            out_specs=vmem,
            name="query",
        )(normed, beside, *wq)

    with jax.named_scope("attention"):
        n_pages = pages.shape[0]
        state = attention(meta, queries, [shard], [0], (), (), n_pages)
        state = attention(meta, queries, [up, down], [-1, 1], state, (), n_pages)
        partial, leaving = attention(meta, queries, [far], [2], state, wo, n_pages)

    with jax.named_scope("out_projection"):
        half = width // 2
        received = swap_core(leaving)
        wide = jax.ShapeDtypeStruct((rows_dev, half + 128), jnp.bfloat16)
        mid, send_1, send_2 = pl.pallas_call(
            gate_kernel,
            out_shape=[jax.ShapeDtypeStruct((rows_dev, width), jnp.bfloat16), wide, wide],
            in_specs=[vmem] * 6,
            out_specs=[vmem] * 3,
            compiler_params=pltpu.CompilerParams(vmem_limit_bytes=16 * 2**20),
            name="gate",
        )(hidden_in, partial, received, moe_gain[None], w_router, base)

    with jax.named_scope("routing"):
        step = 1 - 2 * c
        z = lax.axis_index(("zh", "zl"))
        y_goals = jnp.stack([y, y + step, y - step, y + 2]) % Y
        z_goals = jnp.stack([z, z + step, z - step, z + 2 * step]) % ZL
        cores = jnp.stack([c, 1 - c])
        half = width // 2
        spread = experts_all * CAP

        def keys_of(first):
            inner = jnp.arange(4, dtype=jnp.int32)[:, None] * spread + jnp.arange(CAP, dtype=jnp.int32)
            return (first[:, :, None, None] * CAP + inner[None, None]).reshape(1, -1)

        keys_1 = keys_of(y_goals[:, None] * 8 + (z % ZL) * 2 + cores[None, :])
        keys_2 = keys_of(y * 8 + z_goals[:, None] * 2 + cores[None, :])

    def to_y(a, s):
        return shift_y(a, s)

    def to_z(a, s):
        return shift_z(a, s)

    block = 2 * 4 * CAP

    with jax.named_scope("dispatch"):
        near_1 = jnp.concatenate(spread_out(send_1, to_z), axis=0)
        near_2 = jnp.concatenate(spread_out(send_2, to_y), axis=0)

        def named_of(near):
            ids = near[:, half : half + top].astype(jnp.int32)
            slots = near[:, half + top : half + 2 * top].astype(jnp.int32)
            source = lax.broadcasted_iota(jnp.int32, ids.shape, 0) // rows_dev
            return ids * CAP + slots + source * spread

        def placed_of(keys, named):
            return sum((named[:, k : k + 1] == keys) for k in range(top)).astype(jnp.bfloat16)

        named_1, named_2 = named_of(near_1), named_of(near_2)
        placed_1, placed_2 = placed_of(keys_1, named_1), placed_of(keys_2, named_2)

        def pack(placed, near, send):
            out = []
            for d, s in enumerate((0, 1, -1, 2)):
                packed = lax.dot_general(
                    placed[:, d * block : (d + 1) * block],
                    near[:, :half],
                    (((0,), (0,)), ((), ())),
                    preferred_element_type=jnp.float32,
                ).astype(jnp.bfloat16)
                out.append((send(packed, s) if s else packed).reshape(2, 4, CAP, half))
            return out

        held_1 = pack(placed_1, near_1, to_y)
        held_2 = pack(placed_2, near_2, to_z)

        def joined(core):
            return jnp.concatenate(
                [
                    jnp.stack([a[core] for a in held_1], axis=0),
                    jnp.stack([a[core] for a in held_2], axis=1),
                ],
                axis=-1,
            ).reshape(16 * CAP, width)

        passed = swap_core(joined(1))
        kept = joined(0)

    with jax.named_scope("experts"):
        inner_dim = expert_out.shape[1]

        def expert(rows):
            inner = jnp.dot(rows, expert_in[0], preferred_element_type=jnp.float32)
            active = (jnp.maximum(inner[:, :inner_dim], 0.0) * inner[:, inner_dim:]).astype(
                jnp.bfloat16
            )
            return jnp.dot(active, expert_out[0], preferred_element_type=jnp.float32).astype(
                jnp.bfloat16
            )

        shape = (4, 4, CAP, width)
        passed_back = swap_core(expert(passed)).reshape(shape)
        kept_back = expert(kept).reshape(shape)
        passed_back, near_1, near_2 = lax.optimization_barrier((passed_back, near_1, near_2))
        named_1, named_2 = named_of(near_1), named_of(near_2)

    with jax.named_scope("mix"):

        def mix_of(keys, named, near):
            def weighted(first):
                return sum(
                    jnp.where(
                        named[:, k : k + 1] == keys,
                        near[:, half + first + k : half + first + k + 1].astype(jnp.float32),
                        0.0,
                    )
                    for k in range(top)
                ).astype(jnp.bfloat16)

            return jnp.concatenate([weighted(2 * top), weighted(3 * top)], axis=0)

        mix_1 = mix_of(keys_1, named_1, near_1)
        mix_2 = mix_of(keys_2, named_2, near_2)

    with jax.named_scope("combine"):

        def give_back(parts, send):
            out = []
            for d, s in enumerate((0, -1, 1, -2)):
                out.append(send(parts[d], s) if s else parts[d])
            return out

        parts_1 = [
            jnp.stack([kept_back[i, :, :, :half], passed_back[i, :, :, :half]]).reshape(block, half)
            for i in range(4)
        ]
        parts_2 = [
            jnp.stack([kept_back[:, j, :, half:], passed_back[:, j, :, half:]]).reshape(block, half)
            for j in range(4)
        ]

        def summed(mix, parts, send, back):
            rows = jnp.concatenate(give_back(parts, send), axis=0)
            both_sums = jnp.dot(mix, rows, preferred_element_type=jnp.float32)
            sums = both_sums[: 4 * rows_dev] + both_sums[4 * rows_dev :]
            mine = sums[:rows_dev]
            away = [
                sums[d * rows_dev : (d + 1) * rows_dev].astype(jnp.bfloat16) for d in range(4)
            ]
            return [mine] + give_back(away, back)[1:]

        total_1 = summed(mix_1, parts_1, to_y, to_z)
        total_2 = summed(mix_2, parts_2, to_z, to_y)
        mixed = jnp.concatenate(
            [sum(a.astype(jnp.float32) for a in t) for t in (total_1, total_2)], axis=1
        )
        hidden_out = (mid.astype(jnp.float32) + mixed).astype(jnp.bfloat16)
    return (hidden_out, new_cache)


def solution(mesh):
    axes = ("x", "zh", "y", "zl", "c")
    split = Mesh(mesh.devices.reshape(X, ZH, Y, ZL, C), axes)
    placed = (
        P(axes, None),
        P(axes, None),
        P(),
        P(None, None, ("x", "zh", "y"), None),
        P(),
        P(None, ("zl", "c")),
        P(),
        P(("zl", "c"), None),
        P(),
        P(),
        P(("y", "zl", "c"), None, None),
        P(("y", "zl", "c"), None, None),
    )
    return jax.shard_map(
        body,
        mesh=split,
        in_specs=placed,
        out_specs=(P(axes, None), P(("x", "zh", "y"), ("zl", "c"))),
        check_vma=False,
    )
```
